32 devices in a mesh: cells: 8 (over z, x), genes: 4 (over y, core).
Axes of the slice: x: 2, y: 2, z: 4, core: 2. Of those that a mesh axis runs over, the one named last changes fastest.
Arguments:
- logits: float32 [8192, 4096], P('cells', 'genes'), may hold values from -6 to 6
- expression: float32 [8192, 2048], P('cells', 'genes'), may hold values from 0.05 to 5
- spatial: float32 [4096, 2048], P(None, 'genes'), may hold values from 0.05 to 5
- density_prior: float32 [4096], replicated, may hold values from 1 to 10
- cell_slide: int32 [8192], P('cells'), may hold values from 0 to 3, as said below
- group_live: int32 [8], replicated, may hold values from 256 to 1024, as said below
- spot_counts: int32 [4], replicated, may hold values from 1 to 2048, 4096 in all
Outputs:
- predicted: float32 [4096, 2048], P('cells', 'genes')
- gene_cos: float32 [2048], P('genes')
- spot_cos: float32 [4096], P('cells')
- cos_loss: float32 [], replicated
- density_loss: float32 [], replicated
- grad_logits: float32 [8192, 4096], P('cells', 'genes')
- grad_expression: float32 [8192, 2048], P('cells', 'genes')
The draws below stay inside these ranges and needn't reach their ends.
Inputs may be any that keep to these rules, and one draw needn't show every extreme that they name: `cell_slide`: in each group's block of 1024 slots the first 4 slots hold slides 0 to 3 in order. `group_live`: one group has all 1024 slots live and another has 256.
All inputs are finite; a program needn't handle non-finite values.
Results may differ from the reference program's by a relative error of at most 0.0003.
Values sent between devices are 32-bit elements; how exact they have to be, the bound alone decides.
No kernel may reach another device: no remote copies, remote signals or barrier semaphores. Data moves between devices by JAX's collectives and lax.ppermute only.
A program may use at most 192 MiB of HBM per device.

```python
import math
import jax
import jax.numpy as jnp
import numpy as np
from jax import lax

GENES = 2048
SLIDES = 4
SLOT_DEV = 1024
SPOTS = 4096
GROUPS = 8
SLOTS = 8192
LIVE_LEAST = 256
SPOT_MOST = 2048


def draw_cell_slide(key, part):
    random_slide = jax.random.randint(key, (SLOTS,), 0, SLIDES)
    within = jnp.arange(SLOTS, dtype=jnp.int32) % SLOT_DEV
    return jnp.where(within < SLIDES, within, random_slide).astype(jnp.int32)


def draw_group_live(key, part):
    counts = jax.random.randint(key, (GROUPS,), LIVE_LEAST, SLOT_DEV + 1)
    fullest = jax.random.randint(jax.random.fold_in(key, 7), (), 0, GROUPS)
    offset = jax.random.randint(jax.random.fold_in(key, 11), (), 0, GROUPS - 1)
    emptiest = (fullest + 1 + offset) % GROUPS
    group_ids = jnp.arange(GROUPS, dtype=jnp.int32)
    counts = jnp.where(group_ids == emptiest, LIVE_LEAST, counts)
    return jnp.where(group_ids == fullest, SLOT_DEV, counts).astype(jnp.int32)


def block_levels(key, shape, split, smallest, largest):
    gain, own = 1.0, jax.random.fold_in(key, 6)
    for dim, shards_of in split:
        draws = jnp.exp(jax.random.uniform(jax.random.fold_in(own, dim), (shards_of,), jnp.float32, smallest / len(split), largest / len(split)))
        gain = gain * jnp.repeat(draws, shape[dim] // shards_of).reshape([-1 if axis == dim else 1 for axis in range(len(shape))])
    return gain


def split_up(count, total, limit, slope):
    loads = [(1 << 20) // math.isqrt(standing ** slope) + 1 for standing in range(2, count + 1)]
    spare, given = total - limit - (count - 1), [1] * (count - 1)
    while spare > 0:
        candidates = [i for i in range(count - 1) if given[i] < limit]
        pool, budget = sum([loads[i] for i in candidates]), spare
        for i in candidates:
            extra = min(limit - given[i], max(1, budget * loads[i] // pool), spare)
            given[i] = given[i] + extra
            spare = spare - extra
    return np.array([limit] + given)


def uneven_parts(stream_key, amount, total, bound, skew):
    if amount == 2:
        one = jax.random.randint(stream_key, (), max(1, total - bound), min(bound, total - 1) + 1)
        return jnp.stack([one, total - one])
    sizes = jnp.asarray(split_up(amount, total, bound, skew), jnp.int32)
    twos = (amount - 1) // 2
    giver, receiver = sizes[1:1 + 2 * twos:2], sizes[2:2 + 2 * twos:2]
    margin = jnp.minimum(giver - 1, bound - receiver)
    passed = jax.random.randint(jax.random.fold_in(stream_key, 1), (twos,), 0, 1 << 20) % (margin + 1)
    sizes = sizes.at[1:1 + 2 * twos:2].set(giver - passed).at[2:2 + 2 * twos:2].set(receiver + passed)
    return sizes[jax.random.permutation(jax.random.fold_in(stream_key, 2), amount)]


def normal_values(own_key, dims, scale, most, pieces=(), kind=jnp.bfloat16):
    values = jax.random.normal(own_key, dims, jnp.float32) * scale
    if len(pieces) > 0:
        values = block_levels(own_key, dims, pieces, -0.22, 0.18) * values
    return jnp.clip(values, min=-most, max=most).astype(kind)


def setup_inputs(seed: int = 0) -> dict:
    key_of = jax.random.split(jax.random.key(seed), 8)
    logits = normal_values(key_of[0], (SLOTS, SPOTS), 1.5, 6.0, ((0, 8), (1, 4)), jnp.float32)
    expression = jnp.clip(jnp.exp(math.log(5.0) - 4.6051702 * jax.random.uniform(key_of[1], (SLOTS, GENES), jnp.float32) ** block_levels(key_of[1], (SLOTS, GENES), ((0, 8), (1, 4)), -0.2, 0.2)), 0.05, 5.0)
    spatial = jnp.clip(jnp.exp(math.log(5.0) - 4.6051702 * jax.random.uniform(key_of[2], (SPOTS, GENES), jnp.float32) ** block_levels(key_of[2], (SPOTS, GENES), ((1, 4),), -0.2, 0.2)), 0.05, 5.0)
    density_prior = jnp.clip(jnp.exp(jax.random.uniform(key_of[3], (SPOTS,), jnp.float32, math.log(1.0), math.log(10.0))), 1.0, 10.0)
    cell_slide = draw_cell_slide(jax.random.fold_in(key_of[7], 71), 0)
    group_live = draw_group_live(jax.random.fold_in(key_of[7], 71), 0)
    spot_counts = uneven_parts(key_of[6], SLIDES, SPOTS, SPOT_MOST, 1).astype(jnp.int32)
    return dict(logits=logits, expression=expression, spatial=spatial, density_prior=density_prior, cell_slide=cell_slide, group_live=group_live, spot_counts=spot_counts)


@jax.custom_vjp
def low(v):
    return lax.optimization_barrier(v.astype(jnp.bfloat16)).astype(jnp.float32)

@jax.custom_vjp
def low_back(v):
    return v

def low_keep(v):
    return (low(v), None)

def low_pass(kept, grad):
    return (grad,)

def back_keep(v):
    return (v, None)

def back_low(kept, grad):
    return (low(grad),)
low.defvjp(low_keep, low_pass)
low_back.defvjp(back_keep, back_low)
eps_norm = 1e-06
density_weight = 0.01
highest = lax.Precision.HIGHEST

def reference(logits, expression, spatial, density_prior, cell_slide, group_live, spot_counts):
    slot_index = jnp.arange(SLOTS, dtype=jnp.int32)
    slot_live = slot_index % SLOT_DEV < group_live[slot_index // SLOT_DEV]
    slide_ends = jnp.cumsum(spot_counts).astype(jnp.int32)
    spot_index = jnp.arange(SPOTS, dtype=jnp.int32)
    spot_slide = lax.optimization_barrier(jnp.sum((spot_index[:, None] >= slide_ends[None, :]).astype(jnp.int32), axis=1))
    allowed = slot_live[:, None] & (cell_slide[:, None] == spot_slide[None, :])
    member = spot_slide[None, :] == jnp.arange(SLIDES, dtype=jnp.int32)[:, None]
    prior_total = lax.optimization_barrier(jnp.sum(jnp.where(member, density_prior[None, :], 0.0), axis=1))
    prior_norm = density_prior / prior_total[spot_slide]

    def forward(weights, cell_expr):
        spot_top = lax.optimization_barrier(jnp.max(jnp.where(allowed, weights, -jnp.inf), axis=0))
        exponent = jnp.where(allowed, jnp.exp(weights - spot_top[None, :]), 0.0)
        spot_total = lax.optimization_barrier(jnp.sum(exponent, axis=0))
        mapping = exponent / spot_total[None, :]
        log_mass = spot_top + jnp.log(spot_total)
        predicted = jnp.dot(mapping.T, cell_expr, precision=highest)
        gene_dot = lax.optimization_barrier(jnp.sum(predicted * spatial, axis=0))
        gene_pp = lax.optimization_barrier(jnp.sum(predicted * predicted, axis=0))
        gene_gg = lax.optimization_barrier(jnp.sum(spatial * spatial, axis=0))
        gene_cos = gene_dot * lax.rsqrt(gene_pp + eps_norm) * lax.rsqrt(gene_gg + eps_norm)
        spot_dot = lax.optimization_barrier(jnp.sum(predicted * spatial, axis=1))
        spot_pp = lax.optimization_barrier(jnp.sum(predicted * predicted, axis=1))
        spot_gg = lax.optimization_barrier(jnp.sum(spatial * spatial, axis=1))
        spot_cos = spot_dot * lax.rsqrt(spot_pp + eps_norm) * lax.rsqrt(spot_gg + eps_norm)
        cos_loss = -(jnp.mean(gene_cos) + jnp.mean(spot_cos))
        slide_top = lax.optimization_barrier(jnp.max(jnp.where(member, log_mass[None, :], -jnp.inf), axis=1))
        slide_sum = lax.optimization_barrier(jnp.sum(jnp.where(member, jnp.exp(log_mass[None, :] - slide_top[:, None]), 0.0), axis=1))
        slide_lse = slide_top + jnp.log(slide_sum)
        log_pred = log_mass - slide_lse[spot_slide]
        density_loss = jnp.sum(prior_norm * (jnp.log(prior_norm) - log_pred)) / SLIDES
        objective = SLOTS * SPOTS * (cos_loss + density_weight * density_loss)
        return (objective, (predicted, gene_cos, spot_cos, cos_loss, density_loss))
    objective, pullback, extras = jax.vjp(forward, logits, expression, has_aux=True)
    gradients = pullback(jnp.ones((), logits.dtype))
    predicted, gene_cos, spot_cos, cos_loss, density_loss = extras
    return (predicted, gene_cos, spot_cos, cos_loss, density_loss, gradients[0], gradients[1])
```

```python
import jax
import jax.numpy as jnp
from jax import lax
from jax.sharding import PartitionSpec as P

eps_norm = 1e-06
density_weight = 0.01
high = lax.Precision.HIGH
highest = lax.Precision.HIGHEST


def slide_of(spot_index, slide_ends):
    return jnp.sum((spot_index[:, None] >= slide_ends[None, :]).astype(jnp.int32), axis=1)


def live_of(group_live, group_index, slot_dev):
    groups = group_live.shape[0]
    here = jnp.arange(groups, dtype=jnp.int32) == group_index
    return jnp.arange(slot_dev, dtype=jnp.int32) < jnp.sum(jnp.where(here, group_live, 0))


def spread(logits, expression, spatial, density_prior, cell_slide, group_live, spot_counts):
    slot_dev, spot_dev = logits.shape
    gene_dev = expression.shape[1]
    groups, parts = lax.axis_size("cells"), lax.axis_size("genes")
    spots_all, genes_all = spot_dev * parts, gene_dev * parts
    spot_rows = spots_all // groups
    slides = spot_counts.shape[0]
    group_index, gene_index = lax.axis_index("cells"), lax.axis_index("genes")
    scale = float(slot_dev * groups) * float(spots_all)
    slide_ends = jnp.cumsum(spot_counts)
    spot_slide = slide_of(jnp.arange(spots_all, dtype=jnp.int32), slide_ends)
    own_slide = lax.dynamic_slice_in_dim(spot_slide, gene_index * spot_dev, spot_dev)
    slot_live = live_of(group_live, group_index, slot_dev)
    allowed = slot_live[:, None] & (cell_slide[:, None] == own_slide[None, :])
    weight = jnp.where(allowed, jnp.exp(logits), 0.0)
    spot_total = lax.psum(jnp.sum(weight, axis=0), "cells")
    mapping = weight / spot_total[None, :]
    full_map, full_total = (
        lax.all_gather(mapping, "genes", axis=1, tiled=True),
        lax.all_gather(spot_total, "genes", axis=0, tiled=True),
    )
    pred_rows = lax.psum_scatter(
        lax.dot_general(full_map, expression, (((0,), (0,)), ((), ())), precision=highest),
        "cells",
        scatter_dimension=0,
        tiled=True,
    )
    spatial_rows = lax.dynamic_slice_in_dim(spatial, group_index * spot_rows, spot_rows, 0)
    triple = (pred_rows * spatial_rows, pred_rows * pred_rows, spatial_rows * spatial_rows)
    gene_dot, gene_pp, gene_gg = lax.psum(
        jnp.stack([jnp.sum(part, axis=0) for part in triple]), "cells"
    )
    spot_dot, spot_pp, spot_gg = lax.psum(
        jnp.stack([jnp.sum(part, axis=1) for part in triple]), "genes"
    )
    gene_unit = lax.rsqrt(gene_pp + eps_norm) * lax.rsqrt(gene_gg + eps_norm)
    gene_cos = gene_dot * gene_unit
    spot_unit = lax.rsqrt(spot_pp + eps_norm) * lax.rsqrt(spot_gg + eps_norm)
    spot_cos = spot_dot * spot_unit
    gene_term = gene_unit[None, :] * spatial_rows - (gene_cos / (gene_pp + eps_norm))[None, :] * pred_rows
    spot_term = spot_unit[:, None] * spatial_rows - (spot_cos / (spot_pp + eps_norm))[:, None] * pred_rows
    grad_rows = -(scale / genes_all) * gene_term - scale / spots_all * spot_term
    loss_part = jnp.sum(gene_cos) / (genes_all * groups) + jnp.sum(spot_cos) / (spots_all * parts)
    cos_loss = -lax.psum(loss_part, ("cells", "genes"))
    grad_full = lax.all_gather(grad_rows, "cells", axis=0, tiled=True)
    member = spot_slide[None, :] == jnp.arange(slides, dtype=jnp.int32)[:, None]
    prior_total = jnp.sum(jnp.where(member, density_prior[None, :], 0.0), axis=1)
    prior_norm = density_prior / jnp.sum(jnp.where(member, prior_total[:, None], 0.0), axis=0)
    slide_sum = jnp.sum(jnp.where(member, full_total[None, :], 0.0), axis=1)
    share = full_total / jnp.sum(jnp.where(member, slide_sum[:, None], 0.0), axis=0)
    density_loss = jnp.sum(prior_norm * (jnp.log(prior_norm) - jnp.log(share))) / slides
    mass_grad = scale * density_weight * (share - prior_norm) / slides
    own_mass_grad = lax.dynamic_slice_in_dim(mass_grad, gene_index * spot_dev, spot_dev)
    partial_grad = lax.dot_general(expression, grad_full, (((1,), (1,)), ((), ())), precision=highest)
    map_grad = lax.psum_scatter(partial_grad, "genes", scatter_dimension=1, tiled=True)
    grad_expression = jnp.dot(full_map, grad_full, precision=highest)
    spot_weight = lax.psum(jnp.sum(mapping * map_grad, axis=0), "cells")
    grad_logits = mapping * (map_grad - spot_weight[None, :] + own_mass_grad[None, :])
    return (pred_rows, gene_cos, spot_cos, cos_loss, density_loss, grad_logits, grad_expression)


def shift(value, moves, axis):
    count = lax.axis_size(axis)
    pairs = [(k, moves(k)) for k in range(count) if moves(k) is not None]
    return lax.ppermute(value, axis, pairs)


def over_x(value):
    return shift(value, lambda k: k ^ 1, "cells")


def over_y(value):
    return shift(value, lambda k: k ^ 2, "genes")


def over_core(value):
    return shift(value, lambda k: k ^ 1, "genes")


def hop(value, steps):
    return shift(value, lambda k: steps[k // 2] * 2 + k % 2 if k // 2 in steps else None, "cells")


outward_in = {0: 1, 3: 2}
crossing = {1: 2, 2: 1}
inward_out = {2: 3, 1: 0}


def sum_genes(value, misc):
    kinds, parts, width = value.shape
    flat = jnp.concatenate([value.reshape(kinds * parts, width), misc], axis=0)
    fill = -flat.shape[0] % 8
    flat = jnp.pad(flat, ((0, fill), (0, 0)))
    flat = flat + over_x(flat)
    flat = flat + hop(flat, {0: 3, 3: 0})

    def joined(mine, other, part):
        swapped = other[: kinds * parts].reshape(kinds, parts, width)
        swapped = swapped[:, [r ^ part for r in range(parts)]].reshape(kinds * parts, width)
        return mine + jnp.concatenate([swapped, other[kinds * parts :]], axis=0)

    flat = joined(flat, over_core(flat), 1)
    flat = joined(flat, over_y(flat), 2)
    return flat[: kinds * parts].reshape(kinds, parts, width), flat[kinds * parts]


def slice_4x2(logits, expression, spatial, density_prior, cell_slide, group_live, spot_counts):
    slot_dev, spot_dev = logits.shape
    gene_dev = expression.shape[1]
    groups, parts = 8, 4
    spots_all, genes_all = spot_dev * parts, gene_dev * parts
    slides = spot_counts.shape[0]
    rows, half = spot_dev // 4, gene_dev // 2
    group_index, gene_index = lax.axis_index("cells"), lax.axis_index("genes")
    z, x = group_index // 2, group_index % 2
    near = (z >= 2).astype(jnp.int32)
    is_end = (z == 0) | (z == 3)
    scale = float(slot_dev * groups) * float(spots_all)
    first_half, second_half = slice(0, half), slice(half, gene_dev)

    units = []
    for cut in (first_half, second_half):
        own = expression[:, cut]
        across = over_y(own)
        units.append(jnp.concatenate([own, over_core(own)], axis=1))
        units.append(jnp.concatenate([across, over_core(across)], axis=1))

    keep_near, keep_far = 2 * x + near, 2 * x + 1 - near
    send_near, send_far = 2 * (1 - x) + near, 2 * (1 - x) + 1 - near
    blocks = [keep_near, keep_far, send_near, send_far]
    slide_ends = jnp.cumsum(spot_counts)
    spot_index = jnp.concatenate(
        [
            gene_index * spot_dev + block * rows + jnp.arange(rows, dtype=jnp.int32)
            for block in blocks
        ]
    )
    own_slide = slide_of(spot_index, slide_ends)
    slot_live = live_of(group_live, group_index, slot_dev)
    allowed = slot_live[:, None] & (cell_slide[:, None] == own_slide[None, :])
    ordered = jnp.concatenate(
        [lax.dynamic_slice_in_dim(logits, block * rows, rows, 1) for block in blocks], axis=1
    )
    weight = jnp.where(allowed, jnp.exp(ordered), 0.0)
    local_total = jnp.sum(weight, axis=0)

    def share_of(part):
        return lax.dynamic_slice_in_dim(spatial, part * spot_dev + keep_near * rows, rows, 0)

    g_parts = [
        share_of(gene_index),
        over_core(share_of(gene_index ^ 1)),
        over_y(share_of(gene_index ^ 2)),
        shift(share_of(gene_index ^ 3), lambda k: k ^ 3, "genes"),
    ]
    spat = [
        jnp.concatenate([g_parts[q][:, cut], g_parts[q + 1][:, cut]], axis=1)
        for cut in (first_half, second_half)
        for q in (0, 2)
    ]

    def partial(block, unit):
        product = lax.dot_general(
            weight[:, block * rows : (block + 1) * rows],
            units[unit],
            (((0,), (0,)), ((), ())),
            precision=high,
        )
        if unit == 0:
            total = local_total[block * rows : (block + 1) * rows]
            extra = jnp.pad(total[None, :], ((0, 7), (0, gene_dev - rows)))
            product = jnp.concatenate([product, extra], axis=0)
        return product

    sums = []
    for unit in range(4):
        far = partial(1, unit) + over_x(partial(3, unit))
        close = partial(0, unit) + over_x(partial(2, unit))
        far = far + hop(far, outward_in)
        close = close + hop(far, crossing)
        close = close + hop(close, inward_out)
        sums.append(close)

    total = sums[0][rows, :rows]
    pred = [part[:rows] / total[:, None] for part in sums]

    share_index = gene_index * spot_dev + keep_near * rows + jnp.arange(rows, dtype=jnp.int32)
    share_slide = slide_of(share_index, slide_ends)
    spot_slide = slide_of(jnp.arange(spots_all, dtype=jnp.int32), slide_ends)
    member = spot_slide[None, :] == jnp.arange(slides, dtype=jnp.int32)[:, None]
    share_member = share_slide[None, :] == jnp.arange(slides, dtype=jnp.int32)[:, None]
    prior_total = jnp.sum(jnp.where(member, density_prior[None, :], 0.0), axis=1)
    share_prior = lax.dynamic_slice_in_dim(
        density_prior, gene_index * spot_dev + keep_near * rows, rows
    ) / jnp.sum(jnp.where(share_member, prior_total[:, None], 0.0), axis=0)

    def gene_sums(pair):
        return jnp.stack(
            [
                jnp.concatenate([jnp.sum(f(pred[u], spat[u]), axis=0) for u in pair]).reshape(parts, half)
                for f in (lambda p, g: p * g, lambda p, g: p * p, lambda p, g: g * g)
            ]
        )

    slide_part = jnp.sum(jnp.where(share_member, total[None, :], 0.0), axis=1)
    entropy_part = jnp.sum(share_prior * (jnp.log(share_prior) - jnp.log(total)))
    prior_part = jnp.sum(jnp.where(share_member, share_prior[None, :], 0.0), axis=1)
    misc = jnp.concatenate([slide_part, prior_part, entropy_part[None]])
    first, misc = sum_genes(gene_sums((0, 1)), jnp.pad(misc, (0, half - misc.shape[0]))[None, :])

    spot_dot = sum(jnp.sum(p * g, axis=1) for p, g in zip(pred, spat))
    spot_pp = sum(jnp.sum(p * p, axis=1) for p in pred)
    spot_gg = sum(jnp.sum(g * g, axis=1) for g in spat)
    spot_unit = lax.rsqrt(spot_pp + eps_norm) * lax.rsqrt(spot_gg + eps_norm)
    spot_cos = spot_dot * spot_unit
    spot_slope = scale / spots_all * spot_cos / (spot_pp + eps_norm)
    second, cos_sum = sum_genes(
        gene_sums((2, 3)), jnp.pad(jnp.sum(spot_cos)[None], (0, half - 1))[None, :]
    )

    stats = [
        found[:, 2 * q : 2 * q + 2].reshape(3, gene_dev) for found in (first, second) for q in (0, 1)
    ]
    gene_cos, grads = [None] * 4, [None] * 4
    for unit in (1, 0, 3, 2):
        dot, pp, gg = stats[unit]
        unit_gene = lax.rsqrt(pp + eps_norm) * lax.rsqrt(gg + eps_norm)
        gene_cos[unit] = dot * unit_gene
        slope = scale / genes_all * gene_cos[unit] / (pp + eps_norm)
        grads[unit] = (slope[None, :] + spot_slope[:, None]) * pred[unit] - (
            scale / genes_all * unit_gene[None, :] + scale / spots_all * spot_unit[:, None]
        ) * spat[unit]
    slide_sum, prior_sum, entropy = misc[:slides], misc[slides : 2 * slides], misc[2 * slides]
    density_loss = (entropy + jnp.sum(prior_sum * jnp.log(slide_sum))) / slides
    cos_loss = -(sum(jnp.sum(c) for c in gene_cos) / genes_all + cos_sum[0] / spots_all)
    share_mass = total / jnp.sum(jnp.where(share_member, slide_sum[:, None], 0.0), axis=0)
    mass_grad = scale * density_weight * (share_mass - share_prior) / slides
    spot_weight = sum(jnp.sum(p * d, axis=1) for p, d in zip(pred, grads))
    offset = (mass_grad - spot_weight) / total
    losses = jnp.stack([cos_loss, density_loss])
    tail = jnp.stack(
        [
            jnp.concatenate([gene_cos[0][:half], gene_cos[2][:half]]),
            jnp.pad(offset, (0, gene_dev - rows)),
            jnp.pad(losses, (0, gene_dev - 2)),
        ]
    )
    tail = jnp.pad(tail, ((0, 5), (0, 0)))

    def home(part):
        pairs = []
        for column in range(4):
            for k in range(2):
                for end, sent in ((0, part), (3, part ^ 1)):
                    pairs.append(((2 * end + k) * 4 + column, (2 * column + k) * 4 + (column ^ sent)))
        return pairs

    part_pred = [
        jnp.concatenate([pred[q][:, cut], pred[2 + q][:, cut]], axis=1)
        for q in (0, 1)
        for cut in (first_half, second_half)
    ]
    cos_row = jnp.pad(jnp.pad(spot_cos, (0, gene_dev - rows))[None, :], ((0, 7), (0, 0)))
    landed = []
    for part in range(4):
        value = jnp.where(z == 0, part_pred[part], part_pred[part ^ 1])
        value = jnp.concatenate([value, cos_row], axis=0)
        landed.append(lax.ppermute(value, ("cells", "genes"), home(part)))
    landed = jnp.stack(landed)
    mine = gene_index ^ z
    low = lax.dynamic_index_in_dim(landed, mine, 0, keepdims=False)
    upper = lax.dynamic_index_in_dim(landed, mine ^ 1, 0, keepdims=False)
    pred_out = jnp.concatenate([low[:rows], upper[:rows]], axis=0)
    spot_cos_out = jnp.concatenate([low[rows, :rows], upper[rows, :rows]])

    map_grad = None
    share = [None] * 4
    for unit in (1, 0, 3, 2):
        value = grads[unit] / total[:, None]
        if unit == 2:
            value = jnp.concatenate([value, tail], axis=0)
        close = jnp.where(is_end, value, hop(value, outward_in))
        cross = hop(close, crossing)
        far = jnp.where(is_end, hop(cross, inward_out), cross)
        pieces = [close, far, over_x(close), over_x(far)]
        grad = jnp.concatenate([piece[:rows] for piece in pieces], axis=0)
        part = lax.dot_general(units[unit], grad, (((1,), (1,)), ((), ())), precision=high)
        map_grad = part if map_grad is None else map_grad + part
        share[unit] = jnp.dot(weight, grad, precision=high)
    offset = jnp.concatenate([piece[rows + 1, :rows] for piece in pieces])
    gene_cos_out = close[rows]
    cos_loss, density_loss = close[rows + 2, 0], close[rows + 2, 1]

    ordered_grad = weight * (map_grad + offset[None, :])
    grad_logits = jnp.zeros_like(logits)
    for k, block in enumerate(blocks):
        grad_logits = lax.dynamic_update_slice_in_dim(
            grad_logits, ordered_grad[:, k * rows : (k + 1) * rows], block * rows, 1
        )
    halves = []
    for own, away in ((share[0], share[1]), (share[2], share[3])):
        chip = over_y(away[:, first_half] + over_core(away[:, second_half]))
        halves.append(own[:, first_half] + over_core(own[:, second_half]) + chip)
    grad_expression = jnp.concatenate(halves, axis=1)
    return (pred_out, gene_cos_out, spot_cos_out, cos_loss, density_loss, grad_logits, grad_expression)


def solution(mesh):
    fits = mesh.shape["cells"] == 8 and mesh.shape["genes"] == 4
    return jax.shard_map(
        slice_4x2 if fits else spread,
        mesh=mesh,
        in_specs=(
            P("cells", "genes"),
            P("cells", "genes"),
            P(None, "genes"),
            P(),
            P("cells"),
            P(),
            P(),
        ),
        out_specs=(
            P("cells", "genes"),
            P("genes"),
            P("cells"),
            P(),
            P(),
            P("cells", "genes"),
            P("cells", "genes"),
        ),
        check_vma=False,
    )
```

```python
import functools

import jax
import jax.numpy as jnp
from jax import lax
from jax.experimental import pallas as pl
from jax.experimental.pallas import tpu as pltpu
from jax.sharding import PartitionSpec as P

eps_norm = 1e-06
density_weight = 0.01
high = lax.Precision.HIGH
highest = lax.Precision.HIGHEST


def slide_of(spot_index, slide_ends):
    return jnp.sum((spot_index[:, None] >= slide_ends[None, :]).astype(jnp.int32), axis=1)


def live_of(group_live, group_index, slot_dev):
    groups = group_live.shape[0]
    here = jnp.arange(groups, dtype=jnp.int32) == group_index
    return jnp.arange(slot_dev, dtype=jnp.int32) < jnp.sum(jnp.where(here, group_live, 0))


def spread(logits, expression, spatial, density_prior, cell_slide, group_live, spot_counts):
    slot_dev, spot_dev = logits.shape
    gene_dev = expression.shape[1]
    groups, parts = lax.axis_size("cells"), lax.axis_size("genes")
    spots_all, genes_all = spot_dev * parts, gene_dev * parts
    spot_rows = spots_all // groups
    slides = spot_counts.shape[0]
    group_index, gene_index = lax.axis_index("cells"), lax.axis_index("genes")
    scale = float(slot_dev * groups) * float(spots_all)
    slide_ends = jnp.cumsum(spot_counts)
    spot_slide = slide_of(jnp.arange(spots_all, dtype=jnp.int32), slide_ends)
    own_slide = lax.dynamic_slice_in_dim(spot_slide, gene_index * spot_dev, spot_dev)
    slot_live = live_of(group_live, group_index, slot_dev)
    allowed = slot_live[:, None] & (cell_slide[:, None] == own_slide[None, :])
    weight = jnp.where(allowed, jnp.exp(logits), 0.0)
    spot_total = lax.psum(jnp.sum(weight, axis=0), "cells")
    mapping = weight / spot_total[None, :]
    full_map, full_total = (
        lax.all_gather(mapping, "genes", axis=1, tiled=True),
        lax.all_gather(spot_total, "genes", axis=0, tiled=True),
    )
    pred_rows = lax.psum_scatter(
        lax.dot_general(full_map, expression, (((0,), (0,)), ((), ())), precision=highest),
        "cells",
        scatter_dimension=0,
        tiled=True,
    )
    spatial_rows = lax.dynamic_slice_in_dim(spatial, group_index * spot_rows, spot_rows, 0)
    triple = (pred_rows * spatial_rows, pred_rows * pred_rows, spatial_rows * spatial_rows)
    gene_dot, gene_pp, gene_gg = lax.psum(
        jnp.stack([jnp.sum(part, axis=0) for part in triple]), "cells"
    )
    spot_dot, spot_pp, spot_gg = lax.psum(
        jnp.stack([jnp.sum(part, axis=1) for part in triple]), "genes"
    )
    gene_unit = lax.rsqrt(gene_pp + eps_norm) * lax.rsqrt(gene_gg + eps_norm)
    gene_cos = gene_dot * gene_unit
    spot_unit = lax.rsqrt(spot_pp + eps_norm) * lax.rsqrt(spot_gg + eps_norm)
    spot_cos = spot_dot * spot_unit
    gene_term = gene_unit[None, :] * spatial_rows - (gene_cos / (gene_pp + eps_norm))[None, :] * pred_rows
    spot_term = spot_unit[:, None] * spatial_rows - (spot_cos / (spot_pp + eps_norm))[:, None] * pred_rows
    grad_rows = -(scale / genes_all) * gene_term - scale / spots_all * spot_term
    loss_part = jnp.sum(gene_cos) / (genes_all * groups) + jnp.sum(spot_cos) / (spots_all * parts)
    cos_loss = -lax.psum(loss_part, ("cells", "genes"))
    grad_full = lax.all_gather(grad_rows, "cells", axis=0, tiled=True)
    member = spot_slide[None, :] == jnp.arange(slides, dtype=jnp.int32)[:, None]
    prior_total = jnp.sum(jnp.where(member, density_prior[None, :], 0.0), axis=1)
    prior_norm = density_prior / jnp.sum(jnp.where(member, prior_total[:, None], 0.0), axis=0)
    slide_sum = jnp.sum(jnp.where(member, full_total[None, :], 0.0), axis=1)
    share = full_total / jnp.sum(jnp.where(member, slide_sum[:, None], 0.0), axis=0)
    density_loss = jnp.sum(prior_norm * (jnp.log(prior_norm) - jnp.log(share))) / slides
    mass_grad = scale * density_weight * (share - prior_norm) / slides
    own_mass_grad = lax.dynamic_slice_in_dim(mass_grad, gene_index * spot_dev, spot_dev)
    partial_grad = lax.dot_general(expression, grad_full, (((1,), (1,)), ((), ())), precision=highest)
    map_grad = lax.psum_scatter(partial_grad, "genes", scatter_dimension=1, tiled=True)
    grad_expression = jnp.dot(full_map, grad_full, precision=highest)
    spot_weight = lax.psum(jnp.sum(mapping * map_grad, axis=0), "cells")
    grad_logits = mapping * (map_grad - spot_weight[None, :] + own_mass_grad[None, :])
    return (pred_rows, gene_cos, spot_cos, cos_loss, density_loss, grad_logits, grad_expression)


def shift(value, moves, axis, name):
    count = lax.axis_size(axis)
    pairs = [(k, moves(k)) for k in range(count) if moves(k) is not None]
    with jax.named_scope(name):
        return lax.ppermute(value, axis, pairs)


def over_x(value, name):
    return shift(value, lambda k: k ^ 1, "cells", name)


def over_y(value, name):
    return shift(value, lambda k: k ^ 2, "genes", name)


def over_core(value, name):
    return shift(value, lambda k: k ^ 1, "genes", name)


def over_z(value, step, name):
    return shift(value, lambda k: k ^ (2 * step), "cells", name)


class Order:
    def __init__(self):
        self.last = None

    def __call__(self, step, *operands):
        if self.last is not None:
            operands, _ = lax.optimization_barrier((operands, self.last))
        out = step(*operands)
        self.last = jax.tree.leaves(out)[0]
        return out


f32, bf16 = jnp.float32, jnp.bfloat16


def split(value):
    upper = value.astype(bf16)
    return upper, (value - upper.astype(f32)).astype(bf16)


def mul(p, q):
    return jnp.dot(p, q, preferred_element_type=f32)


def mul_t(p, q):
    return lax.dot_general(p, q, (((1,), (1,)), ((), ())), preferred_element_type=f32)


def whole(shape):
    return pl.BlockSpec(shape, lambda *k: (0,) * len(shape), pipeline_mode=pl.Buffered(1))


def like(*shape, dtype=f32):
    return jax.ShapeDtypeStruct(shape, dtype)


def room(mebi):
    return pltpu.CompilerParams(vmem_limit_bytes=mebi << 20)


light = pl.CostEstimate(flops=1, bytes_accessed=1, transcendentals=0)


def weigh_kernel(slides, info, table, code, wh, wl, th, tl, tot):
    k = pl.program_id(0)
    depth, width = table.shape
    half = width // 2
    odd = info[6 + slides + 2]
    lane = lax.broadcasted_iota(jnp.int32, (1, width), 1)
    spot = info[4] + info[k] * width + jnp.where(odd == 1, lane ^ half, lane)
    slide = sum((spot >= info[6 + q]).astype(jnp.int32) for q in range(slides)).astype(f32)

    def step(a, total):
        at = pl.multiple_of(a * 128, 128)
        own = jnp.broadcast_to(code[pl.ds(a, 1), :].astype(f32), (128, 128)).T
        own = jnp.concatenate([own] * (width // 128), axis=1)
        live = at + lax.broadcasted_iota(jnp.int32, (128, width), 0) < info[5]
        value = table[pl.ds(at, 128), :]
        value = jnp.where(odd == 1, jnp.concatenate([value[:, half:], value[:, :half]], axis=1), value)
        w = jnp.where((own == slide) & live, jnp.exp(value), 0.0)
        wh[pl.ds(at, 128), :], wl[pl.ds(at, 128), :] = split(w)
        th[:, pl.ds(at, 128)], tl[:, pl.ds(at, 128)] = split(w.T)
        return total + jnp.sum(w, axis=0, keepdims=True)

    total = lax.fori_loop(0, depth // 128, step, jnp.zeros((1, width), f32))
    tot[...] = jnp.broadcast_to(total, tot.shape)


def weigh(info, logits, code, slides):
    depth, spots = logits.shape
    rows = spots // 4
    wide = pl.BlockSpec((depth, rows), lambda k, info: (0, k))
    tall = pl.BlockSpec((rows, depth), lambda k, info: (k, 0))
    return pl.pallas_call(
        functools.partial(weigh_kernel, slides),
        name="weigh",
        grid_spec=pltpu.PrefetchScalarGridSpec(
            num_scalar_prefetch=1,
            grid=(4,),
            in_specs=[
                pl.BlockSpec((depth, rows), lambda k, info: (0, info[k])),
                pl.BlockSpec(code.shape, lambda k, info: (0, 0)),
            ],
            out_specs=[wide, wide, tall, tall, pl.BlockSpec((8, rows), lambda k, info: (0, k))],
        ),
        out_shape=[
            like(depth, spots, dtype=bf16),
            like(depth, spots, dtype=bf16),
            like(spots, depth, dtype=bf16),
            like(spots, depth, dtype=bf16),
            like(8, spots),
        ],
        cost_estimate=light,
        compiler_params=room(12),
    )(info, logits, code)


def blend_kernel(counts, has_total, th, tl, ep, eq, *refs):
    k = pl.program_id(0)
    tot = refs[0] if has_total else None
    outs, (eh, el) = refs[int(has_total) : -2], refs[-2:]
    width = ep.shape[1]

    @pl.when(k == 0)
    def _():
        begin = 0
        for out, count in zip(outs, counts):
            out[...] = jnp.zeros_like(out)
            if has_total:
                out[count:, :count] = tot[:, begin : begin + count]
            begin += count

    for place, part in ((slice(0, width), ep), (slice(width, 2 * width), eq)):
        upper, lower = split(part[...])
        eh[:, place], el[:, place] = upper, lower
        value = mul(th[...], upper) + mul(th[...], lower) + mul(tl[...], upper)
        begin = 0
        for out, count in zip(outs, counts):
            out[:count, place] += value[begin : begin + count]
            begin += count


def blend(th, tl, ep, eq, counts, tot=None):
    spots, depth = th.shape
    width = ep.shape[1]
    deep = 256
    extra = 0 if tot is None else 8
    column = pl.BlockSpec((spots, deep), lambda k: (0, k))
    row = pl.BlockSpec((deep, width), lambda k: (k, 0))
    both = pl.BlockSpec((deep, 2 * width), lambda k: (k, 0))
    return pl.pallas_call(
        functools.partial(blend_kernel, counts, tot is not None),
        name="blend",
        grid=(depth // deep,),
        in_specs=[column, column, row, row] + ([] if tot is None else [whole(tot.shape)]),
        out_specs=[pl.BlockSpec((c + extra, 2 * width), lambda k: (0, 0)) for c in counts] + [both, both],
        out_shape=[like(c + extra, 2 * width) for c in counts]
        + [like(depth, 2 * width, dtype=bf16), like(depth, 2 * width, dtype=bf16)],
        cost_estimate=light,
        compiler_params=room(14),
    )(th, tl, ep, eq, *(() if tot is None else (tot,)))


def stats_kernel(first, last, spots_scale, *refs):
    refs = list(refs)
    close, found, gp, gq = refs[:4]
    refs = refs[4:]
    rows = gp.shape[0]
    if first:
        inv, row = refs[-2:]
        total = close[rows : rows + 1, :rows] + found[rows : rows + 1, :rows]
        row[...] = jnp.broadcast_to(total, row.shape)
        for b in range(0, rows, 128):
            inv[b : b + 128, :] = 1.0 / jnp.broadcast_to(total[:, b : b + 128], (128, 128)).T
        inverse = inv[...]
    else:
        inverse = refs[0][...]
        before = refs[1]
        refs = refs[2:]
    pred, gsum, part = refs[:3]
    width = close.shape[1]
    value = (close[:rows] + found[:rows]) * jnp.concatenate([inverse] * (width // 128), axis=1)
    pred[...] = value
    g = jnp.concatenate([gp[...], gq[...]], axis=1)
    sums = []
    for n, product in enumerate((value * g, value * value, g * g)):
        gsum[n : n + 1, :] = jnp.sum(product, axis=0, keepdims=True)
        lanes = sum(product[:, c : c + 128] for c in range(0, width, 128))
        if not first:
            lanes = lanes + before[:, n * 128 : n * 128 + 128]
        sums.append(lanes)
        part[:, n * 128 : n * 128 + 128] = lanes
    gsum[3:, :] = jnp.zeros((5, width), f32)
    if last:
        unit_out, slope_out, cos_out = refs[3:]
        dot, pp, gg = [jnp.sum(lanes, axis=1, keepdims=True) for lanes in sums]
        unit = lax.rsqrt(pp + eps_norm) * lax.rsqrt(gg + eps_norm)
        cos = dot * unit
        wide = lambda v: jnp.broadcast_to(v, (rows, 128))
        unit_out[...] = wide(unit * spots_scale)
        slope_out[...] = wide(spots_scale * cos / (pp + eps_norm))
        for b in range(0, rows, 128):
            turned = wide(cos)[b : b + 128].T
            cos_out[:, b : b + 128] = turned[:8]


def stats(close, found, parts, cut, inv=None, before=None, last=False, spots_scale=0.0):
    rows, width = parts[0].shape
    block = pl.BlockSpec((rows, width // 2), lambda k: (0, cut), pipeline_mode=pl.Buffered(1))
    first = inv is None
    outs = [like(rows, width), like(8, width), like(rows, 384)]
    if first:
        outs += [like(rows, 128), like(8, rows)]
    if last:
        outs += [like(rows, 128), like(rows, 128), like(8, rows)]
    extra = () if first else (inv, before)
    landed = [whole((rows + 8 if first else rows, width))] * 2
    return pl.pallas_call(
        functools.partial(stats_kernel, first, last, spots_scale),
        name="stats",
        grid=(1,),
        in_specs=landed + [block, block] + [whole(v.shape) for v in extra],
        out_specs=[whole(o.shape) for o in outs],
        out_shape=outs,
        cost_estimate=light,
        compiler_params=room(8),
    )(close, found, *parts, *extra)


def grad_kernel(genes_scale, chain, pred, gp, gq, red, unit_in, slope_in, inv, *refs):
    width = pred.shape[1]
    out, weight, cos_out = refs[-3:]
    dot, pp, gg = red[0:1, :], red[1:2, :], red[2:3, :]
    unit = lax.rsqrt(pp + eps_norm) * lax.rsqrt(gg + eps_norm)
    cos = dot * unit
    cos_out[...] = jnp.broadcast_to(cos, cos_out.shape)
    slope = genes_scale * cos / (pp + eps_norm)
    wide = lambda v: jnp.concatenate([v[...]] * (width // 128), axis=1)
    g = jnp.concatenate([gp[...], gq[...]], axis=1)
    p = pred[...]
    grad = (slope + wide(slope_in)) * p - (genes_scale * unit + wide(unit_in)) * g
    out[...] = grad * wide(inv)
    product = grad * p
    lanes = sum(product[:, c : c + 128] for c in range(0, width, 128))
    weight[...] = lanes + refs[0][...] if chain else lanes


def grad_of(pred, parts, cut, red, q, unit, slope, inv, genes_scale, before=None):
    rows, width = pred.shape
    block = pl.BlockSpec((rows, width // 2), lambda k: (0, cut), pipeline_mode=pl.Buffered(1))
    extra = () if before is None else (before,)
    outs = [like(rows, width), like(rows, 128), like(8, width)]
    return pl.pallas_call(
        functools.partial(grad_kernel, genes_scale, before is not None),
        name="grad",
        grid=(1,),
        in_specs=[whole(pred.shape), block, block, pl.BlockSpec((8, width), lambda k: (0, q))]
        + [whole(v.shape) for v in (unit, slope, inv) + extra],
        out_specs=[whole(o.shape) for o in outs],
        out_shape=outs,
        cost_estimate=light,
        compiler_params=room(8),
    )(pred, *parts, red, unit, slope, inv, *extra)


def share_kernel(wh, wl, a, b, c, d, sp, sq, dh, dl):
    k = pl.program_id(0)
    half = sp.shape[1]

    @pl.when(k == 0)
    def _():
        sp[...] = jnp.zeros_like(sp)
        sq[...] = jnp.zeros_like(sq)

    value = jnp.where(k < 2, jnp.where(k == 0, a[...], b[...]), jnp.where(k == 2, c[...], d[...]))
    upper, lower = split(value)
    dh[...], dl[...] = upper, lower
    for place, out in ((slice(0, half), sp), (slice(half, 2 * half), sq)):
        up, low = upper[:, place], lower[:, place]
        out[...] += mul(wh[...], up) + mul(wh[...], low) + mul(wl[...], up)


def share_of(wh, wl, pieces):
    depth, spots = wh.shape
    rows, width = spots // 4, pieces[0].shape[1]
    column = pl.BlockSpec((depth, rows), lambda k: (0, k))
    row = pl.BlockSpec((rows, width), lambda k: (k, 0))
    return pl.pallas_call(
        share_kernel,
        name="share",
        grid=(4,),
        in_specs=[column, column] + [whole((rows, width))] * 4,
        out_specs=[pl.BlockSpec((depth, width // 2), lambda k: (0, 0))] * 2 + [row, row],
        out_shape=[like(depth, width // 2)] * 2 + [like(spots, width, dtype=bf16)] * 2,
        cost_estimate=light,
        compiler_params=room(14),
    )(wh, wl, *pieces)


def back_kernel(eh2, el2, eh3, el3, dh2, dl2, dh3, dl3, out):
    total = mul_t(eh2[...], dh2[...]) + mul_t(eh2[...], dl2[...]) + mul_t(el2[...], dh2[...])
    total += mul_t(eh3[...], dh3[...]) + mul_t(eh3[...], dl3[...]) + mul_t(el3[...], dh3[...])
    out[...] = total


def back(e2, e3, d2, d3):
    depth, width = e2[0].shape
    spots = d2[0].shape[0]
    rows = spots // 4
    row = pl.BlockSpec((rows, width), lambda k: (k, 0))
    return pl.pallas_call(
        back_kernel,
        name="back",
        grid=(4,),
        in_specs=[whole((depth, width))] * 4 + [row] * 4,
        out_specs=pl.BlockSpec((depth, rows), lambda k: (0, k)),
        out_shape=like(depth, spots),
        cost_estimate=light,
        compiler_params=room(14),
    )(*e2, *e3, *d2, *d3)


def half_kernel(chain, info, wh, wl, eh0, el0, eh1, el1, mg, offset, a0, b0, a1, b1, *refs):
    k = pl.program_id(0)
    outs = refs[-5:]
    grad, shares = outs[0], outs[1:]
    half = shares[0].shape[1]
    pick = lambda a, b: split(jnp.where(k == 0, a[...], b[...]))

    @pl.when(k == 0)
    def _():
        for n, share in enumerate(shares):
            share[...] = refs[1 + n][...] if chain else jnp.zeros_like(share)

    total = mg[...]
    for n, (pieces, eh, el) in enumerate((((a0, b0), eh0, el0), ((a1, b1), eh1, el1))):
        upper, lower = pick(*pieces)
        total += mul_t(eh[...], upper) + mul_t(eh[...], lower) + mul_t(el[...], upper)
        for m in range(2):
            place = slice(m * half, (m + 1) * half)
            up, low = upper[:, place], lower[:, place]
            shares[2 * n + m][...] += mul(wh[...], up) + mul(wh[...], low) + mul(wl[...], up)
    value = (wh[...].astype(f32) + wl[...].astype(f32)) * (total + offset[0:1, :])
    width = value.shape[1] // 2
    turned = jnp.concatenate([value[:, width:], value[:, :width]], axis=1)
    grad[...] = jnp.where(info[info.shape[0] - 2] == 1, turned, value)


def half_of(info, base, wh, wl, e0, e1, mg, offset, pieces, chained=None):
    depth, spots = wh.shape
    rows, width = spots // 4, e0[0].shape[1]
    column = pl.BlockSpec((depth, rows), lambda k, info: (0, base + k))
    piece_specs, pieces_in = [], []
    for piece in pieces:
        piece_specs += [
            pl.BlockSpec((rows, width), functools.partial(lambda n, k, info: (n, 0), piece[1]), pipeline_mode=pl.Buffered(1))
        ]
        pieces_in.append(piece[0])
    extra = () if chained is None else chained
    extra_specs = [] if chained is None else [pl.BlockSpec(memory_space=pl.ANY)] + [whole((depth, width // 2))] * 4
    count = 1 + 2 + 4 + 2 + 4
    return pl.pallas_call(
        functools.partial(half_kernel, chained is not None),
        name="half",
        grid_spec=pltpu.PrefetchScalarGridSpec(
            num_scalar_prefetch=1,
            grid=(2,),
            in_specs=[column, column]
            + [whole((depth, width))] * 4
            + [column, pl.BlockSpec((8, rows), lambda k, info: (0, base + k))]
            + piece_specs
            + extra_specs,
            out_specs=[pl.BlockSpec((depth, rows), lambda k, info: (0, info[base + k]))]
            + [pl.BlockSpec((depth, width // 2), lambda k, info: (0, 0))] * 4,
        ),
        out_shape=[like(depth, spots)] + [like(depth, width // 2)] * 4,
        input_output_aliases={} if chained is None else {count: 0},
        cost_estimate=light,
        compiler_params=room(30),
    )(info, wh, wl, *e0, *e1, mg, offset, *pieces_in, *extra)


def small(kernel, name, outs, *operands, info=None, blocks=None, scratch=()):
    specs = []
    for n, operand in enumerate(operands):
        shape, index = (operand.shape, None) if blocks is None or n not in blocks else blocks[n]
        if index is None:
            index = lambda k, *info, rank=len(shape): (0,) * rank
        specs.append(pl.BlockSpec(shape, index, pipeline_mode=pl.Buffered(1)))
    out_specs = [whole(o.shape) for o in outs]
    scalars = () if info is None else (info,)
    return pl.pallas_call(
        kernel,
        name=name,
        grid_spec=pltpu.PrefetchScalarGridSpec(
            num_scalar_prefetch=len(scalars), grid=(1,), in_specs=specs, out_specs=out_specs, scratch_shapes=list(scratch)
        ),
        out_shape=outs,
        cost_estimate=light,
        compiler_params=room(8),
    )(*scalars, *operands)


def add(*parts):
    def kernel(*refs):
        total = refs[0][...]
        for ref in refs[1:-1]:
            total = total + ref[...]
        refs[-1][...] = total

    return small(kernel, "add", [like(*parts[0].shape)], *parts)[0]


def halves(table, axis, *others):
    rows, columns = table.shape
    half = (rows // 2, columns) if axis == 0 else (rows, columns // 2)

    def kernel(*refs):
        total = refs[0][...]
        for ref in refs[1:-2]:
            total = total + ref[...]
        if axis == 0:
            refs[-2][...], refs[-1][...] = total[: rows // 2], total[rows // 2 :]
        else:
            refs[-2][...], refs[-1][...] = total[:, : columns // 2], total[:, columns // 2 :]

    return small(kernel, "halves", [like(*half)] * 2, table, *others)


def part_total(rows, *parts):
    width = parts[0].shape[1]

    def kernel(*refs):
        total = refs[0][...]
        for ref in refs[1:-2]:
            total = total + ref[...]
        for n, out in enumerate(refs[-2:]):
            out[:rows] = total[n * rows : (n + 1) * rows]
            line = total[2 * rows :, n * rows : (n + 1) * rows]
            out[rows:] = jnp.concatenate([line, jnp.zeros((8, width - rows), f32)], axis=1)

    return small(kernel, "part_total", [like(rows + 8, width)] * 2, *parts)


def stack(p, r, rows):
    extra = p.shape[0] - rows

    def kernel(p, r, out):
        out[:rows], out[rows : 2 * rows] = p[:rows], r[:rows]
        if extra:
            out[2 * rows : 2 * rows + extra], out[2 * rows + extra :] = p[rows:], r[rows:]

    return small(kernel, "stack", [like(2 * p.shape[0], p.shape[1])], p, r)[0]


def rows_of(info, table, rows, per_part):
    shape = (rows, table.shape[1])

    def kernel(info, a, b, c, d, *outs):
        for ref, out in zip((a, b, c, d), outs):
            out[...] = ref[...]

    def index(part):
        return lambda k, info: ((info[info.shape[0] - 3] ^ part) * per_part + info[info.shape[0] - 4], 0)

    return small(
        kernel, "rows", [like(*shape)] * 4, *[table] * 4, info=info, blocks={r: (shape, index(r)) for r in range(4)}
    )


def chosen(part, refs):
    low = jnp.where(part == 0, refs[0][...], refs[1][...])
    return jnp.where(part < 2, low, jnp.where(part == 2, refs[2][...], refs[3][...]))


def go_home(info, preds):
    rows, width = preds[0].shape
    half = width // 2

    def kernel(info, a, b, c, d, *refs):
        outs, parts = refs[:4], refs[4:]
        for n in range(4):
            low, upper = ((a, b), (c, d))[n // 2]
            cut = slice(n % 2 * half, n % 2 * half + half)
            parts[n][:, :half], parts[n][:, half:] = low[:, cut], upper[:, cut]
        for n in range(4):
            outs[n][...] = chosen(info[info.shape[0] - 1] ^ n, parts)

    return small(
        kernel, "go_home", [like(rows, width)] * 4, *preds, info=info, scratch=[pltpu.VMEM((rows, width), f32)] * 4
    )


def settle(info, landed):
    rows, width = landed[0].shape

    def kernel(info, a, b, c, d, out):
        mine = info[info.shape[0] - 3] ^ info[info.shape[0] - 1]
        for n, z in enumerate((0, 2, 1, 3)):
            out[n * rows : (n + 1) * rows] = chosen(mine ^ z, (a, b, c, d))

    return small(kernel, "settle", [like(4 * rows, width)], *landed, info=info)[0]


def slide_rows(index, info, slides):
    return sum((index >= info[6 + q]).astype(jnp.int32) for q in range(slides))


def total_of(value):
    return jnp.sum(jnp.sum(value, axis=1, keepdims=True), axis=0, keepdims=True)


def first_message(info, low, high, prior, row, slides):
    rows, width = row.shape[1], low.shape[1]

    def kernel(info, low, high, prior, row, out, share):
        line = lax.broadcasted_iota(jnp.int32, prior.shape, 0)
        lane = lax.broadcasted_iota(jnp.int32, prior.shape, 1)
        slide = slide_rows(line * 128 + lane, info, slides)
        begin = info[4] + info[info.shape[0] - 4] * rows
        spot = begin + lax.broadcasted_iota(jnp.int32, (1, rows), 1)
        own = slide_rows(spot, info, slides)
        here = prior[pl.ds(begin // 128, rows // 128), :]
        here = jnp.concatenate([here[n : n + 1] for n in range(rows // 128)], axis=1)
        totals = jnp.zeros((1, rows), f32)
        for q in range(slides):
            totals = jnp.where(own == q, total_of(jnp.where(slide == q, prior[...], 0.0)), totals)
        here = here / totals
        share[...] = jnp.broadcast_to(here, share.shape)
        total = row[0:1, :]
        values = [total_of(jnp.where(own == q, total, 0.0)) for q in range(slides)]
        values += [total_of(jnp.where(own == q, here, 0.0)) for q in range(slides)]
        values += [total_of(here * (jnp.log(here) - jnp.log(total)))]
        place = lax.broadcasted_iota(jnp.int32, (1, 2 * width), 1)
        extra = jnp.zeros((1, 2 * width), f32)
        for n, value in enumerate(values):
            extra = jnp.where(place == n, value, extra)
        out[...] = jnp.zeros_like(out)
        out[0:3, :width], out[0:3, width:] = low[0:3, :], high[0:3, :]
        out[3:4, :] = extra

    outs = [like(8, 2 * width), like(8, rows)]
    return small(kernel, "first", outs, low, high, prior, row, info=info)


def second_message(info, low, high, cos):
    rows, width = cos.shape[1], low.shape[1]

    def kernel(info, low, high, cos, out):
        place = lax.broadcasted_iota(jnp.int32, (4, 2 * width), 1)
        line = lax.broadcasted_iota(jnp.int32, (4, 2 * width), 0)
        mine = (line == info[info.shape[0] - 3]) & (place // rows == info[info.shape[0] - 4])
        wide = jnp.concatenate([cos[0:4, :]] * (2 * width // rows), axis=1)
        out[0:3, :width], out[0:3, width:] = low[0:3, :], high[0:3, :]
        out[3:4, :] = jnp.where(place[0:1] == 0, total_of(cos[0:1, :]), 0.0)
        out[4:8, :] = jnp.where(mine, wide, 0.0)

    return small(kernel, "second", [like(8, 2 * width)], low, high, cos, info=info)[0]


def join_parts(part, mine, other):
    width = mine.shape[1] // 4

    def kernel(p, r, out):
        value = r[...]
        turned = jnp.concatenate(
            [value[:, (n ^ part) * width : ((n ^ part) + 1) * width] for n in range(4)], axis=1
        )
        line = lax.broadcasted_iota(jnp.int32, value.shape, 0)
        out[...] = p[...] + jnp.where(line < 3, turned, value)

    return small(kernel, "join", [like(*mine.shape)], mine, other)[0]


def finish(info, grad, weight, cosines, first, second, share, row, slides, scale, spots_all, genes_all):
    rows, width = grad.shape

    def kernel(info, grad, weight, c0, c1, c2, c3, first, second, share, row, out, losses, genes):
        spot = info[4] + info[info.shape[0] - 4] * rows + lax.broadcasted_iota(jnp.int32, (1, rows), 1)
        own = slide_rows(spot, info, slides)
        found = lambda n: first[3:4, n : n + 1]
        mass = jnp.zeros((1, rows), f32)
        density = found(2 * slides)
        for q in range(slides):
            mass = jnp.where(own == q, found(q), mass)
            density = density + found(slides + q) * jnp.log(found(q))
        total = row[0:1, :]
        mass_grad = scale * density_weight * (total / mass - share[0:1, :]) / slides
        summed = jnp.broadcast_to(jnp.sum(weight[...], axis=1, keepdims=True), (rows, 128))
        turned = jnp.concatenate([summed[n : n + 128].T[0:1] for n in range(0, rows, 128)], axis=1)
        offset = (mass_grad - turned) / total
        loss = -(total_of(c0[0:1] + c1[0:1] + c2[0:1] + c3[0:1]) / genes_all + second[3:4, 0:1] / spots_all)
        place = lax.broadcasted_iota(jnp.int32, losses.shape, 1)
        losses[...] = jnp.where(place == 0, loss, density / slides)
        out[:rows] = grad[...]
        wide = jnp.concatenate([offset, jnp.zeros((1, width - rows), f32)], axis=1)
        out[rows:] = jnp.broadcast_to(wide, (8, width))
        both = jnp.concatenate([c0[0:1, : width // 2], c1[0:1, : width // 2]], axis=1)
        genes[...] = jnp.broadcast_to(both, genes.shape)

    outs = [like(rows + 8, width), like(8, 128), like(8, width)]
    return small(kernel, "finish", outs, grad, weight, *cosines, first, second, share, row, info=info)


def offsets(tails, rows):
    def kernel(a, b, c, d, out):
        for n, ref in enumerate((a, b, c, d)):
            for m in range(2):
                place = slice((2 * n + m) * rows, (2 * n + m + 1) * rows)
                out[:, place] = ref[8 * m : 8 * m + 8, :rows]

    spec = ((16, tails[0].shape[1]), lambda k: (rows // 8, 0))
    return small(kernel, "offsets", [like(8, 8 * rows)], *tails, blocks={n: spec for n in range(4)})[0]


def gather_expression(a, ca, ya, b, cb, yb):
    depth, half = a.shape
    block = pl.BlockSpec((depth // 4, half), lambda k: (k, 0))

    def kernel(a, ca, ya, b, cb, yb, out):
        out[:, :half] = a[...] + ca[...] + ya[...]
        out[:, half:] = b[...] + cb[...] + yb[...]

    return pl.pallas_call(
        kernel,
        name="gather",
        grid=(4,),
        in_specs=[block] * 6,
        out_specs=pl.BlockSpec((depth // 4, 2 * half), lambda k: (k, 0)),
        out_shape=like(depth, 2 * half),
        cost_estimate=light,
        compiler_params=room(10),
    )(a, ca, ya, b, cb, yb)


def slice_4x2(logits, expression, spatial, density_prior, cell_slide, group_live, spot_counts):
    slot_dev, spot_dev = logits.shape
    gene_dev = expression.shape[1]
    groups, parts = 8, 4
    spots_all, genes_all = spot_dev * parts, gene_dev * parts
    slides = spot_counts.shape[0]
    rows = spot_dev // 8
    group_index, gene_index = lax.axis_index("cells"), lax.axis_index("genes")
    z, x = group_index // 2, group_index % 2
    scale = float(slot_dev * groups) * float(spots_all)
    spots_scale, genes_scale = scale / spots_all, scale / genes_all
    run = Order()
    same = lambda v: v

    place = 4 * x + 2 * (z % 2) + z // 2
    here = jnp.arange(group_live.shape[0], dtype=jnp.int32) == group_index
    info = jnp.concatenate(
        [
            jnp.stack([(2 * m ^ place) // 2 for m in range(4)] + [gene_index * spot_dev]),
            jnp.sum(jnp.where(here, group_live, 0))[None],
            jnp.cumsum(spot_counts),
            jnp.stack([place, gene_index, place % 2, z]),
        ]
    ).astype(jnp.int32)
    prior = density_prior.reshape(-1, 128)

    own_a, own_b = run(lambda e: halves(e, 1), expression)
    across_a, beside_a = over_y(own_a, "expr_y_a"), over_core(own_a, "expr_core_a")
    across_b, beside_b = over_y(own_b, "expr_y_b"), over_core(own_b, "expr_core_b")
    wh, wl, th, tl, tot = run(lambda *v: weigh(*v, slides), info, logits, cell_slide.reshape(-1, 128))
    pairs = (2 * rows,) * 4
    k01, k23, s45, s67, *e0 = run(lambda *v: blend(*v[:4], pairs, v[4]), th, tl, own_a, beside_a, tot)
    x_hi0, x_lo0 = over_x(s67, "x_hi_0"), over_x(s45, "x_lo_0")
    m01, m23, m45, m67, *e1 = run(lambda *v: blend(*v, pairs), th, tl, own_b, beside_b)
    z_hi1, z_lo1 = over_z(m67, 1, "z_hi_1"), over_z(m23, 1, "z_lo_1")
    beyond_a = over_core(run(same, across_a), "expr_beyond_a")
    z_0 = over_z(run(add, k23, x_hi0), 1, "z_0")
    x_1 = over_x(run(add, m45, z_hi1), "x_1")
    p01, p23, p45, p67, *e2 = run(lambda *v: blend(*v, pairs), th, tl, across_a, beyond_a)
    x_hi2, x_lo2 = over_x(p67, "x_hi_2"), over_x(p45, "x_lo_2")
    keep_0, send_0 = run(lambda *v: part_total(rows, *v), k01, x_lo0, z_0)
    w_0 = over_z(send_0, 2, "w_0")
    beyond_b = over_core(run(same, across_b), "expr_beyond_b")
    keep_1, send_1 = run(lambda p, *v: halves(p, 0, *v), m01, z_lo1, x_1)
    w_1 = over_z(send_1, 2, "w_1")
    z_2 = over_z(run(add, p23, x_hi2), 1, "z_2")
    q01, q23, q45, q67, *e3 = run(lambda *v: blend(*v, pairs), th, tl, across_b, beyond_b)
    x_hi3, x_lo3 = over_x(q67, "x_hi_3"), over_x(q45, "x_lo_3")
    g_own = run(lambda i, t: rows_of(i, t, rows, spot_dev // rows), info, spatial)
    g_1, g_2 = over_core(g_own[1], "spatial_core"), over_y(g_own[2], "spatial_y")
    g_3 = shift(g_own[3], lambda k: k ^ 3, "genes", "spatial_y_core")
    low_g, high_g = (g_own[0], g_1), (g_2, g_3)
    pred_0, gsum_0, part, inv, row = run(lambda p, r, *g: stats(p, r, g, 0), keep_0, w_0, *low_g)
    pred_1, gsum_1, part = run(
        lambda p, r, i, b, *g: stats(p, r, g, 1, i, b), keep_1, w_1, inv, part, *low_g
    )
    keep_2, send_2 = run(lambda p, *v: halves(p, 0, *v), p01, x_lo2, z_2)
    w_2 = over_z(send_2, 2, "w_2")
    z_3 = over_z(run(add, q23, x_hi3), 1, "z_3")
    pred_2, gsum_2, part = run(
        lambda p, r, i, b, *g: stats(p, r, g, 0, i, b), keep_2, w_2, inv, part, *high_g
    )
    first, share = run(lambda *v: first_message(*v, slides), info, gsum_0, gsum_2, prior, row)
    for name, move in (("x", over_x), ("z1", lambda v, n: over_z(v, 1, n))):
        first = run(add, first, move(first, "first_" + name))
    keep_3, send_3 = run(lambda p, *v: halves(p, 0, *v), q01, x_lo3, z_3)
    w_3 = over_z(send_3, 2, "w_3")
    first = run(add, first, over_z(first, 2, "first_z2"))
    first = run(functools.partial(join_parts, 1), first, over_core(first, "first_core"))
    first = run(functools.partial(join_parts, 2), first, over_y(first, "first_y"))
    pred_3, gsum_3, part, spot_unit, spot_slope, spot_cos = run(
        lambda p, r, i, b, *g: stats(p, r, g, 1, i, b, True, spots_scale), keep_3, w_3, inv, part, *high_g
    )
    shared = (spot_unit, spot_slope, inv)
    d2, weight, cos2 = run(
        lambda p, s, u, v, i, *g: grad_of(p, g, 0, s, 1, u, v, i, genes_scale), pred_2, first, *shared, *high_g
    )
    b_2 = over_z(d2, 2, "back_w_2")
    second = run(second_message, info, gsum_1, gsum_3, spot_cos)
    second_r = over_x(second, "second_x")
    d0, weight, cos0 = run(
        lambda p, s, u, v, i, b, *g: grad_of(p, g, 0, s, 0, u, v, i, genes_scale, b),
        pred_0, first, *shared, weight, *low_g,
    )
    second = run(add, second, second_r)
    second_r = over_z(second, 1, "second_z1")
    homes = run(lambda i, *v: go_home(i, v), info, pred_0, pred_1, pred_2, pred_3)
    second = run(add, second, second_r)
    second_r = over_z(second, 2, "second_z2")
    lo_2 = run(lambda p, r: stack(p, r, rows), d2, b_2)
    c_2, xlo_2 = over_z(lo_2, 1, "back_z_2"), over_x(lo_2, "back_xlo_2")
    second = run(add, second, second_r)
    second = run(functools.partial(join_parts, 1), second, over_core(second, "second_core"))
    second = run(functools.partial(join_parts, 2), second, over_y(second, "second_y"))
    d3, weight, cos3 = run(
        lambda p, s, u, v, i, b, *g: grad_of(p, g, 1, s, 1, u, v, i, genes_scale, b),
        pred_3, second, *shared, weight, *high_g,
    )
    d1, weight, cos1 = run(
        lambda p, s, u, v, i, b, *g: grad_of(p, g, 1, s, 0, u, v, i, genes_scale, b),
        pred_1, second, *shared, weight, *low_g,
    )
    d3, losses, own_cos = run(
        lambda i, g, w, a, b, c, d, *v: finish(i, g, w, (a, b, c, d), *v, slides, scale, spots_all, genes_all),
        info, d3, weight, cos0, cos1, cos2, cos3, first, second, share, row,
    )
    b_3 = over_z(d3, 2, "back_w_3")
    xhi_2 = over_x(run(same, c_2), "back_xhi_2")
    b_0 = over_z(d0, 2, "back_w_0")
    lo_3 = run(lambda p, r: stack(p, r, rows), d3, b_3)
    c_3, xlo_3 = over_z(lo_3, 1, "back_z_3"), over_x(lo_3, "back_xlo_3")
    lo_0 = run(lambda p, r: stack(p, r, rows), d0, b_0)
    c_0, xlo_0 = over_z(lo_0, 1, "back_z_0"), over_x(lo_0, "back_xlo_0")
    b_1 = over_z(d1, 2, "back_w_1")
    own_2, other_2, *split_2 = run(lambda h, l, *v: share_of(h, l, v), wh, wl, lo_2, c_2, xlo_2, xhi_2)
    chip_a = over_core(other_2, "share_core_a")
    xhi_3 = over_x(run(same, c_3), "back_xhi_3")
    lo_1 = run(lambda p, r: stack(p, r, rows), d1, b_1)
    c_1, xlo_1 = over_z(lo_1, 1, "back_z_1"), over_x(lo_1, "back_xlo_1")
    chip_a = over_y(run(add, own_2, chip_a), "share_y_a")
    xhi_0 = over_x(run(same, c_0), "back_xhi_0")
    own_3, other_3, *split_3 = run(lambda h, l, *v: share_of(h, l, v), wh, wl, lo_3, c_3, xlo_3, xhi_3)
    chip_b = over_core(other_3, "share_core_b")
    xhi_1 = over_x(run(same, c_1), "back_xhi_1")
    chip_b = over_y(run(add, own_3, chip_b), "share_y_b")
    landed = []
    for step, value in enumerate(homes):
        moves = [
            ((2 * zz + xx) * 4 + jj, (2 * jj + xx) * 4 + (jj ^ step ^ zz))
            for zz in range(4) for xx in range(2) for jj in range(4)
        ]
        with jax.named_scope("home"):
            landed.append(lax.ppermute(value, ("cells", "genes"), moves))
    mg = run(lambda *v: back(v[0:2], v[2:4], v[4:6], v[6:8]), *e2, *e3, *split_2, *split_3)
    offset = run(lambda *v: offsets(v, rows), lo_3, c_3, xlo_3, xhi_3)

    def half_step(base, info, wh, wl, e0h, e0l, e1h, e1l, mg, off, a, b, c, d, *past):
        pieces = [(a, 0), (b, 0), (c, 0), (d, 0)]
        return half_of(info, base, wh, wl, (e0h, e0l), (e1h, e1l), mg, off, pieces, past or None)

    chained = run(
        functools.partial(half_step, 0), info, wh, wl, *e0, *e1, mg, offset, lo_0, c_0, lo_1, c_1
    )
    pred_out = run(lambda i, *v: settle(i, v), info, *landed)
    grad_logits, s0p, s0q, s1p, s1q = run(
        functools.partial(half_step, 2), info, wh, wl, *e0, *e1, mg, offset, xlo_0, xhi_0, xlo_1, xhi_1, *chained
    )
    core_a, core_b = over_core(s0q, "own_core_a"), over_core(s1q, "own_core_b")
    grad_expression = run(gather_expression, s0p, core_a, chip_a, s1p, core_b, chip_b)
    spot_cos_out = lax.dynamic_index_in_dim(
        second[4:].reshape(groups, spots_all // groups), group_index, 0, keepdims=False
    )
    return (pred_out, own_cos[0], spot_cos_out, losses[0, 0], losses[0, 1], grad_logits, grad_expression)


def solution(mesh):
    fits = mesh.shape["cells"] == 8 and mesh.shape["genes"] == 4
    return jax.shard_map(
        slice_4x2 if fits else spread,
        mesh=mesh,
        in_specs=(
            P("cells", "genes"),
            P("cells", "genes"),
            P(None, "genes"),
            P(),
            P("cells"),
            P(),
            P(),
        ),
        out_specs=(
            P("cells", "genes"),
            P("genes"),
            P("cells"),
            P(),
            P(),
            P("cells", "genes"),
            P("cells", "genes"),
        ),
        check_vma=False,
    )
```

```python
import functools

import jax
import jax.numpy as jnp
from jax import lax
from jax.experimental import pallas as pl
from jax.experimental.pallas import tpu as pltpu
from jax.sharding import PartitionSpec as P

eps_norm = 1e-06
density_weight = 0.01
high = lax.Precision.HIGH
highest = lax.Precision.HIGHEST


def slide_of(spot_index, slide_ends):
    return jnp.sum((spot_index[:, None] >= slide_ends[None, :]).astype(jnp.int32), axis=1)


def live_of(group_live, group_index, slot_dev):
    groups = group_live.shape[0]
    here = jnp.arange(groups, dtype=jnp.int32) == group_index
    return jnp.arange(slot_dev, dtype=jnp.int32) < jnp.sum(jnp.where(here, group_live, 0))


def spread(logits, expression, spatial, density_prior, cell_slide, group_live, spot_counts):
    slot_dev, spot_dev = logits.shape
    gene_dev = expression.shape[1]
    groups, parts = lax.axis_size("cells"), lax.axis_size("genes")
    spots_all, genes_all = spot_dev * parts, gene_dev * parts
    spot_rows = spots_all // groups
    slides = spot_counts.shape[0]
    group_index, gene_index = lax.axis_index("cells"), lax.axis_index("genes")
    scale = float(slot_dev * groups) * float(spots_all)
    slide_ends = jnp.cumsum(spot_counts)
    spot_slide = slide_of(jnp.arange(spots_all, dtype=jnp.int32), slide_ends)
    own_slide = lax.dynamic_slice_in_dim(spot_slide, gene_index * spot_dev, spot_dev)
    slot_live = live_of(group_live, group_index, slot_dev)
    allowed = slot_live[:, None] & (cell_slide[:, None] == own_slide[None, :])
    weight = jnp.where(allowed, jnp.exp(logits), 0.0)
    spot_total = lax.psum(jnp.sum(weight, axis=0), "cells")
    mapping = weight / spot_total[None, :]
    full_map, full_total = (
        lax.all_gather(mapping, "genes", axis=1, tiled=True),
        lax.all_gather(spot_total, "genes", axis=0, tiled=True),
    )
    pred_rows = lax.psum_scatter(
        lax.dot_general(full_map, expression, (((0,), (0,)), ((), ())), precision=highest),
        "cells",
        scatter_dimension=0,
        tiled=True,
    )
    spatial_rows = lax.dynamic_slice_in_dim(spatial, group_index * spot_rows, spot_rows, 0)
    triple = (pred_rows * spatial_rows, pred_rows * pred_rows, spatial_rows * spatial_rows)
    gene_dot, gene_pp, gene_gg = lax.psum(
        jnp.stack([jnp.sum(part, axis=0) for part in triple]), "cells"
    )
    spot_dot, spot_pp, spot_gg = lax.psum(
        jnp.stack([jnp.sum(part, axis=1) for part in triple]), "genes"
    )
    gene_unit = lax.rsqrt(gene_pp + eps_norm) * lax.rsqrt(gene_gg + eps_norm)
    gene_cos = gene_dot * gene_unit
    spot_unit = lax.rsqrt(spot_pp + eps_norm) * lax.rsqrt(spot_gg + eps_norm)
    spot_cos = spot_dot * spot_unit
    gene_term = gene_unit[None, :] * spatial_rows - (gene_cos / (gene_pp + eps_norm))[None, :] * pred_rows
    spot_term = spot_unit[:, None] * spatial_rows - (spot_cos / (spot_pp + eps_norm))[:, None] * pred_rows
    grad_rows = -(scale / genes_all) * gene_term - scale / spots_all * spot_term
    loss_part = jnp.sum(gene_cos) / (genes_all * groups) + jnp.sum(spot_cos) / (spots_all * parts)
    cos_loss = -lax.psum(loss_part, ("cells", "genes"))
    grad_full = lax.all_gather(grad_rows, "cells", axis=0, tiled=True)
    member = spot_slide[None, :] == jnp.arange(slides, dtype=jnp.int32)[:, None]
    prior_total = jnp.sum(jnp.where(member, density_prior[None, :], 0.0), axis=1)
    prior_norm = density_prior / jnp.sum(jnp.where(member, prior_total[:, None], 0.0), axis=0)
    slide_sum = jnp.sum(jnp.where(member, full_total[None, :], 0.0), axis=1)
    share = full_total / jnp.sum(jnp.where(member, slide_sum[:, None], 0.0), axis=0)
    density_loss = jnp.sum(prior_norm * (jnp.log(prior_norm) - jnp.log(share))) / slides
    mass_grad = scale * density_weight * (share - prior_norm) / slides
    own_mass_grad = lax.dynamic_slice_in_dim(mass_grad, gene_index * spot_dev, spot_dev)
    partial_grad = lax.dot_general(expression, grad_full, (((1,), (1,)), ((), ())), precision=highest)
    map_grad = lax.psum_scatter(partial_grad, "genes", scatter_dimension=1, tiled=True)
    grad_expression = jnp.dot(full_map, grad_full, precision=highest)
    spot_weight = lax.psum(jnp.sum(mapping * map_grad, axis=0), "cells")
    grad_logits = mapping * (map_grad - spot_weight[None, :] + own_mass_grad[None, :])
    return (pred_rows, gene_cos, spot_cos, cos_loss, density_loss, grad_logits, grad_expression)


def shift(value, moves, axis, name):
    if isinstance(value, Later):
        return Later(value, moved=value, move=lambda v: shift(v, moves, axis, name))
    count = lax.axis_size(axis)
    pairs = [(k, moves(k)) for k in range(count) if moves(k) is not None]
    with jax.named_scope(name):
        return lax.ppermute(value, axis, pairs)


def over_x(value, name):
    return shift(value, lambda k: k ^ 1, "cells", name)


def over_y(value, name):
    return shift(value, lambda k: k ^ 2, "genes", name)


def over_core(value, name):
    return shift(value, lambda k: k ^ 1, "genes", name)


def over_z(value, step, name):
    return shift(value, lambda k: k ^ (2 * step), "cells", name)


class Later:
    def __init__(self, like, step=None, place=None, moved=None, move=None):
        self.shape, self.dtype = like.shape, like.dtype
        self.step, self.place, self.moved, self.move = step, place, moved, move


class Steps:
    def __init__(self):
        self.steps, self.values, self.arrived = {}, {}, {}

    def __call__(self, name, step, *operands):
        shapes = [jax.ShapeDtypeStruct(v.shape, v.dtype) for v in operands]
        out = jax.eval_shape(step, *shapes)
        leaves, tree = jax.tree.flatten(out)
        self.steps[name] = (step, operands)
        return jax.tree.unflatten(tree, [Later(v, name, n) for n, v in enumerate(leaves)])

    def value(self, operand):
        if not isinstance(operand, Later):
            return operand
        if operand.step is not None:
            return self.values[operand.step][operand.place]
        if operand not in self.arrived:
            self.arrived[operand] = operand.move(self.value(operand.moved))
        return self.arrived[operand]

    def run(self, order):
        last = None
        for name in order:
            step, operands = self.steps[name]
            operands = [self.value(v) for v in operands]
            if last is not None:
                operands, _ = lax.optimization_barrier((operands, last))
            self.values[name] = jax.tree.leaves(step(*operands))
            last = self.values[name][0]


f32, bf16 = jnp.float32, jnp.bfloat16


def split(value):
    upper = value.astype(bf16)
    return upper, (value - upper.astype(f32)).astype(bf16)


def mul(p, q):
    return jnp.dot(p, q, preferred_element_type=f32)


def mul_t(p, q):
    return lax.dot_general(p, q, (((1,), (1,)), ((), ())), preferred_element_type=f32)


def whole(shape):
    return pl.BlockSpec(shape, lambda *k: (0,) * len(shape), pipeline_mode=pl.Buffered(1))


def like(*shape, dtype=f32):
    return jax.ShapeDtypeStruct(shape, dtype)


def room(mebi):
    return pltpu.CompilerParams(vmem_limit_bytes=mebi << 20)


light = pl.CostEstimate(flops=1, bytes_accessed=1, transcendentals=0)


def weigh_kernel(slides, base, info, table, code, wh, wl, th, tl, tot):
    k = base + pl.program_id(0)
    depth, width = table.shape
    half = width // 2
    odd = info[info.shape[0] - 2]
    lane = lax.broadcasted_iota(jnp.int32, (1, width), 1)
    spot = info[4] + info[k] * width + jnp.where(odd == 1, lane ^ half, lane)
    slide = slide_rows(spot, info, slides).astype(f32)
    alive = info[6 + slides + info[5]]

    def step(a, total):
        at = pl.multiple_of(a * 128, 128)
        own = jnp.broadcast_to(code[pl.ds(a, 1), :].astype(f32), (128, 128)).T
        own = jnp.concatenate([own] * (width // 128), axis=1)
        live = at + lax.broadcasted_iota(jnp.int32, (128, width), 0) < alive
        value = table[pl.ds(at, 128), :]
        value = jnp.where(odd == 1, jnp.concatenate([value[:, half:], value[:, :half]], axis=1), value)
        w = jnp.where((own == slide) & live, jnp.exp(value), 0.0)
        wh[pl.ds(at, 128), :], wl[pl.ds(at, 128), :] = split(w)
        th[:, pl.ds(at, 128)], tl[:, pl.ds(at, 128)] = split(w.T)
        return total + jnp.sum(w, axis=0, keepdims=True)

    total = lax.fori_loop(0, depth // 128, step, jnp.zeros((1, width), f32), unroll=True)
    tot[...] = jnp.broadcast_to(total, tot.shape)


def weigh(info, logits, code, slides, base):
    depth, spots = logits.shape
    rows = spots // 4
    wide = pl.BlockSpec((depth, rows), lambda k, info: (0, k))
    tall = pl.BlockSpec((rows, depth), lambda k, info: (k, 0))
    return pl.pallas_call(
        functools.partial(weigh_kernel, slides, base),
        name="weigh",
        grid_spec=pltpu.PrefetchScalarGridSpec(
            num_scalar_prefetch=1,
            grid=(2,),
            in_specs=[
                pl.BlockSpec((depth, rows), lambda k, info: (0, info[base + k])),
                pl.BlockSpec(code.shape, lambda k, info: (0, 0)),
            ],
            out_specs=[wide, wide, tall, tall, pl.BlockSpec((8, rows), lambda k, info: (0, k))],
        ),
        out_shape=[
            like(depth, 2 * rows, dtype=bf16),
            like(depth, 2 * rows, dtype=bf16),
            like(2 * rows, depth, dtype=bf16),
            like(2 * rows, depth, dtype=bf16),
            like(8, 2 * rows),
        ],
        cost_estimate=light,
        compiler_params=room(12),
    )(info, logits, code)


def blend_kernel(groups, pair, sources, has_total, save, ep, eq0, eq1, *refs):
    k = pl.program_id(0)
    width = ep.shape[1]
    first, second = ep[...], jnp.where(k < 2, eq0[...], eq1[...])
    lefts, refs = refs[: 2 * sources], refs[2 * sources :]
    tots, outs = (refs[:sources], refs[sources:]) if has_total else ((), refs)

    @pl.when(k == 0)
    def _():
        for out, chunks in zip(outs, groups):
            out[...] = jnp.zeros_like(out)
            if has_total:
                for m, (n, begin) in enumerate(chunks):
                    out[len(chunks) * pair :, m * pair : (m + 1) * pair] = tots[n][:, begin : begin + pair]

    for place, part in ((slice(0, width), first), (slice(width, 2 * width), second)):
        upper, lower = split(part)
        if save:
            outs[-2][:, place], outs[-1][:, place] = upper, lower
        values = []
        for n in range(sources):
            th, tl = lefts[2 * n : 2 * n + 2]
            values.append(mul(th[...], upper) + mul(th[...], lower) + mul(tl[...], upper))
        for out, chunks in zip(outs, groups):
            for m, (n, begin) in enumerate(chunks):
                out[m * pair : (m + 1) * pair, place] += values[n][begin : begin + pair]


def blend(sources, ep, eq, groups, tots=(), save=True):
    spots, depth = sources[0][0].shape
    pair, width = spots // 2, ep.shape[1]
    deep = depth // 4
    extra = 8 if tots else 0
    column = pl.BlockSpec((spots, deep), lambda k: (0, k))
    row = pl.BlockSpec((deep, width), lambda k: (k, 0))
    both = pl.BlockSpec((deep, 2 * width), lambda k: (k, 0))
    if isinstance(eq, (list, tuple)):
        halved = [
            pl.BlockSpec((deep, width), lambda k: (jnp.minimum(k, 1), 0)),
            pl.BlockSpec((deep, width), lambda k: (jnp.maximum(k - 2, 0), 0)),
        ]
    else:
        eq, halved = (eq, eq), [row, row]
    number = len(sources)
    heights = [len(chunks) * pair + extra for chunks in groups]
    return pl.pallas_call(
        functools.partial(blend_kernel, groups, pair, number, bool(tots), save),
        name="blend",
        grid=(4,),
        in_specs=[row] + halved + [column] * 2 * number + [whole(t.shape) for t in tots],
        out_specs=[pl.BlockSpec((h, 2 * width), lambda k: (0, 0)) for h in heights] + [both, both] * save,
        out_shape=[like(h, 2 * width) for h in heights] + [like(depth, 2 * width, dtype=bf16)] * 2 * save,
        cost_estimate=light,
        compiler_params=room(14),
    )(ep, *eq, *[t for source in sources for t in source], *tots)


def stats_kernel(first, last, spots_scale, *refs):
    refs = list(refs)
    close, found, gp, gq = refs[:4]
    refs = refs[4:]
    rows = gp.shape[0]
    if first:
        inv, row = refs[-2:]
        total = close[rows : rows + 1, :rows] + found[rows : rows + 1, :rows]
        row[...] = jnp.broadcast_to(total, row.shape)
        for b in range(0, rows, 128):
            inv[b : b + 128, :] = 1.0 / jnp.broadcast_to(total[:, b : b + 128], (128, 128)).T
        inverse = inv[...]
    else:
        inverse = refs[0][...]
        before = refs[1]
        refs = refs[2:]
    pred, gsum, part = refs[:3]
    width = close.shape[1]
    value = (close[:rows] + found[:rows]) * jnp.concatenate([inverse] * (width // 128), axis=1)
    pred[...] = value
    g = jnp.concatenate([gp[...], gq[...]], axis=1)
    sums = []
    for n, product in enumerate((value * g, value * value, g * g)):
        gsum[n : n + 1, :] = jnp.sum(product, axis=0, keepdims=True)
        lanes = sum(product[:, c : c + 128] for c in range(0, width, 128))
        if not first:
            lanes = lanes + before[:, n * 128 : n * 128 + 128]
        sums.append(lanes)
        part[:, n * 128 : n * 128 + 128] = lanes
    gsum[3:, :] = jnp.zeros((5, width), f32)
    if last:
        unit_out, slope_out, cos_out = refs[3:]
        dot, pp, gg = [jnp.sum(lanes, axis=1, keepdims=True) for lanes in sums]
        unit = lax.rsqrt(pp + eps_norm) * lax.rsqrt(gg + eps_norm)
        cos = dot * unit
        wide = lambda v: jnp.broadcast_to(v, (rows, 128))
        unit_out[...] = wide(unit * spots_scale)
        slope_out[...] = wide(spots_scale * cos / (pp + eps_norm))
        for b in range(0, rows, 128):
            turned = wide(cos)[b : b + 128].T
            cos_out[:, b : b + 128] = turned[:8]


def part_blocks(parts, cut, rows):
    width = parts[0][0].shape[1]
    return [
        pl.BlockSpec((rows, width // 2), functools.partial(lambda n, k: (n, cut), n), pipeline_mode=pl.Buffered(1))
        for _, n in parts
    ]


def stats(close, found, parts, cut, inv=None, before=None, last=False, spots_scale=0.0):
    width = parts[0][0].shape[1]
    rows = close.shape[0] - (8 if inv is None else 0)
    first = inv is None
    outs = [like(rows, width), like(8, width), like(rows, 384)]
    if first:
        outs += [like(rows, 128), like(8, rows)]
    if last:
        outs += [like(rows, 128), like(rows, 128), like(8, rows)]
    extra = () if first else (inv, before)
    landed = [whole((rows + 8 if first else rows, width))] * 2
    return pl.pallas_call(
        functools.partial(stats_kernel, first, last, spots_scale),
        name="stats",
        grid=(1,),
        in_specs=landed + part_blocks(parts, cut, rows) + [whole(v.shape) for v in extra],
        out_specs=[whole(o.shape) for o in outs],
        out_shape=outs,
        cost_estimate=light,
        compiler_params=room(8),
    )(close, found, *[p for p, _ in parts], *extra)


def grad_kernel(genes_scale, chain, pred, gp, gq, red, unit_in, slope_in, inv, *refs):
    width = pred.shape[1]
    out, weight, cos_out = refs[-3:]
    dot, pp, gg = red[0:1, :], red[1:2, :], red[2:3, :]
    unit = lax.rsqrt(pp + eps_norm) * lax.rsqrt(gg + eps_norm)
    cos = dot * unit
    cos_out[...] = jnp.broadcast_to(cos, cos_out.shape)
    slope = genes_scale * cos / (pp + eps_norm)
    wide = lambda v: jnp.concatenate([v[...]] * (width // 128), axis=1)
    g = jnp.concatenate([gp[...], gq[...]], axis=1)
    p = pred[...]
    grad = (slope + wide(slope_in)) * p - (genes_scale * unit + wide(unit_in)) * g
    out[...] = grad * wide(inv)
    product = grad * p
    lanes = sum(product[:, c : c + 128] for c in range(0, width, 128))
    weight[...] = lanes + refs[0][...] if chain else lanes


def grad_of(pred, parts, cut, red, q, unit, slope, inv, genes_scale, before=None):
    rows, width = pred.shape
    extra = () if before is None else (before,)
    outs = [like(rows, width), like(rows, 128), like(8, width)]
    return pl.pallas_call(
        functools.partial(grad_kernel, genes_scale, before is not None),
        name="grad",
        grid=(1,),
        in_specs=[whole(pred.shape)] + part_blocks(parts, cut, rows) + [pl.BlockSpec((8, width), lambda k: (0, q))]
        + [whole(v.shape) for v in (unit, slope, inv) + extra],
        out_specs=[whole(o.shape) for o in outs],
        out_shape=outs,
        cost_estimate=light,
        compiler_params=room(8),
    )(pred, *[p for p, _ in parts], red, unit, slope, inv, *extra)


def share_kernel(wah, wal, wbh, wbl, a, b, c, d, p0, p1, q0, q1, dh, dl):
    k = pl.program_id(0)
    deep, half = p0.shape
    wh = jnp.where(k < 2, wah[...], wbh[...])
    wl = jnp.where(k < 2, wal[...], wbl[...])

    @pl.when(k == 0)
    def _():
        for out in (p0, p1, q0, q1):
            out[...] = jnp.zeros_like(out)

    value = jnp.where(k < 2, jnp.where(k == 0, a[...], b[...]), jnp.where(k == 2, c[...], d[...]))
    upper, lower = split(value)
    dh[...], dl[...] = upper, lower
    for place, top, bottom in ((slice(0, half), p0, p1), (slice(half, 2 * half), q0, q1)):
        up, low = upper[:, place], lower[:, place]
        value = mul(wh, up) + mul(wh, low) + mul(wl, up)
        top[...] += value[:deep]
        bottom[...] += value[deep:]


def share_of(weights, pieces):
    depth, spots = weights[0].shape[0], 2 * weights[0].shape[1]
    rows, width = spots // 4, pieces[0][0].shape[1]
    near = pl.BlockSpec((depth, rows), lambda k: (0, jnp.minimum(k, 1)))
    far = pl.BlockSpec((depth, rows), lambda k: (0, jnp.maximum(k - 2, 0)))
    row = pl.BlockSpec((rows, width), lambda k: (k, 0))
    return pl.pallas_call(
        share_kernel,
        name="share",
        grid=(4,),
        in_specs=[near, near, far, far]
        + [
            pl.BlockSpec((rows, width), functools.partial(lambda n, k: (n, 0), n), pipeline_mode=pl.Buffered(1))
            for _, n in pieces
        ],
        out_specs=[pl.BlockSpec((depth // 2, width // 2), lambda k: (0, 0))] * 4 + [row, row],
        out_shape=[like(depth // 2, width // 2)] * 4 + [like(spots, width, dtype=bf16)] * 2,
        cost_estimate=light,
        compiler_params=room(14),
    )(*weights, *[piece for piece, _ in pieces])


def back_kernel(eh2, el2, eh3, el3, dh2, dl2, dh3, dl3, out):
    total = mul_t(eh2[...], dh2[...]) + mul_t(eh2[...], dl2[...]) + mul_t(el2[...], dh2[...])
    total += mul_t(eh3[...], dh3[...]) + mul_t(eh3[...], dl3[...]) + mul_t(el3[...], dh3[...])
    out[...] = total


def back(e2, e3, d2, d3):
    depth, width = e2[0].shape
    spots = d2[0].shape[0]
    rows = spots // 4
    row = pl.BlockSpec((rows, width), lambda k: (k, 0))
    return pl.pallas_call(
        back_kernel,
        name="back",
        grid=(4,),
        in_specs=[whole((depth, width))] * 4 + [row] * 4,
        out_specs=pl.BlockSpec((depth, rows), lambda k: (0, k)),
        out_shape=like(depth, spots),
        cost_estimate=light,
        compiler_params=room(14),
    )(*e2, *e3, *d2, *d3)


def half_kernel(chain, where, info, wh, wl, eh0, el0, eh1, el1, mg, offset, a0, b0, a1, b1, *refs):
    k = pl.program_id(0)
    outs = refs[-9:]
    grad, shares = outs[0], outs[1:]
    added, past = refs[:2], refs[3:11]
    deep, half = shares[0].shape
    pick = lambda a, b: split(jnp.where(k == 0, a[...], b[...]))

    @pl.when(k == 0)
    def _():
        for n, share in enumerate(shares):
            share[...] = past[n][...] if chain else jnp.zeros_like(share)
        for n, more in enumerate(added):
            shares[where + n][...] += more[...]

    total = mg[...]
    for n, (pieces, eh, el) in enumerate((((a0, b0), eh0, el0), ((a1, b1), eh1, el1))):
        upper, lower = pick(*pieces)
        total += mul_t(eh[...], upper) + mul_t(eh[...], lower) + mul_t(el[...], upper)
        for m in range(2):
            place = slice(m * half, (m + 1) * half)
            up, low = upper[:, place], lower[:, place]
            value_of = mul(wh[...], up) + mul(wh[...], low) + mul(wl[...], up)
            shares[4 * n + 2 * m][...] += value_of[:deep]
            shares[4 * n + 2 * m + 1][...] += value_of[deep:]
    value = (wh[...].astype(f32) + wl[...].astype(f32)) * (total + offset[0:1, :])
    width = value.shape[1] // 2
    turned = jnp.concatenate([value[:, width:], value[:, :width]], axis=1)
    grad[...] = jnp.where(info[info.shape[0] - 2] == 1, turned, value)


def half_of(info, base, wh, wl, e0, e1, mg, offset, pieces, added, where, chained=None):
    depth, spots = wh.shape[0], 2 * wh.shape[1]
    rows, width = spots // 4, e0[0].shape[1]
    local = pl.BlockSpec((depth, rows), lambda k, info: (0, k))
    column = pl.BlockSpec((depth, rows), lambda k, info: (0, base + k))
    piece_specs, pieces_in = [], []
    for piece in pieces:
        piece_specs += [
            pl.BlockSpec((rows, width), functools.partial(lambda n, k, info: (n, 0), piece[1]), pipeline_mode=pl.Buffered(1))
        ]
        pieces_in.append(piece[0])
    extra = added + (() if chained is None else chained)
    extra_specs = [whole((depth // 2, width // 2))] * 2
    if chained is not None:
        extra_specs += [pl.BlockSpec(memory_space=pl.ANY)] + [whole((depth // 2, width // 2))] * 8
    count = 1 + 2 + 4 + 2 + 4 + 2
    return pl.pallas_call(
        functools.partial(half_kernel, chained is not None, where),
        name="half",
        grid_spec=pltpu.PrefetchScalarGridSpec(
            num_scalar_prefetch=1,
            grid=(2,),
            in_specs=[local, local]
            + [whole((depth, width))] * 4
            + [column, pl.BlockSpec((8, rows), lambda k, info: (0, base + k))]
            + piece_specs
            + extra_specs,
            out_specs=[pl.BlockSpec((depth, rows), lambda k, info: (0, info[base + k]))]
            + [pl.BlockSpec((depth // 2, width // 2), lambda k, info: (0, 0))] * 8,
        ),
        out_shape=[like(depth, spots)] + [like(depth // 2, width // 2)] * 8,
        input_output_aliases={} if chained is None else {count: 0},
        cost_estimate=light,
        compiler_params=room(26),
    )(info, wh, wl, *e0, *e1, mg, offset, *pieces_in, *extra)


def small(kernel, name, outs, *operands, info=None, blocks=None, scratch=()):
    specs = []
    for n, operand in enumerate(operands):
        shape, index = (operand.shape, None) if blocks is None or n not in blocks else blocks[n]
        if index is None:
            index = lambda k, *info, rank=len(shape): (0,) * rank
        specs.append(pl.BlockSpec(shape, index, pipeline_mode=pl.Buffered(1)))
    out_specs = [whole(o.shape) for o in outs]
    scalars = () if info is None else (info,)
    return pl.pallas_call(
        kernel,
        name=name,
        grid_spec=pltpu.PrefetchScalarGridSpec(
            num_scalar_prefetch=len(scalars), grid=(1,), in_specs=specs, out_specs=out_specs, scratch_shapes=list(scratch)
        ),
        out_shape=outs,
        cost_estimate=light,
        compiler_params=room(8),
    )(*scalars, *operands)


def add(*parts):
    def kernel(*refs):
        total = refs[0][...]
        for ref in refs[1:-1]:
            total = total + ref[...]
        refs[-1][...] = total

    return small(kernel, "add", [like(*parts[0].shape)], *parts)[0]


def add_two(p, q, r, t):
    def kernel(p, q, r, t, first, second):
        first[...], second[...] = p[...] + r[...], q[...] + t[...]

    return small(kernel, "add_two", [like(*p.shape), like(*q.shape)], p, q, r, t)


def halves(table, axis, *others):
    rows, columns = table.shape
    half = (rows // 2, columns) if axis == 0 else (rows, columns // 2)

    def kernel(*refs):
        total = refs[0][...]
        for ref in refs[1:-2]:
            total = total + ref[...]
        if axis == 0:
            refs[-2][...], refs[-1][...] = total[: rows // 2], total[rows // 2 :]
        else:
            refs[-2][...], refs[-1][...] = total[:, : columns // 2], total[:, columns // 2 :]

    return small(kernel, "halves", [like(*half)] * 2, table, *others)


def copy(value):
    def kernel(value, out):
        out[...] = value[...]

    return small(kernel, "copy", [like(*value.shape)], value)[0]


def take(value):
    anywhere = pl.BlockSpec(memory_space=pl.ANY)
    return pl.pallas_call(
        lambda value, out: None,
        name="take",
        in_specs=[anywhere],
        out_specs=anywhere,
        out_shape=like(*value.shape),
        input_output_aliases={0: 0},
        cost_estimate=light,
        compiler_params=room(1),
    )(value)


def part_total(rows, *parts):
    width = parts[0].shape[1]

    def kernel(*refs):
        total = refs[0][...]
        for ref in refs[1:-2]:
            total = total + ref[...]
        for n, out in enumerate(refs[-2:]):
            out[:rows] = total[n * rows : (n + 1) * rows]
            line = total[2 * rows :, n * rows : (n + 1) * rows]
            out[rows:] = jnp.concatenate([line, jnp.zeros((8, width - rows), f32)], axis=1)

    return small(kernel, "part_total", [like(rows + 8, width)] * 2, *parts)


def stack(p, r, rows):
    extra = p.shape[0] - rows

    def kernel(p, r, out):
        out[:rows], out[rows : 2 * rows] = p[:rows], r[:rows]
        if extra:
            out[2 * rows : 2 * rows + extra], out[2 * rows + extra :] = p[rows:], r[rows:]

    return small(kernel, "stack", [like(2 * p.shape[0], p.shape[1])], p, r)[0]


def rows_of(info, table, rows, per_part):
    shape = (rows, table.shape[1])

    def kernel(info, a, b, c, d, first, second, rest):
        first[...], second[...] = a[...], b[...]
        rest[:rows], rest[rows:] = c[...], d[...]

    def index(part):
        return lambda k, info: ((info[info.shape[0] - 3] ^ part) * per_part + info[info.shape[0] - 4], 0)

    return small(
        kernel, "rows", [like(*shape), like(*shape), like(2 * rows, shape[1])], *[table] * 4, info=info,
        blocks={r: (shape, index(r)) for r in range(4)},
    )


def rows_on(kept, landed):
    rows = kept.shape[0]

    def kernel(kept, landed, own, sent):
        own[...] = landed[:rows]
        sent[:rows], sent[rows:] = kept[...], landed[rows:]

    return small(kernel, "rows_on", [like(*kept.shape), like(2 * rows, kept.shape[1])], kept, landed)


def chosen(part, refs):
    low = jnp.where(part == 0, refs[0][...], refs[1][...])
    return jnp.where(part < 2, low, jnp.where(part == 2, refs[2][...], refs[3][...]))


def parted(low, upper):
    rows, width = low.shape
    half = width // 2

    def kernel(low, upper, out):
        for n in range(2):
            cut = slice(n * half, (n + 1) * half)
            out[n * rows : (n + 1) * rows, :half] = low[:, cut]
            out[n * rows : (n + 1) * rows, half:] = upper[:, cut]

    return small(kernel, "parted", [like(2 * rows, width)], low, upper)[0]


def traded(p, r):
    rows = p.shape[0] // 2

    def kernel(p, r, kept, sent):
        kept[:rows], kept[rows:] = p[:rows], r[:rows]
        sent[:rows], sent[rows:] = p[rows:], r[rows:]

    return small(kernel, "traded", [like(*p.shape)] * 2, p, r)


def by_z(info, p, r):
    rows = p.shape[0] // 2

    def kernel(info, p, r, kept, sent):
        turn = info[info.shape[0] - 3] ^ info[info.shape[0] - 1]
        pieces = (p[:rows], r[:rows], p[rows:], r[rows:])
        for out, first in ((kept, 0), (sent, 1)):
            for n in range(2):
                out[n * rows : (n + 1) * rows] = chosen(turn ^ (first + 2 * n), pieces)

    return small(kernel, "by_z", [like(*p.shape)] * 2, p, r, info=info)


def settle(info, p, r):
    rows = p.shape[0] // 2

    def kernel(info, p, r, out):
        pieces = (p[:rows], p[rows:], r[:rows], r[rows:])
        for n, z in enumerate((0, 2, 1, 3)):
            out[n * rows : (n + 1) * rows] = chosen(info[info.shape[0] - 1] ^ z, pieces)

    return small(kernel, "settle", [like(4 * rows, p.shape[1])], p, r, info=info)[0]


def slide_rows(index, info, slides):
    end, slide = 0, jnp.zeros(index.shape, jnp.int32)
    for q in range(slides):
        end = end + info[6 + q]
        slide = slide + (index >= end).astype(jnp.int32)
    return slide


def total_of(value):
    return jnp.sum(jnp.sum(value, axis=1, keepdims=True), axis=0, keepdims=True)


def first_message(info, low, high, prior, row, slides):
    rows, width = row.shape[1], low.shape[1]

    def kernel(info, low, high, prior, row, out, share):
        line = lax.broadcasted_iota(jnp.int32, prior.shape, 0)
        lane = lax.broadcasted_iota(jnp.int32, prior.shape, 1)
        slide = slide_rows(line * 128 + lane, info, slides)
        begin = info[4] + info[info.shape[0] - 4] * rows
        spot = begin + lax.broadcasted_iota(jnp.int32, (1, rows), 1)
        own = slide_rows(spot, info, slides)
        here = prior[pl.ds(begin // 128, rows // 128), :]
        here = jnp.concatenate([here[n : n + 1] for n in range(rows // 128)], axis=1)
        totals = jnp.zeros((1, rows), f32)
        for q in range(slides):
            totals = jnp.where(own == q, total_of(jnp.where(slide == q, prior[...], 0.0)), totals)
        here = here / totals
        share[...] = jnp.broadcast_to(here, share.shape)
        total = row[0:1, :]
        values = [total_of(jnp.where(own == q, total, 0.0)) for q in range(slides)]
        values += [total_of(jnp.where(own == q, here, 0.0)) for q in range(slides)]
        values += [total_of(here * (jnp.log(here) - jnp.log(total)))]
        place = lax.broadcasted_iota(jnp.int32, (1, 2 * width), 1)
        extra = jnp.zeros((1, 2 * width), f32)
        for n, value in enumerate(values):
            extra = jnp.where(place == n, value, extra)
        out[...] = jnp.zeros_like(out)
        out[0:3, :width], out[0:3, width:] = low[0:3, :], high[0:3, :]
        out[3:4, :] = extra

    outs = [like(8, 2 * width), like(8, rows)]
    return small(kernel, "first", outs, low, high, prior, row, info=info)


def second_message(info, low, high, cos):
    rows, width = cos.shape[1], low.shape[1]

    def kernel(info, low, high, cos, out):
        place = lax.broadcasted_iota(jnp.int32, (4, 2 * width), 1)
        line = lax.broadcasted_iota(jnp.int32, (4, 2 * width), 0)
        mine = (line == info[info.shape[0] - 3]) & (place // rows == info[info.shape[0] - 4])
        wide = jnp.concatenate([cos[0:4, :]] * (2 * width // rows), axis=1)
        out[0:3, :width], out[0:3, width:] = low[0:3, :], high[0:3, :]
        out[3:4, :] = jnp.where(place[0:1] == 0, total_of(cos[0:1, :]), 0.0)
        out[4:8, :] = jnp.where(mine, wide, 0.0)

    return small(kernel, "second", [like(8, 2 * width)], low, high, cos, info=info)[0]


def join_parts(part, mine, other):
    width = mine.shape[1] // 4

    def kernel(p, r, out):
        value = r[...]
        turned = jnp.concatenate(
            [value[:, (n ^ part) * width : ((n ^ part) + 1) * width] for n in range(4)], axis=1
        )
        line = lax.broadcasted_iota(jnp.int32, value.shape, 0)
        out[...] = p[...] + jnp.where(line < 3, turned, value)

    return small(kernel, "join", [like(*mine.shape)], mine, other)[0]


def finish(info, grad, weight, cosines, first, second, share, row, slides, scale, spots_all, genes_all):
    rows, width = grad.shape

    def kernel(info, grad, weight, c0, c1, c2, c3, first, second, share, row, out, losses, genes):
        spot = info[4] + info[info.shape[0] - 4] * rows + lax.broadcasted_iota(jnp.int32, (1, rows), 1)
        own = slide_rows(spot, info, slides)
        found = lambda n: first[3:4, n : n + 1]
        mass = jnp.zeros((1, rows), f32)
        density = found(2 * slides)
        for q in range(slides):
            mass = jnp.where(own == q, found(q), mass)
            density = density + found(slides + q) * jnp.log(found(q))
        total = row[0:1, :]
        mass_grad = scale * density_weight * (total / mass - share[0:1, :]) / slides
        summed = jnp.broadcast_to(jnp.sum(weight[...], axis=1, keepdims=True), (rows, 128))
        turned = jnp.concatenate([summed[n : n + 128].T[0:1] for n in range(0, rows, 128)], axis=1)
        offset = (mass_grad - turned) / total
        loss = -(total_of(c0[0:1] + c1[0:1] + c2[0:1] + c3[0:1]) / genes_all + second[3:4, 0:1] / spots_all)
        place = lax.broadcasted_iota(jnp.int32, losses.shape, 1)
        losses[...] = jnp.where(place == 0, loss, density / slides)
        out[:rows] = grad[...]
        wide = jnp.concatenate([offset, jnp.zeros((1, width - rows), f32)], axis=1)
        out[rows:] = jnp.broadcast_to(wide, (8, width))
        both = jnp.concatenate([c0[0:1, : width // 2], c1[0:1, : width // 2]], axis=1)
        genes[...] = jnp.broadcast_to(both, genes.shape)

    outs = [like(rows + 8, width), like(8, 128), like(8, width)]
    return small(kernel, "finish", outs, grad, weight, *cosines, first, second, share, row, info=info)


def offsets(tails, rows):
    def kernel(a, b, c, d, out):
        for n, ref in enumerate((a, b, c, d)):
            for m in range(2):
                place = slice((2 * n + m) * rows, (2 * n + m + 1) * rows)
                out[:, place] = ref[8 * m : 8 * m + 8, :rows]

    spec = ((16, tails[0].shape[1]), lambda k: (rows // 8, 0))
    return small(kernel, "offsets", [like(8, 8 * rows)], *tails, blocks={n: spec for n in range(4)})[0]


def gather_expression(*parts):
    depth, half = parts[0].shape
    each = len(parts) // 4

    def kernel(*refs):
        out = refs[-1]
        for n in range(2):

            @pl.when(pl.program_id(0) == n)
            def _():
                for m in range(2):
                    total = sum(ref[...] for ref in refs[(2 * m + n) * each : (2 * m + n + 1) * each])
                    out[:, m * half : (m + 1) * half] = total

    return pl.pallas_call(
        kernel,
        name="gather",
        grid=(2,),
        in_specs=[whole((depth, half))] * len(parts),
        out_specs=pl.BlockSpec((depth, 2 * half), lambda k: (k, 0)),
        out_shape=like(2 * depth, 2 * half),
        cost_estimate=light,
        compiler_params=room(40),
    )(*parts)


def slice_4x2(logits, expression, spatial, density_prior, cell_slide, group_live, spot_counts):
    slot_dev, spot_dev = logits.shape
    gene_dev = expression.shape[1]
    groups, parts = 8, 4
    spots_all, genes_all = spot_dev * parts, gene_dev * parts
    slides = spot_counts.shape[0]
    rows = spot_dev // 8
    group_index, gene_index = lax.axis_index("cells"), lax.axis_index("genes")
    z, x = group_index // 2, group_index % 2
    scale = float(slot_dev * groups) * float(spots_all)
    spots_scale, genes_scale = scale / spots_all, scale / genes_all
    run = Steps()
    early = lambda name, value: run(name, take, value) if name in order else value

    place = 4 * x + 2 * (z % 2) + z // 2
    info = jnp.concatenate(
        [
            jnp.stack([(2 * m ^ place) // 2 for m in range(4)] + [gene_index * spot_dev, group_index]),
            spot_counts,
            group_live,
            jnp.stack([place, gene_index, place % 2, z]),
        ]
    ).astype(jnp.int32)
    prior = density_prior.reshape(-1, 128)

    pair = 2 * rows
    code = cell_slide.reshape(-1, 128)
    both = lambda move, values, name: [move(v, name) for v in values]
    cut = lambda *v: halves(v[0], 0, *v[1:])
    one, two = [[(0, 0), (0, pair)]], [[(0, 0), (0, pair)], [(1, 0), (1, pair)]]
    own_a, own_b = run("own", lambda e: halves(e, 1), expression)
    across_a = over_y(own_a, "expr_y_a")
    beside_a, beside_b = over_core(own_a, "expr_core_a"), over_core(own_b, "expr_core_b")
    wbh, wbl, tbh, tbl, tot_b = run("weigh_b", lambda *v: weigh(*v, slides, 2), info, logits, code)
    sent_0, *e0 = run(
        "blend_0b", lambda h, l, p, q, t: blend([(h, l)], p, q, one, (t,)), tbh, tbl, own_a, beside_a, tot_b
    )
    x_0 = over_x(sent_0, "x_0")
    wah, wal, tah, tal, tot_a = run("weigh_a", lambda *v: weigh(*v, slides, 0), info, logits, code)
    full = lambda groups: lambda ah, al, bh, bl, p, *q: blend(
        [(ah, al), (bh, bl)], p, q if len(q) > 1 else q[0], groups
    )
    turned = (tah, tal, tbh, tbl)
    keep_1, sent_1, *e1 = run(
        "blend_1", full([[(0, 0), (1, 0)], [(0, pair), (1, pair)]]), *turned, own_b, beside_b
    )
    z_1 = over_z(sent_1, 1, "z_1")
    z_1 = early("taken_z1", z_1)
    (keep_0,) = run(
        "blend_0a", lambda h, l, p, q, t: blend([(h, l)], p, q, one, (t,), False), tah, tal, own_a, beside_a, tot_a
    )
    beyond_a = both(over_core, run("beyond_a", cut, across_a), "expr_beyond_a")
    across_b = over_y(run("own_b", copy, own_b), "expr_y_b")
    keep_2, sent_2, *e2 = run("blend_2", full(two), *turned, across_a, *beyond_a)
    x_2 = over_x(sent_2, "x_2")
    x_2 = early("taken_x2", x_2)
    keep_0, sent_0 = run("half_0", lambda *v: part_total(pair, *v), keep_0, x_0)
    z_0 = over_z(sent_0, 1, "z_0")
    keep_1, sent_1 = run("half_1", cut, keep_1, z_1)
    x_1 = over_x(sent_1, "x_1")
    beyond_b = both(over_core, run("beyond_b", cut, across_b), "expr_beyond_b")
    g_0, g_1, g_far = run("rows", lambda i, t: rows_of(i, t, rows, spot_dev // rows), info, spatial)
    g_far = over_y(g_far, "spatial_y")
    keep_0, sent_0 = run("quarter_0", lambda *v: part_total(rows, *v), keep_0, z_0)
    w_0 = over_z(sent_0, 2, "w_0")
    w_0 = early("taken_w0", w_0)
    q01, q23, q45, q67, *e3 = run(
        "blend_3", full([[(0, 0)], [(0, pair)], [(1, 0)], [(1, pair)]]), *turned, across_b, *beyond_b
    )
    x_hi3, x_lo3 = over_x(q67, "x_hi_3"), over_x(q45, "x_lo_3")
    x_lo3 = early("taken_xlo3f", x_lo3)
    keep_2, sent_2 = run("half_2", cut, keep_2, x_2)
    z_2 = over_z(sent_2, 1, "z_2")
    keep_1, sent_1 = run("quarter_1", cut, keep_1, x_1)
    w_1 = over_z(sent_1, 2, "w_1")
    w_1 = early("taken_w1", w_1)
    g_2, g_1 = run("rows_on", rows_on, g_1, g_far)
    g_1 = over_core(g_1, "spatial_core")
    pred_0, gsum_0, part_0, inv, row = run(
        "stats_0", lambda p, r, g, h: stats(p, r, [(g, 0), (h, 0)], 0), keep_0, w_0, g_0, g_1
    )
    keep_2, sent_2 = run("quarter_2", cut, keep_2, z_2)
    w_2 = over_z(sent_2, 2, "w_2")
    pred_1, gsum_1, part_1 = run(
        "stats_1", lambda p, r, i, b, g, h: stats(p, r, [(g, 0), (h, 0)], 1, i, b),
        keep_1, w_1, inv, part_0, g_0, g_1,
    )
    z_3 = over_z(run("half_3", add, q23, x_hi3), 1, "z_3")
    pred_2, gsum_2, part_2 = run(
        "stats_2", lambda p, r, i, b, g, h: stats(p, r, [(g, 0), (h, 1)], 0, i, b),
        keep_2, w_2, inv, part_1, g_2, g_1,
    )
    first, share = run("first", lambda *v: first_message(*v, slides), info, gsum_0, gsum_2, prior, row)
    keep_3, sent_3 = run("quarter_3", cut, q01, x_lo3, z_3)
    w_3 = over_z(sent_3, 2, "w_3")

    def sum_up(name, value):
        value = run(name + "_1", add, value, over_x(value, name + "_x"))
        value = run(name + "_2", add, value, over_z(value, 1, name + "_z1"))
        value = run(name + "_3", add, value, over_z(value, 2, name + "_z2"))
        value = run(name + "_4", functools.partial(join_parts, 1), value, over_core(value, name + "_core"))
        return run(name + "_5", functools.partial(join_parts, 2), value, over_y(value, name + "_y"))

    first = sum_up("first", first)
    pred_3, gsum_3, _, spot_unit, spot_slope, spot_cos = run(
        "stats_3", lambda p, r, i, b, g, h: stats(p, r, [(g, 0), (h, 1)], 1, i, b, True, spots_scale),
        keep_3, w_3, inv, part_2, g_2, g_1,
    )
    second = sum_up("second", run("second", second_message, info, gsum_1, gsum_3, spot_cos))
    shared = (spot_unit, spot_slope, inv)
    d2, weight_2, cos2 = run(
        "grad_2", lambda p, s, u, v, i, g, h: grad_of(p, [(g, 0), (h, 1)], 0, s, 1, u, v, i, genes_scale),
        pred_2, first, *shared, g_2, g_1,
    )
    b_2 = over_z(d2, 2, "back_w_2")
    d0, weight_0, cos0 = run(
        "grad_0", lambda p, s, u, v, i, b, g, h: grad_of(p, [(g, 0), (h, 0)], 0, s, 0, u, v, i, genes_scale, b),
        pred_0, first, *shared, weight_2, g_0, g_1,
    )
    home_r = over_y(run("home_0", parted, pred_2, pred_3), "home_y")
    home = run("home_1", parted, pred_0, pred_1)
    lo_2 = run("lo_2", lambda p, r: stack(p, r, rows), d2, b_2)
    c_2, xlo_2 = over_z(lo_2, 1, "back_z_2"), over_x(lo_2, "back_xlo_2")
    xlo_2 = early("taken_xlo2", xlo_2)
    b_0 = over_z(run("go_0", copy, d0), 2, "back_w_0")
    b_0 = early("taken_b0", b_0)
    d3, weight_3, cos3 = run(
        "grad_3", lambda p, s, u, v, i, b, g, h: grad_of(p, [(g, 0), (h, 1)], 1, s, 1, u, v, i, genes_scale, b),
        pred_3, second, *shared, weight_0, g_2, g_1,
    )
    d1, weight_1, cos1 = run(
        "grad_1", lambda p, s, u, v, i, b, g, h: grad_of(p, [(g, 0), (h, 0)], 1, s, 0, u, v, i, genes_scale, b),
        pred_1, second, *shared, weight_3, g_0, g_1,
    )
    d3, losses, own_cos = run(
        "finish",
        lambda i, g, w, a, b, c, d, *v: finish(i, g, w, (a, b, c, d), *v, slides, scale, spots_all, genes_all),
        info, d3, weight_1, cos0, cos1, cos2, cos3, first, second, share, row,
    )
    b_3 = over_z(d3, 2, "back_w_3")
    home, sent = run("home_2", traded, home, home_r)
    home_r = over_core(sent, "home_core")
    lo_0 = run("lo_0", lambda p, r: stack(p, r, rows), d0, b_0)
    c_0, xlo_0 = over_z(lo_0, 1, "back_z_0"), over_x(lo_0, "back_xlo_0")
    xlo_0 = early("taken_xlo0", xlo_0)
    hi_2 = run("hi_2", copy, c_2)
    xhi_2 = over_x(hi_2, "back_xhi_2")
    home, sent = run("home_3", lambda i, p, r: by_z(i, p, r), info, home, home_r)
    home_r = over_z(sent, 1, "home_z1")
    lo_3 = run("lo_3", lambda p, r: stack(p, r, rows), d3, b_3)
    c_3, xlo_3 = over_z(lo_3, 1, "back_z_3"), over_x(lo_3, "back_xlo_3")
    xlo_3 = early("taken_xlo3", xlo_3)
    hi_0 = run("hi_0", copy, c_0)
    xhi_0 = over_x(hi_0, "back_xhi_0")
    xhi_0 = early("taken_xhi0", xhi_0)
    b_1 = over_z(run("go_1", copy, d1), 2, "back_w_1")
    b_1 = early("taken_b1", b_1)
    weights = (wah, wal, wbh, wbl)
    back_share = lambda a, b, c, d, *v: share_of((a, b, c, d), [(p, 0) for p in v])
    *parts_2, dh2, dl2 = run("share_2", back_share, *weights, lo_2, hi_2, xlo_2, xhi_2)
    chip_a = both(over_core, parts_2[2:], "share_core_a")
    hi_3 = run("hi_3", copy, c_3)
    xhi_3 = over_x(hi_3, "back_xhi_3")
    chip_a = both(over_y, run("chip_a", add_two, *parts_2[:2], *chip_a), "share_y_a")
    chip_a[1] = early("taken_chip_a", chip_a[1])
    lo_1 = run("lo_1", lambda p, r: stack(p, r, rows), d1, b_1)
    c_1, xlo_1 = over_z(lo_1, 1, "back_z_1"), over_x(lo_1, "back_xlo_1")
    xlo_1 = early("taken_xlo1", xlo_1)
    *parts_3, dh3, dl3 = run("share_3", back_share, *weights, lo_3, hi_3, xlo_3, xhi_3)
    chip_b = both(over_core, parts_3[2:], "share_core_b")
    hi_1 = run("hi_1", copy, c_1)
    xhi_1 = over_x(hi_1, "back_xhi_1")
    chip_b = both(over_y, run("chip_b", add_two, *parts_3[:2], *chip_b), "share_y_b")
    home, sent = run("home_4", traded, home, home_r)
    home_r = over_z(sent, 2, "home_z2")
    mg = run("back", lambda *v: back(v[0:2], v[2:4], v[4:6], v[6:8]), *e2, *e3, dh2, dl2, dh3, dl3)
    offset = run("offsets", lambda *v: offsets(v, rows), lo_3, hi_3, xlo_3, xhi_3)

    def half_step(base, where, info, wh, wl, e0h, e0l, e1h, e1l, mg, off, a, b, c, d, p, q, *past):
        pieces = [(a, 0), (b, 0), (c, 0), (d, 0)]
        return half_of(info, base, wh, wl, (e0h, e0l), (e1h, e1l), mg, off, pieces, (p, q), where, past or None)

    chained = run(
        "near", functools.partial(half_step, 0, 0),
        info, wah, wal, *e0, *e1, mg, offset, lo_0, hi_0, lo_1, hi_1, *chip_a,
    )
    grad_logits, *shares = run(
        "far", functools.partial(half_step, 2, 4),
        info, wbh, wbl, *e0, *e1, mg, offset, xlo_0, xhi_0, xlo_1, xhi_1, *chip_b, *chained,
    )
    core_a, core_b = both(over_core, shares[2:4], "own_core_a"), both(over_core, shares[6:], "own_core_b")
    pred_out = run("settle", lambda i, p, r: settle(i, p, r), info, home, home_r)
    summands = []
    for kept, core in ((shares[0:2], core_a), (shares[4:6], core_b)):
        for n in range(2):
            summands += [kept[n], core[n]]
    grad_expression = run("gather", gather_expression, *summands)
    run.run(order)
    get = lambda v: run.value(v)
    spot_cos_out = lax.dynamic_index_in_dim(
        get(second)[4:].reshape(groups, spots_all // groups), group_index, 0, keepdims=False
    )
    losses, own_cos = get(losses), get(own_cos)
    return (
        get(pred_out), own_cos[0], spot_cos_out, losses[0, 0], losses[0, 1], get(grad_logits), get(grad_expression)
    )


order = (
    "own", "weigh_a", "weigh_b", "blend_0b", "blend_1", "own_b", "blend_0a", "rows", "beyond_a", "blend_2",
    "half_0", "half_1", "beyond_b", "quarter_0", "blend_3", "half_2", "taken_w0", "quarter_1", "rows_on",
    "quarter_2", "taken_w1", "half_3", "taken_xlo3f", "stats_0", "stats_1", "quarter_3", "stats_2", "first",
    "first_1", "first_2", "first_3", "first_4", "stats_3", "first_5", "grad_2", "second", "second_1", "grad_0",
    "go_0", "home_0", "second_2", "second_3", "lo_2", "second_4", "second_5", "grad_3", "grad_1", "finish",
    "lo_0", "taken_xlo2", "hi_2", "home_1", "home_2", "taken_xlo0", "lo_3", "go_1", "hi_0", "share_2", "lo_1",
    "hi_3", "home_3", "taken_xlo3", "chip_a", "share_3", "taken_chip_a", "hi_1", "home_4", "taken_xlo1",
    "chip_b", "offsets", "back", "near", "taken_xhi0", "far", "settle", "gather",
)


def solution(mesh):
    fits = mesh.shape["cells"] == 8 and mesh.shape["genes"] == 4
    return jax.shard_map(
        slice_4x2 if fits else spread,
        mesh=mesh,
        in_specs=(
            P("cells", "genes"),
            P("cells", "genes"),
            P(None, "genes"),
            P(),
            P("cells"),
            P(),
            P(),
        ),
        out_specs=(
            P("cells", "genes"),
            P("genes"),
            P("cells"),
            P(),
            P(),
            P("cells", "genes"),
            P("cells", "genes"),
        ),
        check_vma=False,
    )
```

```python
import functools

import jax
import jax.numpy as jnp
from jax import lax
from jax.experimental import pallas as pl
from jax.experimental.pallas import tpu as pltpu
from jax.sharding import PartitionSpec as P

eps_norm = 1e-06
density_weight = 0.01
high = lax.Precision.HIGH
highest = lax.Precision.HIGHEST


def slide_of(spot_index, slide_ends):
    return jnp.sum((spot_index[:, None] >= slide_ends[None, :]).astype(jnp.int32), axis=1)


def live_of(group_live, group_index, slot_dev):
    groups = group_live.shape[0]
    here = jnp.arange(groups, dtype=jnp.int32) == group_index
    return jnp.arange(slot_dev, dtype=jnp.int32) < jnp.sum(jnp.where(here, group_live, 0))


def spread(logits, expression, spatial, density_prior, cell_slide, group_live, spot_counts):
    slot_dev, spot_dev = logits.shape
    gene_dev = expression.shape[1]
    groups, parts = lax.axis_size("cells"), lax.axis_size("genes")
    spots_all, genes_all = spot_dev * parts, gene_dev * parts
    spot_rows = spots_all // groups
    slides = spot_counts.shape[0]
    group_index, gene_index = lax.axis_index("cells"), lax.axis_index("genes")
    scale = float(slot_dev * groups) * float(spots_all)
    slide_ends = jnp.cumsum(spot_counts)
    spot_slide = slide_of(jnp.arange(spots_all, dtype=jnp.int32), slide_ends)
    own_slide = lax.dynamic_slice_in_dim(spot_slide, gene_index * spot_dev, spot_dev)
    slot_live = live_of(group_live, group_index, slot_dev)
    allowed = slot_live[:, None] & (cell_slide[:, None] == own_slide[None, :])
    weight = jnp.where(allowed, jnp.exp(logits), 0.0)
    spot_total = lax.psum(jnp.sum(weight, axis=0), "cells")
    mapping = weight / spot_total[None, :]
    full_map, full_total = (
        lax.all_gather(mapping, "genes", axis=1, tiled=True),
        lax.all_gather(spot_total, "genes", axis=0, tiled=True),
    )
    pred_rows = lax.psum_scatter(
        lax.dot_general(full_map, expression, (((0,), (0,)), ((), ())), precision=highest),
        "cells",
        scatter_dimension=0,
        tiled=True,
    )
    spatial_rows = lax.dynamic_slice_in_dim(spatial, group_index * spot_rows, spot_rows, 0)
    triple = (pred_rows * spatial_rows, pred_rows * pred_rows, spatial_rows * spatial_rows)
    gene_dot, gene_pp, gene_gg = lax.psum(
        jnp.stack([jnp.sum(part, axis=0) for part in triple]), "cells"
    )
    spot_dot, spot_pp, spot_gg = lax.psum(
        jnp.stack([jnp.sum(part, axis=1) for part in triple]), "genes"
    )
    gene_unit = lax.rsqrt(gene_pp + eps_norm) * lax.rsqrt(gene_gg + eps_norm)
    gene_cos = gene_dot * gene_unit
    spot_unit = lax.rsqrt(spot_pp + eps_norm) * lax.rsqrt(spot_gg + eps_norm)
    spot_cos = spot_dot * spot_unit
    gene_term = gene_unit[None, :] * spatial_rows - (gene_cos / (gene_pp + eps_norm))[None, :] * pred_rows
    spot_term = spot_unit[:, None] * spatial_rows - (spot_cos / (spot_pp + eps_norm))[:, None] * pred_rows
    grad_rows = -(scale / genes_all) * gene_term - scale / spots_all * spot_term
    loss_part = jnp.sum(gene_cos) / (genes_all * groups) + jnp.sum(spot_cos) / (spots_all * parts)
    cos_loss = -lax.psum(loss_part, ("cells", "genes"))
    grad_full = lax.all_gather(grad_rows, "cells", axis=0, tiled=True)
    member = spot_slide[None, :] == jnp.arange(slides, dtype=jnp.int32)[:, None]
    prior_total = jnp.sum(jnp.where(member, density_prior[None, :], 0.0), axis=1)
    prior_norm = density_prior / jnp.sum(jnp.where(member, prior_total[:, None], 0.0), axis=0)
    slide_sum = jnp.sum(jnp.where(member, full_total[None, :], 0.0), axis=1)
    share = full_total / jnp.sum(jnp.where(member, slide_sum[:, None], 0.0), axis=0)
    density_loss = jnp.sum(prior_norm * (jnp.log(prior_norm) - jnp.log(share))) / slides
    mass_grad = scale * density_weight * (share - prior_norm) / slides
    own_mass_grad = lax.dynamic_slice_in_dim(mass_grad, gene_index * spot_dev, spot_dev)
    partial_grad = lax.dot_general(expression, grad_full, (((1,), (1,)), ((), ())), precision=highest)
    map_grad = lax.psum_scatter(partial_grad, "genes", scatter_dimension=1, tiled=True)
    grad_expression = jnp.dot(full_map, grad_full, precision=highest)
    spot_weight = lax.psum(jnp.sum(mapping * map_grad, axis=0), "cells")
    grad_logits = mapping * (map_grad - spot_weight[None, :] + own_mass_grad[None, :])
    return (pred_rows, gene_cos, spot_cos, cos_loss, density_loss, grad_logits, grad_expression)


def shift(value, moves, axis):
    if isinstance(value, Later):
        return Later(value, moved=value, move=lambda v: shift(v, moves, axis))
    count = lax.axis_size(axis)
    pairs = [(k, moves(k)) for k in range(count) if moves(k) is not None]
    return lax.ppermute(value, axis, pairs)


def over_x(value):
    return shift(value, lambda k: k ^ 1, "cells")


def over_y(value):
    return shift(value, lambda k: k ^ 2, "genes")


def over_core(value):
    return shift(value, lambda k: k ^ 1, "genes")


def over_z(value, step):
    return shift(value, lambda k: k ^ (2 * step), "cells")


class Step:
    (
        own, weigh_b, blend_0b, weigh_a, blend_1, blend_0a, beyond_a, own_b, blend_2, half_0, half_1,
        beyond_b, rows, quarter_0, blend_3, blend_4, half_2, quarter_1, rows_on, stats_0, quarter_2,
        stats_1, half_3, half_4, stats_2, first, quarter_3, quarter_4, stats_3, second, grad_2, grad_0,
        home_0, home_1, lo_2, go_0, grad_3, grad_1, finish, home_2, lo_0, hi_2, home_3, lo_3, hi_0, go_1,
        share_2, hi_3, chip_a, lo_1, share_3, hi_1, chip_b, home_4, back, offsets, near, far, settle, late,
        gather, taken_z1, taken_x2, taken_w0, taken_x3, taken_w1, taken_xlo2, taken_b0, taken_xlo0,
        taken_xlo3, taken_xhi0, taken_b1, taken_chip_a, taken_xlo1, first_1, first_2, first_3, second_1,
        second_2, second_3,
    ) = range(80)


class Later:
    def __init__(self, like, step=None, place=None, moved=None, move=None):
        self.shape, self.dtype = like.shape, like.dtype
        self.step, self.place, self.moved, self.move = step, place, moved, move


class Steps:
    def __init__(self):
        self.steps, self.values, self.arrived = {}, {}, {}

    def __call__(self, name, step, *operands):
        shapes = [jax.ShapeDtypeStruct(v.shape, v.dtype) for v in operands]
        out = jax.eval_shape(step, *shapes)
        leaves, tree = jax.tree.flatten(out)
        self.steps[name] = (step, operands)
        return jax.tree.unflatten(tree, [Later(v, name, n) for n, v in enumerate(leaves)])

    def value(self, operand):
        if not isinstance(operand, Later):
            return operand
        if operand.step is not None:
            return self.values[operand.step][operand.place]
        if operand not in self.arrived:
            self.arrived[operand] = operand.move(self.value(operand.moved))
        return self.arrived[operand]

    def run(self, order):
        last = None
        for name in order:
            step, operands = self.steps[name]
            operands = [self.value(v) for v in operands]
            if last is not None:
                operands, _ = lax.optimization_barrier((operands, last))
            self.values[name] = jax.tree.leaves(step(*operands))
            last = self.values[name][0]


f32, bf16 = jnp.float32, jnp.bfloat16


def split(value):
    upper = value.astype(bf16)
    return upper, (value - upper.astype(f32)).astype(bf16)


def mul(p, q):
    return jnp.dot(p, q, preferred_element_type=f32)


def mul_t(p, q):
    return lax.dot_general(p, q, (((1,), (1,)), ((), ())), preferred_element_type=f32)


def whole(shape):
    return pl.BlockSpec(shape, lambda *k: (0,) * len(shape), pipeline_mode=pl.Buffered(1))


def like(*shape, dtype=f32):
    return jax.ShapeDtypeStruct(shape, dtype)


def room(mebi):
    return pltpu.CompilerParams(vmem_limit_bytes=mebi << 20)


light = pl.CostEstimate(flops=1, bytes_accessed=1, transcendentals=0)


def in_hbm(value):
    return pltpu.with_memory_space_constraint(value, pltpu.HBM)


def weigh_kernel(slides, base, info, table, code, wh, wl, th, tl, tot):
    k = base + pl.program_id(0)
    depth, width = table.shape
    half = width // 2
    odd = info[info.shape[0] - 2]
    lane = lax.broadcasted_iota(jnp.int32, (1, width), 1)
    spot = info[4] + info[k] * width + jnp.where(odd == 1, lane ^ half, lane)
    slide = slide_rows(spot, info, slides).astype(f32)
    alive = info[6 + slides + info[5]]

    def step(a, total):
        at = pl.multiple_of(a * 128, 128)
        own = jnp.broadcast_to(code[pl.ds(a, 1), :].astype(f32), (128, 128)).T
        own = jnp.concatenate([own] * (width // 128), axis=1)
        live = at + lax.broadcasted_iota(jnp.int32, (128, width), 0) < alive
        value = table[pl.ds(at, 128), :]
        value = jnp.where(odd == 1, jnp.concatenate([value[:, half:], value[:, :half]], axis=1), value)
        w = jnp.where((own == slide) & live, jnp.exp(value), 0.0)
        wh[pl.ds(at, 128), :], wl[pl.ds(at, 128), :] = split(w)
        th[:, pl.ds(at, 128)], tl[:, pl.ds(at, 128)] = split(w.T)
        return total + jnp.sum(w, axis=0, keepdims=True)

    total = lax.fori_loop(0, depth // 128, step, jnp.zeros((1, width), f32), unroll=True)
    tot[...] = jnp.broadcast_to(total, tot.shape)


def weigh(info, logits, code, slides, base):
    depth, spots = logits.shape
    rows = spots // 4
    wide = pl.BlockSpec((depth, rows), lambda k, info: (0, k))
    tall = pl.BlockSpec((rows, depth), lambda k, info: (k, 0))
    return pl.pallas_call(
        functools.partial(weigh_kernel, slides, base),
        name="weigh",
        grid_spec=pltpu.PrefetchScalarGridSpec(
            num_scalar_prefetch=1,
            grid=(2,),
            in_specs=[
                pl.BlockSpec((depth, rows), lambda k, info: (0, info[base + k])),
                pl.BlockSpec(code.shape, lambda k, info: (0, 0)),
            ],
            out_specs=[wide, wide, tall, tall, pl.BlockSpec((8, rows), lambda k, info: (0, k))],
        ),
        out_shape=[
            like(depth, 2 * rows, dtype=bf16),
            like(depth, 2 * rows, dtype=bf16),
            like(2 * rows, depth, dtype=bf16),
            like(2 * rows, depth, dtype=bf16),
            like(8, 2 * rows),
        ],
        cost_estimate=light,
        compiler_params=room(12),
    )(info, in_hbm(logits), in_hbm(code))


def blend_kernel(groups, pair, sources, halved, has_total, save, *refs):
    k = pl.program_id(0)
    parts = []
    for half in halved:
        parts.append(jnp.where(k < 2, refs[0][...], refs[1][...]) if half else refs[0][...])
        refs = refs[1 + half :]
    width = parts[0].shape[1]
    lefts, refs = refs[: 2 * sources], refs[2 * sources :]
    tots, outs = (refs[:sources], refs[sources:]) if has_total else ((), refs)

    @pl.when(k == 0)
    def _():
        for out, chunks in zip(outs, groups):
            out[...] = jnp.zeros_like(out)
            if has_total:
                for m, (n, begin) in enumerate(chunks):
                    out[len(chunks) * pair :, m * pair : (m + 1) * pair] = tots[n][:, begin : begin + pair]

    for c, part in enumerate(parts):
        place = slice(c * width, (c + 1) * width)
        upper, lower = split(part)
        if save:
            outs[-2][:, place], outs[-1][:, place] = upper, lower
        values = []
        for n in range(sources):
            th, tl = lefts[2 * n : 2 * n + 2]
            values.append(mul(th[...], upper) + mul(th[...], lower) + mul(tl[...], upper))
        for out, chunks in zip(outs, groups):
            for m, (n, begin) in enumerate(chunks):
                out[m * pair : (m + 1) * pair, place] += values[n][begin : begin + pair]


def blend(sources, parts, groups, tots=(), save=True):
    spots, depth = sources[0][0].shape
    halved = [isinstance(part, tuple) for part in parts]
    pair, width = spots // 2, (parts[0][0] if halved[0] else parts[0]).shape[1]
    deep, wide = depth // 4, len(parts) * width
    extra = 8 if tots else 0
    column = pl.BlockSpec((spots, deep), lambda k: (0, k))
    row = pl.BlockSpec((deep, width), lambda k: (k, 0))
    top = pl.BlockSpec((deep, width), lambda k: (jnp.minimum(k, 1), 0))
    bottom = pl.BlockSpec((deep, width), lambda k: (jnp.maximum(k - 2, 0), 0))
    both = pl.BlockSpec((deep, wide), lambda k: (k, 0))
    specs, given = [], []
    for part, half in zip(parts, halved):
        specs += [top, bottom] if half else [row]
        given += part if half else [part]
    number = len(sources)
    heights = [len(chunks) * pair + extra for chunks in groups]
    return pl.pallas_call(
        functools.partial(blend_kernel, groups, pair, number, halved, bool(tots), save),
        name="blend",
        grid=(4,),
        in_specs=specs + [column] * 2 * number + [whole(t.shape) for t in tots],
        out_specs=[pl.BlockSpec((h, wide), lambda k: (0, 0)) for h in heights] + [both, both] * save,
        out_shape=[like(h, wide) for h in heights] + [like(depth, wide, dtype=bf16)] * 2 * save,
        cost_estimate=light,
        compiler_params=room(14),
    )(*given, *[t for source in sources for t in source], *tots)


def stats_kernel(first, last, spots_scale, pieces, *refs):
    refs = list(refs)
    glue = lambda parts: jnp.concatenate([ref[...] for ref in parts], axis=1)
    close, found = glue(refs[:pieces]), glue(refs[pieces : 2 * pieces])
    gp, gq = refs[2 * pieces : 2 * pieces + 2]
    refs = refs[2 * pieces + 2 :]
    rows = gp.shape[0]
    if first:
        inv, row = refs[-2:]
        total = close[rows : rows + 1, :rows] + found[rows : rows + 1, :rows]
        row[...] = jnp.broadcast_to(total, row.shape)
        for b in range(0, rows, 128):
            inv[b : b + 128, :] = 1.0 / jnp.broadcast_to(total[:, b : b + 128], (128, 128)).T
        inverse = inv[...]
    else:
        inverse = refs[0][...]
        before = refs[1]
        refs = refs[2:]
    pred, gsum, part = refs[:3]
    width = close.shape[1]
    value = (close[:rows] + found[:rows]) * jnp.concatenate([inverse] * (width // 128), axis=1)
    pred[...] = value
    g = jnp.concatenate([gp[...], gq[...]], axis=1)
    sums = []
    for n, product in enumerate((value * g, value * value, g * g)):
        gsum[n : n + 1, :] = jnp.sum(product, axis=0, keepdims=True)
        lanes = sum(product[:, c : c + 128] for c in range(0, width, 128))
        if not first:
            lanes = lanes + before[:, n * 128 : n * 128 + 128]
        sums.append(lanes)
        part[:, n * 128 : n * 128 + 128] = lanes
    gsum[3:, :] = jnp.zeros((5, width), f32)
    if last:
        unit_out, slope_out, cos_out = refs[3:]
        dot, pp, gg = [jnp.sum(lanes, axis=1, keepdims=True) for lanes in sums]
        unit = lax.rsqrt(pp + eps_norm) * lax.rsqrt(gg + eps_norm)
        cos = dot * unit
        wide = lambda v: jnp.broadcast_to(v, (rows, 128))
        unit_out[...] = wide(unit * spots_scale)
        slope_out[...] = wide(spots_scale * cos / (pp + eps_norm))
        for b in range(0, rows, 128):
            turned = wide(cos)[b : b + 128].T
            cos_out[:, b : b + 128] = turned[:8]


def part_blocks(parts, cut, rows):
    width = parts[0][0].shape[1]
    return [
        pl.BlockSpec((rows, width // 2), functools.partial(lambda n, k: (n, cut), n), pipeline_mode=pl.Buffered(1))
        for _, n in parts
    ]


def stats(close, found, parts, cut, inv=None, before=None, last=False, spots_scale=0.0):
    width = parts[0][0].shape[1]
    rows = close[0].shape[0] - (8 if inv is None else 0)
    first = inv is None
    outs = [like(rows, width), like(8, width), like(rows, 384)]
    if first:
        outs += [like(rows, 128), like(8, rows)]
    if last:
        outs += [like(rows, 128), like(rows, 128), like(8, rows)]
    extra = () if first else (inv, before)
    landed = [whole(v.shape) for v in close + found]
    return pl.pallas_call(
        functools.partial(stats_kernel, first, last, spots_scale, len(close)),
        name="stats",
        grid=(1,),
        in_specs=landed + part_blocks(parts, cut, rows) + [whole(v.shape) for v in extra],
        out_specs=[whole(o.shape) for o in outs],
        out_shape=outs,
        cost_estimate=light,
        compiler_params=room(8),
    )(*close, *found, *[p for p, _ in parts], *extra)


def grad_kernel(genes_scale, chain, pred, gp, gq, red, unit_in, slope_in, inv, *refs):
    width = pred.shape[1]
    out, weight, cos_out = refs[-3:]
    dot, pp, gg = red[0:1, :], red[1:2, :], red[2:3, :]
    unit = lax.rsqrt(pp + eps_norm) * lax.rsqrt(gg + eps_norm)
    cos = dot * unit
    cos_out[...] = jnp.broadcast_to(cos, cos_out.shape)
    slope = genes_scale * cos / (pp + eps_norm)
    wide = lambda v: jnp.concatenate([v[...]] * (width // 128), axis=1)
    g = jnp.concatenate([gp[...], gq[...]], axis=1)
    p = pred[...]
    grad = (slope + wide(slope_in)) * p - (genes_scale * unit + wide(unit_in)) * g
    out[...] = grad * wide(inv)
    product = grad * p
    lanes = sum(product[:, c : c + 128] for c in range(0, width, 128))
    weight[...] = lanes + refs[0][...] if chain else lanes


def grad_of(pred, parts, cut, red, q, unit, slope, inv, genes_scale, before=None):
    rows, width = pred.shape
    extra = () if before is None else (before,)
    outs = [like(rows, width), like(rows, 128), like(8, width)]
    return pl.pallas_call(
        functools.partial(grad_kernel, genes_scale, before is not None),
        name="grad",
        grid=(1,),
        in_specs=[whole(pred.shape)] + part_blocks(parts, cut, rows) + [pl.BlockSpec((8, width), lambda k: (0, q))]
        + [whole(v.shape) for v in (unit, slope, inv) + extra],
        out_specs=[whole(o.shape) for o in outs],
        out_shape=outs,
        cost_estimate=light,
        compiler_params=room(8),
    )(pred, *[p for p, _ in parts], red, unit, slope, inv, *extra)


def share_kernel(wah, wal, wbh, wbl, a, b, c, d, p0, p1, q0, q1, dh, dl):
    k = pl.program_id(0)
    deep, half = p0.shape
    wh = jnp.where(k < 2, wah[...], wbh[...])
    wl = jnp.where(k < 2, wal[...], wbl[...])

    @pl.when(k == 0)
    def _():
        for out in (p0, p1, q0, q1):
            out[...] = jnp.zeros_like(out)

    value = jnp.where(k < 2, jnp.where(k == 0, a[...], b[...]), jnp.where(k == 2, c[...], d[...]))
    upper, lower = split(value)
    dh[...], dl[...] = upper, lower
    for place, top, bottom in ((slice(0, half), p0, p1), (slice(half, 2 * half), q0, q1)):
        up, low = upper[:, place], lower[:, place]
        value = mul(wh, up) + mul(wh, low) + mul(wl, up)
        top[...] += value[:deep]
        bottom[...] += value[deep:]


def share_of(weights, pieces):
    depth, spots = weights[0].shape[0], 2 * weights[0].shape[1]
    rows, width = spots // 4, pieces[0][0].shape[1]
    near = pl.BlockSpec((depth, rows), lambda k: (0, jnp.minimum(k, 1)))
    far = pl.BlockSpec((depth, rows), lambda k: (0, jnp.maximum(k - 2, 0)))
    row = pl.BlockSpec((rows, width), lambda k: (k, 0))
    return pl.pallas_call(
        share_kernel,
        name="share",
        grid=(4,),
        in_specs=[near, near, far, far]
        + [
            pl.BlockSpec((rows, width), functools.partial(lambda n, k: (n, 0), n), pipeline_mode=pl.Buffered(1))
            for _, n in pieces
        ],
        out_specs=[pl.BlockSpec((depth // 2, width // 2), lambda k: (0, 0))] * 4 + [row, row],
        out_shape=[like(depth // 2, width // 2)] * 4 + [like(spots, width, dtype=bf16)] * 2,
        cost_estimate=light,
        compiler_params=room(14),
    )(*weights, *[piece for piece, _ in pieces])


def back_kernel(widths, *refs):
    out, rights = refs[-1], refs[-5:-1]
    begin, total = [0, 0], None
    for n, (unit, width) in enumerate(widths):
        eh, el = refs[2 * n : 2 * n + 2]
        place = slice(begin[unit], begin[unit] + width)
        begin[unit] += width
        dh, dl = [ref[:, place] for ref in rights[2 * unit : 2 * unit + 2]]
        value = mul_t(eh[...], dh) + mul_t(eh[...], dl) + mul_t(el[...], dh)
        total = value if total is None else total + value
    out[...] = total


def back(lefts, d2, d3):
    depth = lefts[0][1].shape[0]
    spots, width = d2[0].shape
    rows = spots // 4
    row = pl.BlockSpec((rows, width), lambda k: (k, 0))
    return pl.pallas_call(
        functools.partial(back_kernel, [(unit, upper.shape[1]) for unit, upper, _ in lefts]),
        name="back",
        grid=(4,),
        in_specs=[whole(part.shape) for _, *both in lefts for part in both] + [row] * 4,
        out_specs=pl.BlockSpec((depth, rows), lambda k: (0, k)),
        out_shape=like(depth, spots),
        cost_estimate=light,
        compiler_params=room(14),
    )(*[part for _, *both in lefts for part in both], *d2, *d3)


def half_kernel(sides, grads, chain, added, info, wh, wl, *refs):
    k = pl.program_id(0)
    refs = list(refs)
    if grads:
        eh0, el0, eh1, el1, mg, offset = refs[:6]
        refs = refs[6:]
    pieces, refs = (refs[0:2], refs[2:4]), refs[4:]
    number = 4 * len(sides)
    more, past = refs[: len(added)], refs[len(added) + (chain and grads) :][:number]
    shares = refs[-number:]
    grad = refs[-number - 1]
    deep, half = shares[0].shape

    @pl.when(k == 0)
    def _():
        for n, share in enumerate(shares):
            share[...] = past[n][...] if chain else jnp.zeros_like(share)
        for n, ref in zip(added, more):
            shares[n][...] += ref[:deep]
            shares[n + 1][...] += ref[deep:]

    total = mg[...] if grads else None
    for n in range(2):
        upper, lower = split(jnp.where(k == 0, pieces[n][0][...], pieces[n][1][...]))
        if grads:
            eh, el = ((eh0, el0), (eh1, el1))[n]
            total += mul_t(eh[...], upper) + mul_t(eh[...], lower) + mul_t(el[...], upper)
        for m, side in enumerate(sides):
            place = slice(side * half, (side + 1) * half)
            up, low = upper[:, place], lower[:, place]
            value = mul(wh[...], up) + mul(wh[...], low) + mul(wl[...], up)
            at = 2 * (len(sides) * n + m)
            shares[at][...] += value[:deep]
            shares[at + 1][...] += value[deep:]
    if grads:
        value = (wh[...].astype(f32) + wl[...].astype(f32)) * (total + offset[0:1, :])
        width = value.shape[1] // 2
        turned = jnp.concatenate([value[:, width:], value[:, :width]], axis=1)
        grad[...] = jnp.where(info[info.shape[0] - 2] == 1, turned, value)


def half_of(info, base, weights, pieces, sides, added=(), grads=(), grad=None, past=()):
    depth, width = weights[0].shape[0], pieces[0].shape[1]
    rows = weights[0].shape[1] // 2
    spots = 4 * rows
    local = pl.BlockSpec((depth, rows), lambda k, info: (0, k))
    column = pl.BlockSpec((depth, rows), lambda k, info: (0, base + k))
    line = pl.BlockSpec((8, rows), lambda k, info: (0, base + k))
    part = whole((depth // 2, width // 2))
    specs, given = [local, local], list(weights)
    if grads:
        specs += [whole((depth, width))] * 4 + [column, line]
        given += grads
    specs += [pl.BlockSpec((rows, width), lambda k, info: (0, 0), pipeline_mode=pl.Buffered(1))] * 4
    given += pieces
    specs += [whole((depth, width // 2))] * len(added)
    given += [array for _, array in added]
    aliases = {}
    if grad is not None:
        aliases = {1 + len(given): 0}
        specs.append(pl.BlockSpec(memory_space=pl.ANY))
        given.append(grad)
    specs += [part] * len(past)
    given += past
    number = 4 * len(sides)
    outs = [like(depth, spots)] if grads else []
    out_specs = [pl.BlockSpec((depth, rows), lambda k, info: (0, info[base + k]))] if grads else []
    return pl.pallas_call(
        functools.partial(half_kernel, sides, bool(grads), bool(past), [n for n, _ in added]),
        name="half",
        grid_spec=pltpu.PrefetchScalarGridSpec(
            num_scalar_prefetch=1,
            grid=(2,),
            in_specs=specs,
            out_specs=out_specs + [pl.BlockSpec((depth // 2, width // 2), lambda k, info: (0, 0))] * number,
        ),
        out_shape=outs + [like(depth // 2, width // 2)] * number,
        input_output_aliases=aliases,
        cost_estimate=light,
        compiler_params=room(26 if grads else 14),
    )(info, *given)


def small(kernel, name, outs, *operands, info=None, blocks=None, scratch=()):
    specs = []
    for n, operand in enumerate(operands):
        shape, index = (operand.shape, None) if blocks is None or n not in blocks else blocks[n]
        if index is None:
            index = lambda k, *info, rank=len(shape): (0,) * rank
        specs.append(pl.BlockSpec(shape, index, pipeline_mode=pl.Buffered(1)))
    out_specs = [whole(o.shape) for o in outs]
    scalars = () if info is None else (info,)
    return pl.pallas_call(
        kernel,
        name=name,
        grid_spec=pltpu.PrefetchScalarGridSpec(
            num_scalar_prefetch=len(scalars), grid=(1,), in_specs=specs, out_specs=out_specs, scratch_shapes=list(scratch)
        ),
        out_shape=outs,
        cost_estimate=light,
        compiler_params=room(8),
    )(*scalars, *operands)


def add(*parts):
    def kernel(*refs):
        total = refs[0][...]
        for ref in refs[1:-1]:
            total = total + ref[...]
        refs[-1][...] = total

    return small(kernel, "add", [like(*parts[0].shape)], *parts)[0]


def add_rows(p, q, r, t):
    rows = p.shape[0]

    def kernel(p, q, r, t, out):
        out[:rows], out[rows:] = p[...] + r[...], q[...] + t[...]

    return small(kernel, "add_rows", [like(2 * rows, p.shape[1])], p, q, r, t)[0]


def add_below(p, q, both):
    rows = p.shape[0]

    def kernel(p, q, both, first, second):
        first[...], second[...] = p[...] + both[:rows], q[...] + both[rows:]

    return small(kernel, "add_below", [like(*p.shape)] * 2, p, q, both)


def halves(table, axis, *others):
    rows, columns = table.shape
    half = (rows // 2, columns) if axis == 0 else (rows, columns // 2)

    def kernel(*refs):
        total = refs[0][...]
        for ref in refs[1:-2]:
            total = total + ref[...]
        if axis == 0:
            refs[-2][...], refs[-1][...] = total[: rows // 2], total[rows // 2 :]
        else:
            refs[-2][...], refs[-1][...] = total[:, : columns // 2], total[:, columns // 2 :]

    return small(kernel, "halves", [like(*half)] * 2, table, *others)


def copy(value):
    def kernel(value, out):
        out[...] = value[...]

    return small(kernel, "copy", [like(*value.shape)], value)[0]


def take(value):
    anywhere = pl.BlockSpec(memory_space=pl.ANY)
    return pl.pallas_call(
        lambda value, out: None,
        name="take",
        in_specs=[anywhere],
        out_specs=anywhere,
        out_shape=like(*value.shape),
        input_output_aliases={0: 0},
        cost_estimate=light,
        compiler_params=room(1),
    )(value)


def part_total(rows, *parts):
    width = parts[0].shape[1]

    def kernel(*refs):
        total = refs[0][...]
        for ref in refs[1:-2]:
            total = total + ref[...]
        for n, out in enumerate(refs[-2:]):
            out[:rows] = total[n * rows : (n + 1) * rows]
            line = total[2 * rows :, n * rows : (n + 1) * rows]
            out[rows:] = jnp.concatenate([line, jnp.zeros((8, width - rows), f32)], axis=1)

    return small(kernel, "part_total", [like(rows + 8, width)] * 2, *parts)


def stack(p, r, rows):
    extra = p.shape[0] - rows

    def kernel(p, r, out):
        out[:rows], out[rows : 2 * rows] = p[:rows], r[:rows]
        if extra:
            out[2 * rows : 2 * rows + extra], out[2 * rows + extra :] = p[rows:], r[rows:]

    return small(kernel, "stack", [like(2 * p.shape[0], p.shape[1])], p, r)[0]


def rows_of(info, table, rows, per_part):
    shape = (rows, table.shape[1])

    def kernel(info, a, b, c, d, first, second, rest):
        first[...], second[...] = a[...], b[...]
        rest[:rows], rest[rows:] = c[...], d[...]

    def index(part):
        return lambda k, info: ((info[info.shape[0] - 3] ^ part) * per_part + info[info.shape[0] - 4], 0)

    return small(
        kernel, "rows", [like(*shape), like(*shape), like(2 * rows, shape[1])], *[table] * 4, info=info,
        blocks={r: (shape, index(r)) for r in range(4)},
    )


def rows_on(kept, landed):
    rows = kept.shape[0]

    def kernel(kept, landed, own, sent):
        own[...] = landed[:rows]
        sent[:rows], sent[rows:] = kept[...], landed[rows:]

    return small(kernel, "rows_on", [like(*kept.shape), like(2 * rows, kept.shape[1])], kept, landed)


def chosen(part, refs):
    low = jnp.where(part == 0, refs[0][...], refs[1][...])
    return jnp.where(part < 2, low, jnp.where(part == 2, refs[2][...], refs[3][...]))


def parted(low, upper):
    rows, width = low.shape
    half = width // 2

    def kernel(low, upper, out):
        for n in range(2):
            cut = slice(n * half, (n + 1) * half)
            out[n * rows : (n + 1) * rows, :half] = low[:, cut]
            out[n * rows : (n + 1) * rows, half:] = upper[:, cut]

    return small(kernel, "parted", [like(2 * rows, width)], low, upper)[0]


def traded(p, r):
    rows = p.shape[0] // 2

    def kernel(p, r, kept, sent):
        kept[:rows], kept[rows:] = p[:rows], r[:rows]
        sent[:rows], sent[rows:] = p[rows:], r[rows:]

    return small(kernel, "traded", [like(*p.shape)] * 2, p, r)


def by_z(info, p, r):
    rows = p.shape[0] // 2

    def kernel(info, p, r, kept, sent):
        turn = info[info.shape[0] - 3] ^ info[info.shape[0] - 1]
        pieces = (p[:rows], r[:rows], p[rows:], r[rows:])
        for out, first in ((kept, 0), (sent, 1)):
            for n in range(2):
                out[n * rows : (n + 1) * rows] = chosen(turn ^ (first + 2 * n), pieces)

    return small(kernel, "by_z", [like(*p.shape)] * 2, p, r, info=info)


def settle(info, p, r):
    rows = p.shape[0] // 2

    def kernel(info, p, r, out):
        pieces = (p[:rows], p[rows:], r[:rows], r[rows:])
        for n, z in enumerate((0, 2, 1, 3)):
            out[n * rows : (n + 1) * rows] = chosen(info[info.shape[0] - 1] ^ z, pieces)

    return small(kernel, "settle", [like(4 * rows, p.shape[1])], p, r, info=info)[0]


def slide_rows(index, info, slides):
    end, slide = 0, jnp.zeros(index.shape, jnp.int32)
    for q in range(slides):
        end = end + info[6 + q]
        slide = slide + (index >= end).astype(jnp.int32)
    return slide


def total_of(value):
    return jnp.sum(jnp.sum(value, axis=1, keepdims=True), axis=0, keepdims=True)


def first_message(info, low, high, prior, row, slides):
    rows, width = row.shape[1], low.shape[1]

    def kernel(info, low, high, prior, row, out, share):
        line = lax.broadcasted_iota(jnp.int32, prior.shape, 0)
        lane = lax.broadcasted_iota(jnp.int32, prior.shape, 1)
        slide = slide_rows(line * 128 + lane, info, slides)
        begin = info[4] + info[info.shape[0] - 4] * rows
        spot = begin + lax.broadcasted_iota(jnp.int32, (1, rows), 1)
        own = slide_rows(spot, info, slides)
        here = prior[pl.ds(begin // 128, rows // 128), :]
        here = jnp.concatenate([here[n : n + 1] for n in range(rows // 128)], axis=1)
        totals = jnp.zeros((1, rows), f32)
        for q in range(slides):
            totals = jnp.where(own == q, total_of(jnp.where(slide == q, prior[...], 0.0)), totals)
        here = here / totals
        share[...] = jnp.broadcast_to(here, share.shape)
        total = row[0:1, :]
        values = [total_of(jnp.where(own == q, total, 0.0)) for q in range(slides)]
        values += [total_of(jnp.where(own == q, here, 0.0)) for q in range(slides)]
        values += [total_of(here * (jnp.log(here) - jnp.log(total)))]
        place = lax.broadcasted_iota(jnp.int32, (1, 2 * width), 1)
        extra = jnp.zeros((1, 2 * width), f32)
        for n, value in enumerate(values):
            extra = jnp.where(place == n, value, extra)
        out[...] = jnp.zeros_like(out)
        out[0:3, :width], out[0:3, width:] = low[0:3, :], high[0:3, :]
        out[3:4, :] = extra

    outs = [like(8, 2 * width), like(8, rows)]
    return small(kernel, "first", outs, low, high, prior, row, info=info)


def second_message(info, low, high, cos):
    rows, width = cos.shape[1], low.shape[1]

    def kernel(info, low, high, cos, out):
        place = lax.broadcasted_iota(jnp.int32, (4, 2 * width), 1)
        line = lax.broadcasted_iota(jnp.int32, (4, 2 * width), 0)
        mine = (line == info[info.shape[0] - 3]) & (place // rows == info[info.shape[0] - 4])
        wide = jnp.concatenate([cos[0:4, :]] * (2 * width // rows), axis=1)
        out[0:3, :width], out[0:3, width:] = low[0:3, :], high[0:3, :]
        out[3:4, :] = jnp.where(place[0:1] == 0, total_of(cos[0:1, :]), 0.0)
        out[4:8, :] = jnp.where(mine, wide, 0.0)

    return small(kernel, "second", [like(8, 2 * width)], low, high, cos, info=info)[0]


def join_parts(mine, *others):
    width = mine.shape[1] // 4

    def kernel(mine, *refs):
        total = mine[...]
        line = lax.broadcasted_iota(jnp.int32, total.shape, 0)
        for part, ref in enumerate(refs[:-1], 1):
            value = ref[...]
            turned = jnp.concatenate(
                [value[:, (n ^ part) * width : ((n ^ part) + 1) * width] for n in range(4)], axis=1
            )
            total = total + jnp.where(line < 3, turned, value)
        refs[-1][...] = total

    return small(kernel, "join", [like(*mine.shape)], mine, *others)[0]


def finish(info, grad, weight, cosines, first, second, share, row, slides, scale, spots_all, genes_all):
    rows, width = grad.shape

    def kernel(info, grad, weight, c0, c1, c2, c3, first, second, share, row, out, losses, genes):
        spot = info[4] + info[info.shape[0] - 4] * rows + lax.broadcasted_iota(jnp.int32, (1, rows), 1)
        own = slide_rows(spot, info, slides)
        found = lambda n: first[3:4, n : n + 1]
        mass = jnp.zeros((1, rows), f32)
        density = found(2 * slides)
        for q in range(slides):
            mass = jnp.where(own == q, found(q), mass)
            density = density + found(slides + q) * jnp.log(found(q))
        total = row[0:1, :]
        mass_grad = scale * density_weight * (total / mass - share[0:1, :]) / slides
        summed = jnp.broadcast_to(jnp.sum(weight[...], axis=1, keepdims=True), (rows, 128))
        turned = jnp.concatenate([summed[n : n + 128].T[0:1] for n in range(0, rows, 128)], axis=1)
        offset = (mass_grad - turned) / total
        loss = -(total_of(c0[0:1] + c1[0:1] + c2[0:1] + c3[0:1]) / genes_all + second[3:4, 0:1] / spots_all)
        place = lax.broadcasted_iota(jnp.int32, losses.shape, 1)
        losses[...] = jnp.where(place == 0, loss, density / slides)
        out[:rows] = grad[...]
        wide = jnp.concatenate([offset, jnp.zeros((1, width - rows), f32)], axis=1)
        out[rows:] = jnp.broadcast_to(wide, (8, width))
        both = jnp.concatenate([c0[0:1, : width // 2], c1[0:1, : width // 2]], axis=1)
        genes[...] = jnp.broadcast_to(both, genes.shape)

    outs = [like(rows + 8, width), like(8, 128), like(8, width)]
    return small(kernel, "finish", outs, grad, weight, *cosines, first, second, share, row, info=info)


def offsets(tails, rows):
    def kernel(a, b, c, d, out):
        for n, ref in enumerate((a, b, c, d)):
            for m in range(2):
                place = slice((2 * n + m) * rows, (2 * n + m + 1) * rows)
                out[:, place] = ref[8 * m : 8 * m + 8, :rows]

    spec = ((16, tails[0].shape[1]), lambda k: (rows // 8, 0))
    return small(kernel, "offsets", [like(8, 8 * rows)], *tails, blocks={n: spec for n in range(4)})[0]


def gather_expression(*parts):
    depth, half = parts[0].shape
    each = len(parts) // 4

    def kernel(*refs):
        out = refs[-1]
        for n in range(2):

            @pl.when(pl.program_id(0) == n)
            def _():
                for m in range(2):
                    total = sum(ref[...] for ref in refs[(2 * m + n) * each : (2 * m + n + 1) * each])
                    out[:, m * half : (m + 1) * half] = total

    return pl.pallas_call(
        kernel,
        name="gather",
        grid=(2,),
        in_specs=[whole((depth, half))] * len(parts),
        out_specs=pl.BlockSpec((depth, 2 * half), lambda k: (k, 0)),
        out_shape=like(2 * depth, 2 * half),
        cost_estimate=light,
        compiler_params=room(40),
    )(*parts)


def slice_4x2(logits, expression, spatial, density_prior, cell_slide, group_live, spot_counts):
    slot_dev, spot_dev = logits.shape
    gene_dev = expression.shape[1]
    groups, parts = 8, 4
    spots_all, genes_all = spot_dev * parts, gene_dev * parts
    slides = spot_counts.shape[0]
    rows = spot_dev // 8
    group_index, gene_index = lax.axis_index("cells"), lax.axis_index("genes")
    z, x = group_index // 2, group_index % 2
    scale = float(slot_dev * groups) * float(spots_all)
    spots_scale, genes_scale = scale / spots_all, scale / genes_all
    run = Steps()
    early = lambda name, value: run(name, take, value) if name in order else value

    place = 4 * x + 2 * (z % 2) + z // 2
    info = jnp.concatenate(
        [
            jnp.stack([(2 * m ^ place) // 2 for m in range(4)] + [gene_index * spot_dev, group_index]),
            spot_counts,
            group_live,
            jnp.stack([place, gene_index, place % 2, z]),
        ]
    ).astype(jnp.int32)
    prior = density_prior.reshape(-1, 128)

    pair = 2 * rows
    code = cell_slide.reshape(-1, 128)
    both = lambda move, values: [move(v) for v in values]
    cut = lambda *v: halves(v[0], 0, *v[1:])
    one, two = [[(0, 0), (0, pair)]], [[(0, 0), (0, pair)], [(1, 0), (1, pair)]]
    own_a, own_b = run(Step.own, lambda e: halves(in_hbm(e), 1), expression)
    across_a = over_y(own_a)
    beside_a, beside_b = over_core(own_a), over_core(own_b)
    wbh, wbl, tbh, tbl, tot_b = run(Step.weigh_b, lambda *v: weigh(*v, slides, 2), info, logits, code)
    sent_0, *e0 = run(
        Step.blend_0b, lambda h, l, p, q, t: blend([(h, l)], [p, q], one, (t,)), tbh, tbl, own_a, beside_a, tot_b
    )
    x_0 = over_x(sent_0)
    wah, wal, tah, tal, tot_a = run(Step.weigh_a, lambda *v: weigh(*v, slides, 0), info, logits, code)
    full = lambda groups, gather: lambda ah, al, bh, bl, *v: blend([(ah, al), (bh, bl)], gather(*v), groups)
    turned = (tah, tal, tbh, tbl)
    keep_1, sent_1, *e1 = run(
        Step.blend_1, full([[(0, 0), (1, 0)], [(0, pair), (1, pair)]], lambda p, q: [p, q]), *turned, own_b, beside_b
    )
    z_1 = over_z(sent_1, 1)
    z_1 = early(Step.taken_z1, z_1)
    (keep_0,) = run(
        Step.blend_0a, lambda h, l, p, q, t: blend([(h, l)], [p, q], one, (t,), False), tah, tal, own_a, beside_a, tot_a
    )
    beyond_a = both(over_core, run(Step.beyond_a, cut, across_a))
    across_b = over_y(run(Step.own_b, copy, own_b))
    keep_2, sent_2, *e2 = run(Step.blend_2, full(two, lambda p, *q: [p, q]), *turned, across_a, *beyond_a)
    x_2 = over_x(sent_2)
    x_2 = early(Step.taken_x2, x_2)
    keep_0, sent_0 = run(Step.half_0, lambda *v: part_total(pair, *v), keep_0, x_0)
    z_0 = over_z(sent_0, 1)
    keep_1, sent_1 = run(Step.half_1, cut, keep_1, z_1)
    x_1 = over_x(sent_1)
    beyond_b = both(over_core, run(Step.beyond_b, cut, across_b))
    g_0, g_1, g_far = run(Step.rows, lambda i, t: rows_of(i, t, rows, spot_dev // rows), info, spatial)
    g_far = over_y(g_far)
    keep_0, sent_0 = run(Step.quarter_0, lambda *v: part_total(rows, *v), keep_0, z_0)
    w_0 = over_z(sent_0, 2)
    w_0 = early(Step.taken_w0, w_0)
    keep_3, sent_3, *e3 = run(Step.blend_3, full(two, lambda p: [p]), *turned, across_b)
    x_3 = over_x(sent_3)
    keep_4, sent_4, *e4 = run(Step.blend_4, full(two, lambda *q: [q]), *turned, *beyond_b)
    x_4 = over_x(sent_4)
    x_3 = early(Step.taken_x3, x_3)
    keep_2, sent_2 = run(Step.half_2, cut, keep_2, x_2)
    z_2 = over_z(sent_2, 1)
    keep_1, sent_1 = run(Step.quarter_1, cut, keep_1, x_1)
    w_1 = over_z(sent_1, 2)
    w_1 = early(Step.taken_w1, w_1)
    g_2, g_1 = run(Step.rows_on, rows_on, g_1, g_far)
    g_1 = over_core(g_1)
    pred_0, gsum_0, part_0, inv, row = run(
        Step.stats_0, lambda p, r, g, h: stats([p], [r], [(g, 0), (h, 0)], 0), keep_0, w_0, g_0, g_1
    )
    keep_2, sent_2 = run(Step.quarter_2, cut, keep_2, z_2)
    w_2 = over_z(sent_2, 2)
    pred_1, gsum_1, part_1 = run(
        Step.stats_1, lambda p, r, i, b, g, h: stats([p], [r], [(g, 0), (h, 0)], 1, i, b),
        keep_1, w_1, inv, part_0, g_0, g_1,
    )
    keep_3, sent_3 = run(Step.half_3, cut, keep_3, x_3)
    z_3 = over_z(sent_3, 1)
    keep_4, sent_4 = run(Step.half_4, cut, keep_4, x_4)
    z_4 = over_z(sent_4, 1)
    pred_2, gsum_2, part_2 = run(
        Step.stats_2, lambda p, r, i, b, g, h: stats([p], [r], [(g, 0), (h, 1)], 0, i, b),
        keep_2, w_2, inv, part_1, g_2, g_1,
    )
    first, share = run(Step.first, lambda *v: first_message(*v, slides), info, gsum_0, gsum_2, prior, row)
    keep_3, sent_3 = run(Step.quarter_3, cut, keep_3, z_3)
    w_3 = over_z(sent_3, 2)
    keep_4, sent_4 = run(Step.quarter_4, cut, keep_4, z_4)
    w_4 = over_z(sent_4, 2)

    def sum_up(names, value):
        value = run(names[0], add, value, over_x(value))
        others = [over_z(value, 1), over_z(value, 2), over_z(value, 3)]
        value = run(names[1], add, value, *others)
        others = [over_core(value), over_y(value), shift(value, lambda k: k ^ 3, "genes")]
        return run(names[2], join_parts, value, *others)

    first = sum_up((Step.first_1, Step.first_2, Step.first_3), first)
    pred_3, gsum_3, _, spot_unit, spot_slope, spot_cos = run(
        Step.stats_3,
        lambda p, q, r, t, i, b, g, h: stats([p, q], [r, t], [(g, 0), (h, 1)], 1, i, b, True, spots_scale),
        keep_3, keep_4, w_3, w_4, inv, part_2, g_2, g_1,
    )
    second = run(Step.second, second_message, info, gsum_1, gsum_3, spot_cos)
    second = sum_up((Step.second_1, Step.second_2, Step.second_3), second)
    shared = (spot_unit, spot_slope, inv)
    d2, weight_2, cos2 = run(
        Step.grad_2, lambda p, s, u, v, i, g, h: grad_of(p, [(g, 0), (h, 1)], 0, s, 1, u, v, i, genes_scale),
        pred_2, first, *shared, g_2, g_1,
    )
    b_2 = over_z(d2, 2)
    d0, weight_0, cos0 = run(
        Step.grad_0, lambda p, s, u, v, i, b, g, h: grad_of(p, [(g, 0), (h, 0)], 0, s, 0, u, v, i, genes_scale, b),
        pred_0, first, *shared, weight_2, g_0, g_1,
    )
    home_r = over_y(run(Step.home_0, parted, pred_2, pred_3))
    home = run(Step.home_1, parted, pred_0, pred_1)
    lo_2 = run(Step.lo_2, lambda p, r: stack(p, r, rows), d2, b_2)
    c_2, xlo_2 = over_z(lo_2, 1), over_x(lo_2)
    xlo_2 = early(Step.taken_xlo2, xlo_2)
    b_0 = over_z(run(Step.go_0, copy, d0), 2)
    b_0 = early(Step.taken_b0, b_0)
    d3, weight_3, cos3 = run(
        Step.grad_3, lambda p, s, u, v, i, b, g, h: grad_of(p, [(g, 0), (h, 1)], 1, s, 1, u, v, i, genes_scale, b),
        pred_3, second, *shared, weight_0, g_2, g_1,
    )
    d1, weight_1, cos1 = run(
        Step.grad_1, lambda p, s, u, v, i, b, g, h: grad_of(p, [(g, 0), (h, 0)], 1, s, 0, u, v, i, genes_scale, b),
        pred_1, second, *shared, weight_3, g_0, g_1,
    )
    d3, losses, own_cos = run(
        Step.finish,
        lambda i, g, w, a, b, c, d, *v: finish(i, g, w, (a, b, c, d), *v, slides, scale, spots_all, genes_all),
        info, d3, weight_1, cos0, cos1, cos2, cos3, first, second, share, row,
    )
    b_3 = over_z(d3, 2)
    home, sent = run(Step.home_2, traded, home, home_r)
    home_r = over_core(sent)
    lo_0 = run(Step.lo_0, lambda p, r: stack(p, r, rows), d0, b_0)
    c_0, xlo_0 = over_z(lo_0, 1), over_x(lo_0)
    xlo_0 = early(Step.taken_xlo0, xlo_0)
    hi_2 = run(Step.hi_2, copy, c_2)
    xhi_2 = over_x(hi_2)
    home, sent = run(Step.home_3, lambda i, p, r: by_z(i, p, r), info, home, home_r)
    home_r = over_z(sent, 1)
    lo_3 = run(Step.lo_3, lambda p, r: stack(p, r, rows), d3, b_3)
    c_3, xlo_3 = over_z(lo_3, 1), over_x(lo_3)
    xlo_3 = early(Step.taken_xlo3, xlo_3)
    hi_0 = run(Step.hi_0, copy, c_0)
    xhi_0 = over_x(hi_0)
    xhi_0 = early(Step.taken_xhi0, xhi_0)
    b_1 = over_z(run(Step.go_1, copy, d1), 2)
    b_1 = early(Step.taken_b1, b_1)
    weights = (wah, wal, wbh, wbl)
    back_share = lambda a, b, c, d, *v: share_of((a, b, c, d), [(p, 0) for p in v])
    *parts_2, dh2, dl2 = run(Step.share_2, back_share, *weights, lo_2, hi_2, xlo_2, xhi_2)
    chip_a = both(over_core, parts_2[2:])
    hi_3 = run(Step.hi_3, copy, c_3)
    xhi_3 = over_x(hi_3)
    chip_a = over_y(run(Step.chip_a, add_rows, *parts_2[:2], *chip_a))
    chip_a = early(Step.taken_chip_a, chip_a)
    lo_1 = run(Step.lo_1, lambda p, r: stack(p, r, rows), d1, b_1)
    c_1, xlo_1 = over_z(lo_1, 1), over_x(lo_1)
    xlo_1 = early(Step.taken_xlo1, xlo_1)
    *parts_3, dh3, dl3 = run(Step.share_3, back_share, *weights, lo_3, hi_3, xlo_3, xhi_3)
    chip_b = both(over_core, parts_3[2:])
    hi_1 = run(Step.hi_1, copy, c_1)
    xhi_1 = over_x(hi_1)
    chip_b = over_y(run(Step.chip_b, add_rows, *parts_3[:2], *chip_b))
    home, sent = run(Step.home_4, traded, home, home_r)
    home_r = over_z(sent, 2)
    mg = run(
        Step.back,
        lambda a, b, c, d, e, f, *v: back([(0, a, b), (1, c, d), (1, e, f)], v[0:2], v[2:4]),
        *e2, *e3, *e4, dh2, dl2, dh3, dl3,
    )
    offset = run(Step.offsets, lambda *v: offsets(v, rows), lo_3, hi_3, xlo_3, xhi_3)
    outcome = run(
        Step.near,
        lambda i, wh, wl, e0h, e0l, e1h, e1l, mg, off, a, b, c, d, p: half_of(
            i, 0, (wh, wl), [a, b, c, d], (0, 1), ((0, p),), [e0h, e0l, e1h, e1l, mg, off]
        ),
        info, wah, wal, *e0, *e1, mg, offset, lo_0, hi_0, lo_1, hi_1, chip_a,
    )
    near_grad, near = outcome[0], outcome[1:]
    grad_logits, *shares = run(
        Step.far,
        lambda i, wh, wl, e0h, e0l, e1h, e1l, mg, off, a, b, c, d, grad, *v: half_of(
            i, 2, (wh, wl), [a, b, c, d], (0, 1), (), [e0h, e0l, e1h, e1l, mg, off], grad, v
        ),
        info, wbh, wbl, *e0, *e1, mg, offset, xlo_0, xhi_0, xlo_1, xhi_1, near_grad, *near,
    )
    core_a, core_b = both(over_core, shares[2:4]), both(over_core, shares[6:])
    pred_out = run(Step.settle, lambda i, p, r: settle(i, p, r), info, home, home_r)
    shares[4:6] = run(Step.late, add_below, *shares[4:6], chip_b)
    summands = []
    for kept, core in ((shares[0:2], core_a), (shares[4:6], core_b)):
        for n in range(2):
            summands += [kept[n], core[n]]
    grad_expression = run(Step.gather, gather_expression, *summands)
    run.run(order)
    get = lambda v: run.value(v)
    spot_cos_out = lax.dynamic_index_in_dim(
        get(second)[4:].reshape(groups, spots_all // groups), group_index, 0, keepdims=False
    )
    losses, own_cos = get(losses), get(own_cos)
    return (
        get(pred_out), own_cos[0], spot_cos_out, losses[0, 0], losses[0, 1], get(grad_logits), get(grad_expression)
    )


order = (
    Step.own, Step.weigh_a, Step.weigh_b, Step.blend_0b, Step.blend_1, Step.own_b, Step.blend_0a, Step.rows,
    Step.beyond_a, Step.blend_2, Step.half_0, Step.half_1, Step.blend_3, Step.beyond_b, Step.quarter_0,
    Step.blend_4, Step.half_2, Step.rows_on, Step.taken_w0, Step.quarter_1, Step.quarter_2, Step.half_4,
    Step.half_3, Step.stats_0, Step.stats_1, Step.stats_2, Step.quarter_4, Step.first, Step.quarter_3, Step.first_1,
    Step.first_2, Step.stats_3, Step.home_0, Step.first_3, Step.grad_2, Step.second, Step.second_1, Step.second_2,
    Step.lo_2, Step.grad_0, Step.go_0, Step.second_3, Step.grad_3, Step.home_1, Step.home_2, Step.grad_1, Step.go_1,
    Step.finish, Step.lo_0, Step.hi_2, Step.lo_3, Step.taken_xlo2, Step.share_2, Step.home_3, Step.hi_0,
    Step.taken_xlo3, Step.chip_a, Step.hi_3, Step.taken_xlo0, Step.lo_1, Step.offsets, Step.share_3, Step.hi_1,
    Step.taken_chip_a, Step.back, Step.taken_xlo1, Step.home_4, Step.chip_b, Step.near, Step.far, Step.settle,
    Step.late, Step.gather,
)


def solution(mesh):
    fits = mesh.shape["cells"] == 8 and mesh.shape["genes"] == 4
    return jax.shard_map(
        slice_4x2 if fits else spread,
        mesh=mesh,
        in_specs=(
            P("cells", "genes"),
            P("cells", "genes"),
            P(None, "genes"),
            P(),
            P("cells"),
            P(),
            P(),
        ),
        out_specs=(
            P("cells", "genes"),
            P("genes"),
            P("cells"),
            P(),
            P(),
            P("cells", "genes"),
            P("cells", "genes"),
        ),
        check_vma=False,
    )
```

```python
import functools

import jax
import jax.numpy as jnp
from jax import lax
from jax.experimental import pallas as pl
from jax.experimental.pallas import tpu as pltpu
from jax.sharding import PartitionSpec as P

eps_norm = 1e-06
density_weight = 0.01
high = lax.Precision.HIGH
highest = lax.Precision.HIGHEST


def slide_of(spot_index, slide_ends):
    return jnp.sum((spot_index[:, None] >= slide_ends[None, :]).astype(jnp.int32), axis=1)


def live_of(group_live, group_index, slot_dev):
    groups = group_live.shape[0]
    here = jnp.arange(groups, dtype=jnp.int32) == group_index
    return jnp.arange(slot_dev, dtype=jnp.int32) < jnp.sum(jnp.where(here, group_live, 0))


def spread(logits, expression, spatial, density_prior, cell_slide, group_live, spot_counts):
    slot_dev, spot_dev = logits.shape
    gene_dev = expression.shape[1]
    groups, parts = lax.axis_size("cells"), lax.axis_size("genes")
    spots_all, genes_all = spot_dev * parts, gene_dev * parts
    spot_rows = spots_all // groups
    slides = spot_counts.shape[0]
    group_index, gene_index = lax.axis_index("cells"), lax.axis_index("genes")
    scale = float(slot_dev * groups) * float(spots_all)
    slide_ends = jnp.cumsum(spot_counts)
    spot_slide = slide_of(jnp.arange(spots_all, dtype=jnp.int32), slide_ends)
    own_slide = lax.dynamic_slice_in_dim(spot_slide, gene_index * spot_dev, spot_dev)
    slot_live = live_of(group_live, group_index, slot_dev)
    allowed = slot_live[:, None] & (cell_slide[:, None] == own_slide[None, :])
    weight = jnp.where(allowed, jnp.exp(logits), 0.0)
    spot_total = lax.psum(jnp.sum(weight, axis=0), "cells")
    mapping = weight / spot_total[None, :]
    full_map, full_total = (
        lax.all_gather(mapping, "genes", axis=1, tiled=True),
        lax.all_gather(spot_total, "genes", axis=0, tiled=True),
    )
    pred_rows = lax.psum_scatter(
        lax.dot_general(full_map, expression, (((0,), (0,)), ((), ())), precision=highest),
        "cells",
        scatter_dimension=0,
        tiled=True,
    )
    spatial_rows = lax.dynamic_slice_in_dim(spatial, group_index * spot_rows, spot_rows, 0)
    triple = (pred_rows * spatial_rows, pred_rows * pred_rows, spatial_rows * spatial_rows)
    gene_dot, gene_pp, gene_gg = lax.psum(
        jnp.stack([jnp.sum(part, axis=0) for part in triple]), "cells"
    )
    spot_dot, spot_pp, spot_gg = lax.psum(
        jnp.stack([jnp.sum(part, axis=1) for part in triple]), "genes"
    )
    gene_unit = lax.rsqrt(gene_pp + eps_norm) * lax.rsqrt(gene_gg + eps_norm)
    gene_cos = gene_dot * gene_unit
    spot_unit = lax.rsqrt(spot_pp + eps_norm) * lax.rsqrt(spot_gg + eps_norm)
    spot_cos = spot_dot * spot_unit
    gene_term = gene_unit[None, :] * spatial_rows - (gene_cos / (gene_pp + eps_norm))[None, :] * pred_rows
    spot_term = spot_unit[:, None] * spatial_rows - (spot_cos / (spot_pp + eps_norm))[:, None] * pred_rows
    grad_rows = -(scale / genes_all) * gene_term - scale / spots_all * spot_term
    loss_part = jnp.sum(gene_cos) / (genes_all * groups) + jnp.sum(spot_cos) / (spots_all * parts)
    cos_loss = -lax.psum(loss_part, ("cells", "genes"))
    grad_full = lax.all_gather(grad_rows, "cells", axis=0, tiled=True)
    member = spot_slide[None, :] == jnp.arange(slides, dtype=jnp.int32)[:, None]
    prior_total = jnp.sum(jnp.where(member, density_prior[None, :], 0.0), axis=1)
    prior_norm = density_prior / jnp.sum(jnp.where(member, prior_total[:, None], 0.0), axis=0)
    slide_sum = jnp.sum(jnp.where(member, full_total[None, :], 0.0), axis=1)
    share = full_total / jnp.sum(jnp.where(member, slide_sum[:, None], 0.0), axis=0)
    density_loss = jnp.sum(prior_norm * (jnp.log(prior_norm) - jnp.log(share))) / slides
    mass_grad = scale * density_weight * (share - prior_norm) / slides
    own_mass_grad = lax.dynamic_slice_in_dim(mass_grad, gene_index * spot_dev, spot_dev)
    partial_grad = lax.dot_general(expression, grad_full, (((1,), (1,)), ((), ())), precision=highest)
    map_grad = lax.psum_scatter(partial_grad, "genes", scatter_dimension=1, tiled=True)
    grad_expression = jnp.dot(full_map, grad_full, precision=highest)
    spot_weight = lax.psum(jnp.sum(mapping * map_grad, axis=0), "cells")
    grad_logits = mapping * (map_grad - spot_weight[None, :] + own_mass_grad[None, :])
    return (pred_rows, gene_cos, spot_cos, cos_loss, density_loss, grad_logits, grad_expression)


def shift(value, moves, axis):
    if isinstance(value, Later):
        return Later(value, moved=value, move=lambda v: shift(v, moves, axis))
    count = lax.axis_size(axis)
    pairs = [(k, moves(k)) for k in range(count) if moves(k) is not None]
    return lax.ppermute(value, axis, pairs)


def over_x(value):
    return shift(value, lambda k: k ^ 1, "cells")


def over_y(value):
    return shift(value, lambda k: k ^ 2, "genes")


def over_core(value):
    return shift(value, lambda k: k ^ 1, "genes")


def over_z(value, step):
    return shift(value, lambda k: k ^ (2 * step), "cells")


class Step:
    (
        own, weigh_b, blend_0b, weigh_a, blend_1, blend_0a, beyond_a, own_b, blend_2, half_0, half_1,
        beyond_b, rows, quarter_0, blend_3, blend_4, half_2, quarter_1, rows_on, stats_0, quarter_2,
        stats_1, half_3, half_4, stats_2, first, quarter_3, quarter_4, stats_3, second, grad_2, grad_0,
        home_0, home_1, lo_2, go_0, grad_3, grad_1, finish, home_2, lo_0, hi_2, home_3, lo_3, hi_0, go_1,
        share_2, hi_3, chip_a, lo_1, share_3, hi_1, chip_b, home_4, back, offsets, near, far, settle, late,
        gather, taken_z1, taken_x2, taken_w0, taken_x3, taken_w1, taken_xlo2, taken_b0, taken_xlo0,
        taken_xlo3, taken_xhi0, taken_b1, taken_chip_a, taken_xlo1, first_1, first_2, first_3, second_1,
        second_2, second_3,
    ) = range(80)


class Later:
    def __init__(self, like, step=None, place=None, moved=None, move=None):
        self.shape, self.dtype = like.shape, like.dtype
        self.step, self.place, self.moved, self.move = step, place, moved, move


class Steps:
    def __init__(self):
        self.steps, self.values, self.arrived = {}, {}, {}

    def __call__(self, name, step, *operands):
        shapes = [jax.ShapeDtypeStruct(v.shape, v.dtype) for v in operands]
        out = jax.eval_shape(step, *shapes)
        leaves, tree = jax.tree.flatten(out)
        self.steps[name] = (step, operands)
        return jax.tree.unflatten(tree, [Later(v, name, n) for n, v in enumerate(leaves)])

    def value(self, operand):
        if not isinstance(operand, Later):
            return operand
        if operand.step is not None:
            return self.values[operand.step][operand.place]
        if operand not in self.arrived:
            self.arrived[operand] = operand.move(self.value(operand.moved))
        return self.arrived[operand]

    def run(self, order):
        last = None
        for name in order:
            step, operands = self.steps[name]
            operands = [self.value(v) for v in operands]
            if last is not None:
                operands, _ = lax.optimization_barrier((operands, last))
            self.values[name] = jax.tree.leaves(step(*operands))
            last = self.values[name][0]


f32, bf16 = jnp.float32, jnp.bfloat16


def split(value):
    upper = value.astype(bf16)
    return upper, (value - upper.astype(f32)).astype(bf16)


def mul(p, q):
    return jnp.dot(p, q, preferred_element_type=f32)


def mul_t(p, q):
    return lax.dot_general(p, q, (((1,), (1,)), ((), ())), preferred_element_type=f32)


def whole(shape):
    return pl.BlockSpec(shape, lambda *k: (0,) * len(shape), pipeline_mode=pl.Buffered(1))


def like(*shape, dtype=f32):
    return jax.ShapeDtypeStruct(shape, dtype)


def room(mebi):
    return pltpu.CompilerParams(vmem_limit_bytes=mebi << 20)


light = pl.CostEstimate(flops=1, bytes_accessed=1, transcendentals=0)


def in_hbm(value):
    return pltpu.with_memory_space_constraint(value, pltpu.HBM)


def weigh_kernel(slides, base, info, table, code, wh, wl, th, tl, tot):
    k = base + pl.program_id(0)
    depth, width = table.shape
    half = width // 2
    odd = info[info.shape[0] - 2]
    lane = lax.broadcasted_iota(jnp.int32, (1, width), 1)
    spot = info[4] + info[k] * width + jnp.where(odd == 1, lane ^ half, lane)
    slide = slide_rows(spot, info, slides).astype(f32)
    alive = info[6 + slides + info[5]]

    def step(a, total):
        at = pl.multiple_of(a * 128, 128)
        own = jnp.broadcast_to(code[pl.ds(a, 1), :].astype(f32), (128, 128)).T
        own = jnp.concatenate([own] * (width // 128), axis=1)
        live = at + lax.broadcasted_iota(jnp.int32, (128, width), 0) < alive
        value = table[pl.ds(at, 128), :]
        value = jnp.where(odd == 1, jnp.concatenate([value[:, half:], value[:, :half]], axis=1), value)
        w = jnp.where((own == slide) & live, jnp.exp(value), 0.0)
        wh[pl.ds(at, 128), :], wl[pl.ds(at, 128), :] = split(w)
        th[:, pl.ds(at, 128)], tl[:, pl.ds(at, 128)] = split(w.T)
        return total + jnp.sum(w, axis=0, keepdims=True)

    total = lax.fori_loop(0, depth // 128, step, jnp.zeros((1, width), f32), unroll=True)
    tot[...] = jnp.broadcast_to(total, tot.shape)


def weigh(info, logits, code, slides, base):
    depth, spots = logits.shape
    rows = spots // 4
    wide = pl.BlockSpec((depth, rows), lambda k, info: (0, k))
    tall = pl.BlockSpec((rows, depth), lambda k, info: (k, 0))
    return pl.pallas_call(
        functools.partial(weigh_kernel, slides, base),
        name="weigh",
        grid_spec=pltpu.PrefetchScalarGridSpec(
            num_scalar_prefetch=1,
            grid=(2,),
            in_specs=[
                pl.BlockSpec((depth, rows), lambda k, info: (0, info[base + k])),
                pl.BlockSpec(code.shape, lambda k, info: (0, 0)),
            ],
            out_specs=[wide, wide, tall, tall, pl.BlockSpec((8, rows), lambda k, info: (0, k))],
        ),
        out_shape=[
            like(depth, 2 * rows, dtype=bf16),
            like(depth, 2 * rows, dtype=bf16),
            like(2 * rows, depth, dtype=bf16),
            like(2 * rows, depth, dtype=bf16),
            like(8, 2 * rows),
        ],
        cost_estimate=light,
        compiler_params=room(12),
    )(info, in_hbm(logits), in_hbm(code))


def blend_kernel(groups, pair, sources, halved, has_total, save, *refs):
    k = pl.program_id(0)
    parts = []
    for half in halved:
        parts.append(jnp.where(k < 2, refs[0][...], refs[1][...]) if half else refs[0][...])
        refs = refs[1 + half :]
    width = parts[0].shape[1]
    lefts, refs = refs[: 2 * sources], refs[2 * sources :]
    tots, outs = (refs[:sources], refs[sources:]) if has_total else ((), refs)

    @pl.when(k == 0)
    def _():
        for out, chunks in zip(outs, groups):
            out[...] = jnp.zeros_like(out)
            if has_total:
                for m, (n, begin) in enumerate(chunks):
                    out[len(chunks) * pair :, m * pair : (m + 1) * pair] = tots[n][:, begin : begin + pair]

    for c, part in enumerate(parts):
        place = slice(c * width, (c + 1) * width)
        upper, lower = split(part)
        if save:
            outs[-2][:, place], outs[-1][:, place] = upper, lower
        values = []
        for n in range(sources):
            th, tl = lefts[2 * n : 2 * n + 2]
            values.append(mul(th[...], upper) + mul(th[...], lower) + mul(tl[...], upper))
        for out, chunks in zip(outs, groups):
            for m, (n, begin) in enumerate(chunks):
                out[m * pair : (m + 1) * pair, place] += values[n][begin : begin + pair]


def blend(sources, parts, groups, tots=(), save=True):
    spots, depth = sources[0][0].shape
    halved = [isinstance(part, tuple) for part in parts]
    pair, width = spots // 2, (parts[0][0] if halved[0] else parts[0]).shape[1]
    deep, wide = depth // 4, len(parts) * width
    extra = 8 if tots else 0
    column = pl.BlockSpec((spots, deep), lambda k: (0, k))
    row = pl.BlockSpec((deep, width), lambda k: (k, 0))
    top = pl.BlockSpec((deep, width), lambda k: (jnp.minimum(k, 1), 0))
    bottom = pl.BlockSpec((deep, width), lambda k: (jnp.maximum(k - 2, 0), 0))
    both = pl.BlockSpec((deep, wide), lambda k: (k, 0))
    specs, given = [], []
    for part, half in zip(parts, halved):
        specs += [top, bottom] if half else [row]
        given += part if half else [part]
    number = len(sources)
    heights = [len(chunks) * pair + extra for chunks in groups]
    return pl.pallas_call(
        functools.partial(blend_kernel, groups, pair, number, halved, bool(tots), save),
        name="blend",
        grid=(4,),
        in_specs=specs + [column] * 2 * number + [whole(t.shape) for t in tots],
        out_specs=[pl.BlockSpec((h, wide), lambda k: (0, 0)) for h in heights] + [both, both] * save,
        out_shape=[like(h, wide) for h in heights] + [like(depth, wide, dtype=bf16)] * 2 * save,
        cost_estimate=light,
        compiler_params=room(14),
    )(*given, *[t for source in sources for t in source], *tots)


def stats_kernel(first, last, spots_scale, pieces, *refs):
    refs = list(refs)
    glue = lambda parts: jnp.concatenate([ref[...] for ref in parts], axis=1)
    close, found = glue(refs[:pieces]), glue(refs[pieces : 2 * pieces])
    gp, gq = refs[2 * pieces : 2 * pieces + 2]
    refs = refs[2 * pieces + 2 :]
    rows = gp.shape[0]
    if first:
        inv, row = refs[-2:]
        total = close[rows : rows + 1, :rows] + found[rows : rows + 1, :rows]
        row[...] = jnp.broadcast_to(total, row.shape)
        for b in range(0, rows, 128):
            inv[b : b + 128, :] = 1.0 / jnp.broadcast_to(total[:, b : b + 128], (128, 128)).T
        inverse = inv[...]
    else:
        inverse = refs[0][...]
        before = refs[1]
        refs = refs[2:]
    pred, gsum, part = refs[:3]
    width = close.shape[1]
    value = (close[:rows] + found[:rows]) * jnp.concatenate([inverse] * (width // 128), axis=1)
    pred[...] = value
    g = jnp.concatenate([gp[...], gq[...]], axis=1)
    sums = []
    for n, product in enumerate((value * g, value * value, g * g)):
        gsum[n : n + 1, :] = jnp.sum(product, axis=0, keepdims=True)
        lanes = sum(product[:, c : c + 128] for c in range(0, width, 128))
        if not first:
            lanes = lanes + before[:, n * 128 : n * 128 + 128]
        sums.append(lanes)
        part[:, n * 128 : n * 128 + 128] = lanes
    gsum[3:, :] = jnp.zeros((5, width), f32)
    if last:
        unit_out, slope_out, cos_out = refs[3:]
        dot, pp, gg = [jnp.sum(lanes, axis=1, keepdims=True) for lanes in sums]
        unit = lax.rsqrt(pp + eps_norm) * lax.rsqrt(gg + eps_norm)
        cos = dot * unit
        wide = lambda v: jnp.broadcast_to(v, (rows, 128))
        unit_out[...] = wide(unit * spots_scale)
        slope_out[...] = wide(spots_scale * cos / (pp + eps_norm))
        for b in range(0, rows, 128):
            turned = wide(cos)[b : b + 128].T
            cos_out[:, b : b + 128] = turned[:8]


def part_blocks(parts, cut, rows):
    width = parts[0][0].shape[1]
    return [
        pl.BlockSpec((rows, width // 2), functools.partial(lambda n, k: (n, cut), n), pipeline_mode=pl.Buffered(1))
        for _, n in parts
    ]


def stats(close, found, parts, cut, inv=None, before=None, last=False, spots_scale=0.0):
    width = parts[0][0].shape[1]
    rows = close[0].shape[0] - (8 if inv is None else 0)
    first = inv is None
    outs = [like(rows, width), like(8, width), like(rows, 384)]
    if first:
        outs += [like(rows, 128), like(8, rows)]
    if last:
        outs += [like(rows, 128), like(rows, 128), like(8, rows)]
    extra = () if first else (inv, before)
    landed = [whole(v.shape) for v in close + found]
    return pl.pallas_call(
        functools.partial(stats_kernel, first, last, spots_scale, len(close)),
        name="stats",
        grid=(1,),
        in_specs=landed + part_blocks(parts, cut, rows) + [whole(v.shape) for v in extra],
        out_specs=[whole(o.shape) for o in outs],
        out_shape=outs,
        cost_estimate=light,
        compiler_params=room(8),
    )(*close, *found, *[p for p, _ in parts], *extra)


def grad_kernel(genes_scale, chain, pred, gp, gq, red, unit_in, slope_in, inv, *refs):
    width = pred.shape[1]
    out, weight, cos_out = refs[-3:]
    dot, pp, gg = red[0:1, :], red[1:2, :], red[2:3, :]
    unit = lax.rsqrt(pp + eps_norm) * lax.rsqrt(gg + eps_norm)
    cos = dot * unit
    cos_out[...] = jnp.broadcast_to(cos, cos_out.shape)
    slope = genes_scale * cos / (pp + eps_norm)
    wide = lambda v: jnp.concatenate([v[...]] * (width // 128), axis=1)
    g = jnp.concatenate([gp[...], gq[...]], axis=1)
    p = pred[...]
    grad = (slope + wide(slope_in)) * p - (genes_scale * unit + wide(unit_in)) * g
    out[...] = grad * wide(inv)
    product = grad * p
    lanes = sum(product[:, c : c + 128] for c in range(0, width, 128))
    weight[...] = lanes + refs[0][...] if chain else lanes


def grad_of(pred, parts, cut, red, q, unit, slope, inv, genes_scale, before=None):
    rows, width = pred.shape
    extra = () if before is None else (before,)
    outs = [like(rows, width), like(rows, 128), like(8, width)]
    return pl.pallas_call(
        functools.partial(grad_kernel, genes_scale, before is not None),
        name="grad",
        grid=(1,),
        in_specs=[whole(pred.shape)] + part_blocks(parts, cut, rows) + [pl.BlockSpec((8, width), lambda k: (0, q))]
        + [whole(v.shape) for v in (unit, slope, inv) + extra],
        out_specs=[whole(o.shape) for o in outs],
        out_shape=outs,
        cost_estimate=light,
        compiler_params=room(8),
    )(pred, *[p for p, _ in parts], red, unit, slope, inv, *extra)


def share_kernel(wah, wal, wbh, wbl, a, b, c, d, p0, p1, q0, q1, dh, dl):
    k = pl.program_id(0)
    deep, half = p0.shape
    wh = jnp.where(k < 2, wah[...], wbh[...])
    wl = jnp.where(k < 2, wal[...], wbl[...])

    @pl.when(k == 0)
    def _():
        for out in (p0, p1, q0, q1):
            out[...] = jnp.zeros_like(out)

    value = jnp.where(k < 2, jnp.where(k == 0, a[...], b[...]), jnp.where(k == 2, c[...], d[...]))
    upper, lower = split(value)
    dh[...], dl[...] = upper, lower
    for place, top, bottom in ((slice(0, half), p0, p1), (slice(half, 2 * half), q0, q1)):
        up, low = upper[:, place], lower[:, place]
        value = mul(wh, up) + mul(wh, low) + mul(wl, up)
        top[...] += value[:deep]
        bottom[...] += value[deep:]


def share_of(weights, pieces):
    depth, spots = weights[0].shape[0], 2 * weights[0].shape[1]
    rows, width = spots // 4, pieces[0][0].shape[1]
    near = pl.BlockSpec((depth, rows), lambda k: (0, jnp.minimum(k, 1)))
    far = pl.BlockSpec((depth, rows), lambda k: (0, jnp.maximum(k - 2, 0)))
    row = pl.BlockSpec((rows, width), lambda k: (k, 0))
    return pl.pallas_call(
        share_kernel,
        name="share",
        grid=(4,),
        in_specs=[near, near, far, far]
        + [
            pl.BlockSpec((rows, width), functools.partial(lambda n, k: (n, 0), n), pipeline_mode=pl.Buffered(1))
            for _, n in pieces
        ],
        out_specs=[pl.BlockSpec((depth // 2, width // 2), lambda k: (0, 0))] * 4 + [row, row],
        out_shape=[like(depth // 2, width // 2)] * 4 + [like(spots, width, dtype=bf16)] * 2,
        cost_estimate=light,
        compiler_params=room(14),
    )(*weights, *[piece for piece, _ in pieces])


def back_kernel(widths, *refs):
    out, rights = refs[-1], refs[-5:-1]
    begin, total = [0, 0], None
    for n, (unit, width) in enumerate(widths):
        eh, el = refs[2 * n : 2 * n + 2]
        place = slice(begin[unit], begin[unit] + width)
        begin[unit] += width
        dh, dl = [ref[:, place] for ref in rights[2 * unit : 2 * unit + 2]]
        value = mul_t(eh[...], dh) + mul_t(eh[...], dl) + mul_t(el[...], dh)
        total = value if total is None else total + value
    out[...] = total


def back(lefts, d2, d3):
    depth = lefts[0][1].shape[0]
    spots, width = d2[0].shape
    rows = spots // 4
    row = pl.BlockSpec((rows, width), lambda k: (k, 0))
    return pl.pallas_call(
        functools.partial(back_kernel, [(unit, upper.shape[1]) for unit, upper, _ in lefts]),
        name="back",
        grid=(4,),
        in_specs=[whole(part.shape) for _, *both in lefts for part in both] + [row] * 4,
        out_specs=pl.BlockSpec((depth, rows), lambda k: (0, k)),
        out_shape=like(depth, spots),
        cost_estimate=light,
        compiler_params=room(14),
    )(*[part for _, *both in lefts for part in both], *d2, *d3)


def half_kernel(sides, grads, chain, added, info, wh, wl, *refs):
    k = pl.program_id(0)
    refs = list(refs)
    if grads:
        eh0, el0, eh1, el1, mg, offset = refs[:6]
        refs = refs[6:]
    pieces, refs = (refs[0:2], refs[2:4]), refs[4:]
    number = 4 * len(sides)
    more, past = refs[: len(added)], refs[len(added) + (chain and grads) :][:number]
    shares = refs[-number:]
    grad = refs[-number - 1]
    deep, half = shares[0].shape

    @pl.when(k == 0)
    def _():
        for n, share in enumerate(shares):
            share[...] = past[n][...] if chain else jnp.zeros_like(share)
        for n, ref in zip(added, more):
            shares[n][...] += ref[:deep]
            shares[n + 1][...] += ref[deep:]

    total = mg[...] if grads else None
    for n in range(2):
        upper, lower = split(jnp.where(k == 0, pieces[n][0][...], pieces[n][1][...]))
        if grads:
            eh, el = ((eh0, el0), (eh1, el1))[n]
            total += mul_t(eh[...], upper) + mul_t(eh[...], lower) + mul_t(el[...], upper)
        for m, side in enumerate(sides):
            place = slice(side * half, (side + 1) * half)
            up, low = upper[:, place], lower[:, place]
            value = mul(wh[...], up) + mul(wh[...], low) + mul(wl[...], up)
            at = 2 * (len(sides) * n + m)
            shares[at][...] += value[:deep]
            shares[at + 1][...] += value[deep:]
    if grads:
        value = (wh[...].astype(f32) + wl[...].astype(f32)) * (total + offset[0:1, :])
        width = value.shape[1] // 2
        turned = jnp.concatenate([value[:, width:], value[:, :width]], axis=1)
        grad[...] = jnp.where(info[info.shape[0] - 2] == 1, turned, value)


def half_of(info, base, weights, pieces, sides, added=(), grads=(), grad=None, past=()):
    depth, width = weights[0].shape[0], pieces[0].shape[1]
    rows = weights[0].shape[1] // 2
    spots = 4 * rows
    local = pl.BlockSpec((depth, rows), lambda k, info: (0, k))
    column = pl.BlockSpec((depth, rows), lambda k, info: (0, base + k))
    line = pl.BlockSpec((8, rows), lambda k, info: (0, base + k))
    part = whole((depth // 2, width // 2))
    specs, given = [local, local], list(weights)
    if grads:
        specs += [whole((depth, width))] * 4 + [column, line]
        given += grads
    specs += [pl.BlockSpec((rows, width), lambda k, info: (0, 0), pipeline_mode=pl.Buffered(1))] * 4
    given += pieces
    specs += [whole((depth, width // 2))] * len(added)
    given += [array for _, array in added]
    aliases = {}
    if grad is not None:
        aliases = {1 + len(given): 0}
        specs.append(pl.BlockSpec(memory_space=pl.ANY))
        given.append(grad)
    specs += [part] * len(past)
    given += past
    number = 4 * len(sides)
    outs = [like(depth, spots)] if grads else []
    out_specs = [pl.BlockSpec((depth, rows), lambda k, info: (0, info[base + k]))] if grads else []
    return pl.pallas_call(
        functools.partial(half_kernel, sides, bool(grads), bool(past), [n for n, _ in added]),
        name="half",
        grid_spec=pltpu.PrefetchScalarGridSpec(
            num_scalar_prefetch=1,
            grid=(2,),
            in_specs=specs,
            out_specs=out_specs + [pl.BlockSpec((depth // 2, width // 2), lambda k, info: (0, 0))] * number,
        ),
        out_shape=outs + [like(depth // 2, width // 2)] * number,
        input_output_aliases=aliases,
        cost_estimate=light,
        compiler_params=room(26 if grads else 14),
    )(info, *given)


def small(kernel, name, outs, *operands, info=None, blocks=None, scratch=()):
    specs = []
    for n, operand in enumerate(operands):
        shape, index = (operand.shape, None) if blocks is None or n not in blocks else blocks[n]
        if index is None:
            index = lambda k, *info, rank=len(shape): (0,) * rank
        specs.append(pl.BlockSpec(shape, index, pipeline_mode=pl.Buffered(1)))
    out_specs = [whole(o.shape) for o in outs]
    scalars = () if info is None else (info,)
    return pl.pallas_call(
        kernel,
        name=name,
        grid_spec=pltpu.PrefetchScalarGridSpec(
            num_scalar_prefetch=len(scalars), grid=(1,), in_specs=specs, out_specs=out_specs, scratch_shapes=list(scratch)
        ),
        out_shape=outs,
        cost_estimate=light,
        compiler_params=room(8),
    )(*scalars, *operands)


def add(*parts):
    def kernel(*refs):
        total = refs[0][...]
        for ref in refs[1:-1]:
            total = total + ref[...]
        refs[-1][...] = total

    return small(kernel, "add", [like(*parts[0].shape)], *parts)[0]


def add_rows(p, q, r, t):
    rows = p.shape[0]

    def kernel(p, q, r, t, out):
        out[:rows], out[rows:] = p[...] + r[...], q[...] + t[...]

    return small(kernel, "add_rows", [like(2 * rows, p.shape[1])], p, q, r, t)[0]


def add_below(p, q, both):
    rows = p.shape[0]

    def kernel(p, q, both, first, second):
        first[...], second[...] = p[...] + both[:rows], q[...] + both[rows:]

    return small(kernel, "add_below", [like(*p.shape)] * 2, p, q, both)


def halves(table, axis, *others):
    rows, columns = table.shape
    half = (rows // 2, columns) if axis == 0 else (rows, columns // 2)

    def kernel(*refs):
        total = refs[0][...]
        for ref in refs[1:-2]:
            total = total + ref[...]
        if axis == 0:
            refs[-2][...], refs[-1][...] = total[: rows // 2], total[rows // 2 :]
        else:
            refs[-2][...], refs[-1][...] = total[:, : columns // 2], total[:, columns // 2 :]

    return small(kernel, "halves", [like(*half)] * 2, table, *others)


def copy(value):
    def kernel(value, out):
        out[...] = value[...]

    return small(kernel, "copy", [like(*value.shape)], value)[0]


def take(value):
    anywhere = pl.BlockSpec(memory_space=pl.ANY)
    return pl.pallas_call(
        lambda value, out: None,
        name="take",
        in_specs=[anywhere],
        out_specs=anywhere,
        out_shape=like(*value.shape),
        input_output_aliases={0: 0},
        cost_estimate=light,
        compiler_params=room(1),
    )(value)


def part_total(rows, *parts):
    width = parts[0].shape[1]

    def kernel(*refs):
        total = refs[0][...]
        for ref in refs[1:-2]:
            total = total + ref[...]
        for n, out in enumerate(refs[-2:]):
            out[:rows] = total[n * rows : (n + 1) * rows]
            line = total[2 * rows :, n * rows : (n + 1) * rows]
            out[rows:] = jnp.concatenate([line, jnp.zeros((8, width - rows), f32)], axis=1)

    return small(kernel, "part_total", [like(rows + 8, width)] * 2, *parts)


def stack(p, r, rows):
    extra = p.shape[0] - rows

    def kernel(p, r, out):
        out[:rows], out[rows : 2 * rows] = p[:rows], r[:rows]
        if extra:
            out[2 * rows : 2 * rows + extra], out[2 * rows + extra :] = p[rows:], r[rows:]

    return small(kernel, "stack", [like(2 * p.shape[0], p.shape[1])], p, r)[0]


def rows_of(info, table, rows, per_part):
    shape = (rows, table.shape[1])

    def kernel(info, a, b, c, d, first, second, rest):
        first[...], second[...] = a[...], b[...]
        rest[:rows], rest[rows:] = c[...], d[...]

    def index(part):
        return lambda k, info: ((info[info.shape[0] - 3] ^ part) * per_part + info[info.shape[0] - 4], 0)

    return small(
        kernel, "rows", [like(*shape), like(*shape), like(2 * rows, shape[1])], *[table] * 4, info=info,
        blocks={r: (shape, index(r)) for r in range(4)},
    )


def rows_on(kept, landed):
    rows = kept.shape[0]

    def kernel(kept, landed, own, sent):
        own[...] = landed[:rows]
        sent[:rows], sent[rows:] = kept[...], landed[rows:]

    return small(kernel, "rows_on", [like(*kept.shape), like(2 * rows, kept.shape[1])], kept, landed)


def chosen(part, refs):
    low = jnp.where(part == 0, refs[0][...], refs[1][...])
    return jnp.where(part < 2, low, jnp.where(part == 2, refs[2][...], refs[3][...]))


def parted(low, upper):
    rows, width = low.shape
    half = width // 2

    def kernel(low, upper, out):
        for n in range(2):
            cut = slice(n * half, (n + 1) * half)
            out[n * rows : (n + 1) * rows, :half] = low[:, cut]
            out[n * rows : (n + 1) * rows, half:] = upper[:, cut]

    return small(kernel, "parted", [like(2 * rows, width)], low, upper)[0]


def traded(p, r):
    rows = p.shape[0] // 2

    def kernel(p, r, kept, sent):
        kept[:rows], kept[rows:] = p[:rows], r[:rows]
        sent[:rows], sent[rows:] = p[rows:], r[rows:]

    return small(kernel, "traded", [like(*p.shape)] * 2, p, r)


def by_z(info, p, r):
    rows = p.shape[0] // 2

    def kernel(info, p, r, kept, sent):
        turn = info[info.shape[0] - 3] ^ info[info.shape[0] - 1]
        pieces = (p[:rows], r[:rows], p[rows:], r[rows:])
        for out, first in ((kept, 0), (sent, 1)):
            for n in range(2):
                out[n * rows : (n + 1) * rows] = chosen(turn ^ (first + 2 * n), pieces)

    return small(kernel, "by_z", [like(*p.shape)] * 2, p, r, info=info)


def settle(info, p, r):
    rows = p.shape[0] // 2

    def kernel(info, p, r, out):
        pieces = (p[:rows], p[rows:], r[:rows], r[rows:])
        for n, z in enumerate((0, 2, 1, 3)):
            out[n * rows : (n + 1) * rows] = chosen(info[info.shape[0] - 1] ^ z, pieces)

    return small(kernel, "settle", [like(4 * rows, p.shape[1])], p, r, info=info)[0]


def slide_rows(index, info, slides):
    end, slide = 0, jnp.zeros(index.shape, jnp.int32)
    for q in range(slides):
        end = end + info[6 + q]
        slide = slide + (index >= end).astype(jnp.int32)
    return slide


def total_of(value):
    return jnp.sum(jnp.sum(value, axis=1, keepdims=True), axis=0, keepdims=True)


def first_message(info, low, high, prior, row, slides):
    rows, width = row.shape[1], low.shape[1]

    def kernel(info, low, high, prior, row, out, share):
        line = lax.broadcasted_iota(jnp.int32, prior.shape, 0)
        lane = lax.broadcasted_iota(jnp.int32, prior.shape, 1)
        slide = slide_rows(line * 128 + lane, info, slides)
        begin = info[4] + info[info.shape[0] - 4] * rows
        spot = begin + lax.broadcasted_iota(jnp.int32, (1, rows), 1)
        own = slide_rows(spot, info, slides)
        here = prior[pl.ds(begin // 128, rows // 128), :]
        here = jnp.concatenate([here[n : n + 1] for n in range(rows // 128)], axis=1)
        totals = jnp.zeros((1, rows), f32)
        for q in range(slides):
            totals = jnp.where(own == q, total_of(jnp.where(slide == q, prior[...], 0.0)), totals)
        here = here / totals
        share[...] = jnp.broadcast_to(here, share.shape)
        total = row[0:1, :]
        values = [total_of(jnp.where(own == q, total, 0.0)) for q in range(slides)]
        values += [total_of(jnp.where(own == q, here, 0.0)) for q in range(slides)]
        values += [total_of(here * (jnp.log(here) - jnp.log(total)))]
        place = lax.broadcasted_iota(jnp.int32, (1, 2 * width), 1)
        extra = jnp.zeros((1, 2 * width), f32)
        for n, value in enumerate(values):
            extra = jnp.where(place == n, value, extra)
        out[...] = jnp.zeros_like(out)
        out[0:3, :width], out[0:3, width:] = low[0:3, :], high[0:3, :]
        out[3:4, :] = extra

    outs = [like(8, 2 * width), like(8, rows)]
    return small(kernel, "first", outs, low, high, prior, row, info=info)


def second_message(info, low, high, cos):
    rows, width = cos.shape[1], low.shape[1]

    def kernel(info, low, high, cos, out):
        place = lax.broadcasted_iota(jnp.int32, (4, 2 * width), 1)
        line = lax.broadcasted_iota(jnp.int32, (4, 2 * width), 0)
        mine = (line == info[info.shape[0] - 3]) & (place // rows == info[info.shape[0] - 4])
        wide = jnp.concatenate([cos[0:4, :]] * (2 * width // rows), axis=1)
        out[0:3, :width], out[0:3, width:] = low[0:3, :], high[0:3, :]
        out[3:4, :] = jnp.where(place[0:1] == 0, total_of(cos[0:1, :]), 0.0)
        out[4:8, :] = jnp.where(mine, wide, 0.0)

    return small(kernel, "second", [like(8, 2 * width)], low, high, cos, info=info)[0]


def join_parts(mine, *others):
    width = mine.shape[1] // 4

    def kernel(mine, *refs):
        total = mine[...]
        line = lax.broadcasted_iota(jnp.int32, total.shape, 0)
        for part, ref in enumerate(refs[:-1], 1):
            value = ref[...]
            turned = jnp.concatenate(
                [value[:, (n ^ part) * width : ((n ^ part) + 1) * width] for n in range(4)], axis=1
            )
            total = total + jnp.where(line < 3, turned, value)
        refs[-1][...] = total

    return small(kernel, "join", [like(*mine.shape)], mine, *others)[0]


def finish(info, grad, weight, cosines, first, second, share, row, slides, scale, spots_all, genes_all):
    rows, width = grad.shape

    def kernel(info, grad, weight, c0, c1, c2, c3, first, second, share, row, out, losses, genes, spots):
        spot = info[4] + info[info.shape[0] - 4] * rows + lax.broadcasted_iota(jnp.int32, (1, rows), 1)
        own = slide_rows(spot, info, slides)
        found = lambda n: first[3:4, n : n + 1]
        mass = jnp.zeros((1, rows), f32)
        density = found(2 * slides)
        for q in range(slides):
            mass = jnp.where(own == q, found(q), mass)
            density = density + found(slides + q) * jnp.log(found(q))
        total = row[0:1, :]
        mass_grad = scale * density_weight * (total / mass - share[0:1, :]) / slides
        summed = jnp.broadcast_to(jnp.sum(weight[...], axis=1, keepdims=True), (rows, 128))
        turned = jnp.concatenate([summed[n : n + 128].T[0:1] for n in range(0, rows, 128)], axis=1)
        offset = (mass_grad - turned) / total
        loss = -(total_of(c0[0:1] + c1[0:1] + c2[0:1] + c3[0:1]) / genes_all + second[3:4, 0:1] / spots_all)
        place = lax.broadcasted_iota(jnp.int32, losses.shape, 1)
        losses[...] = jnp.where(place == 0, loss, density / slides)
        out[:rows] = grad[...]
        wide = jnp.concatenate([offset, jnp.zeros((1, width - rows), f32)], axis=1)
        out[rows:] = jnp.broadcast_to(wide, (8, width))
        both = jnp.concatenate([c0[0:1, : width // 2], c1[0:1, : width // 2]], axis=1)
        genes[...] = jnp.broadcast_to(both, genes.shape)
        group = jnp.zeros((1, width), f32)
        for n in range(8):
            line = second[4 + n // 2 : 5 + n // 2, n % 2 * width : n % 2 * width + width]
            group = jnp.where(info[5] == n, line, group)
        spots[...] = jnp.broadcast_to(group, spots.shape)

    outs = [like(rows + 8, width), like(8, 128), like(8, width), like(8, width)]
    return small(kernel, "finish", outs, grad, weight, *cosines, first, second, share, row, info=info)


def offsets(tails, rows):
    def kernel(a, b, c, d, out):
        for n, ref in enumerate((a, b, c, d)):
            for m in range(2):
                place = slice((2 * n + m) * rows, (2 * n + m + 1) * rows)
                out[:, place] = ref[8 * m : 8 * m + 8, :rows]

    spec = ((16, tails[0].shape[1]), lambda k: (rows // 8, 0))
    return small(kernel, "offsets", [like(8, 8 * rows)], *tails, blocks={n: spec for n in range(4)})[0]


def gather_expression(*parts):
    depth, half = parts[0].shape
    each = len(parts) // 4

    def kernel(*refs):
        out = refs[-1]
        for n in range(2):

            @pl.when(pl.program_id(0) == n)
            def _():
                for m in range(2):
                    total = sum(ref[...] for ref in refs[(2 * m + n) * each : (2 * m + n + 1) * each])
                    out[:, m * half : (m + 1) * half] = total

    return pl.pallas_call(
        kernel,
        name="gather",
        grid=(2,),
        in_specs=[whole((depth, half))] * len(parts),
        out_specs=pl.BlockSpec((depth, 2 * half), lambda k: (k, 0)),
        out_shape=like(2 * depth, 2 * half),
        cost_estimate=light,
        compiler_params=room(40),
    )(*parts)


def slice_4x2(logits, expression, spatial, density_prior, cell_slide, group_live, spot_counts):
    slot_dev, spot_dev = logits.shape
    gene_dev = expression.shape[1]
    groups, parts = 8, 4
    spots_all, genes_all = spot_dev * parts, gene_dev * parts
    slides = spot_counts.shape[0]
    rows = spot_dev // 8
    group_index, gene_index = lax.axis_index("cells"), lax.axis_index("genes")
    z, x = group_index // 2, group_index % 2
    scale = float(slot_dev * groups) * float(spots_all)
    spots_scale, genes_scale = scale / spots_all, scale / genes_all
    run = Steps()
    early = lambda name, value: run(name, take, value) if name in order else value

    place = 4 * x + 2 * (z % 2) + z // 2
    info = jnp.concatenate(
        [
            jnp.stack([(2 * m ^ place) // 2 for m in range(4)] + [gene_index * spot_dev, group_index]),
            spot_counts,
            group_live,
            jnp.stack([place, gene_index, place % 2, z]),
        ]
    ).astype(jnp.int32)
    prior = density_prior.reshape(-1, 128)

    pair = 2 * rows
    code = cell_slide.reshape(-1, 128)
    both = lambda move, values: [move(v) for v in values]
    cut = lambda *v: halves(v[0], 0, *v[1:])
    one, two = [[(0, 0), (0, pair)]], [[(0, 0), (0, pair)], [(1, 0), (1, pair)]]
    own_a, own_b = run(Step.own, lambda e: halves(in_hbm(e), 1), expression)
    across_a = over_y(own_a)
    beside_a, beside_b = over_core(own_a), over_core(own_b)
    wbh, wbl, tbh, tbl, tot_b = run(Step.weigh_b, lambda *v: weigh(*v, slides, 2), info, logits, code)
    sent_0, *e0 = run(
        Step.blend_0b, lambda h, l, p, q, t: blend([(h, l)], [p, q], one, (t,)), tbh, tbl, own_a, beside_a, tot_b
    )
    x_0 = over_x(sent_0)
    wah, wal, tah, tal, tot_a = run(Step.weigh_a, lambda *v: weigh(*v, slides, 0), info, logits, code)
    full = lambda groups, gather: lambda ah, al, bh, bl, *v: blend([(ah, al), (bh, bl)], gather(*v), groups)
    turned = (tah, tal, tbh, tbl)
    keep_1, sent_1, *e1 = run(
        Step.blend_1, full([[(0, 0), (1, 0)], [(0, pair), (1, pair)]], lambda p, q: [p, q]), *turned, own_b, beside_b
    )
    z_1 = over_z(sent_1, 1)
    z_1 = early(Step.taken_z1, z_1)
    (keep_0,) = run(
        Step.blend_0a, lambda h, l, p, q, t: blend([(h, l)], [p, q], one, (t,), False), tah, tal, own_a, beside_a, tot_a
    )
    beyond_a = both(over_core, run(Step.beyond_a, cut, across_a))
    across_b = over_y(run(Step.own_b, copy, own_b))
    keep_2, sent_2, *e2 = run(Step.blend_2, full(two, lambda p, *q: [p, q]), *turned, across_a, *beyond_a)
    x_2 = over_x(sent_2)
    x_2 = early(Step.taken_x2, x_2)
    keep_0, sent_0 = run(Step.half_0, lambda *v: part_total(pair, *v), keep_0, x_0)
    z_0 = over_z(sent_0, 1)
    keep_1, sent_1 = run(Step.half_1, cut, keep_1, z_1)
    x_1 = over_x(sent_1)
    beyond_b = both(over_core, run(Step.beyond_b, cut, across_b))
    g_0, g_1, g_far = run(Step.rows, lambda i, t: rows_of(i, t, rows, spot_dev // rows), info, spatial)
    g_far = over_y(g_far)
    keep_0, sent_0 = run(Step.quarter_0, lambda *v: part_total(rows, *v), keep_0, z_0)
    w_0 = over_z(sent_0, 2)
    w_0 = early(Step.taken_w0, w_0)
    keep_3, sent_3, *e3 = run(Step.blend_3, full(two, lambda p: [p]), *turned, across_b)
    x_3 = over_x(sent_3)
    keep_4, sent_4, *e4 = run(Step.blend_4, full(two, lambda *q: [q]), *turned, *beyond_b)
    x_4 = over_x(sent_4)
    x_3 = early(Step.taken_x3, x_3)
    keep_2, sent_2 = run(Step.half_2, cut, keep_2, x_2)
    z_2 = over_z(sent_2, 1)
    keep_1, sent_1 = run(Step.quarter_1, cut, keep_1, x_1)
    w_1 = over_z(sent_1, 2)
    w_1 = early(Step.taken_w1, w_1)
    g_2, g_1 = run(Step.rows_on, rows_on, g_1, g_far)
    g_1 = over_core(g_1)
    pred_0, gsum_0, part_0, inv, row = run(
        Step.stats_0, lambda p, r, g, h: stats([p], [r], [(g, 0), (h, 0)], 0), keep_0, w_0, g_0, g_1
    )
    keep_2, sent_2 = run(Step.quarter_2, cut, keep_2, z_2)
    w_2 = over_z(sent_2, 2)
    pred_1, gsum_1, part_1 = run(
        Step.stats_1, lambda p, r, i, b, g, h: stats([p], [r], [(g, 0), (h, 0)], 1, i, b),
        keep_1, w_1, inv, part_0, g_0, g_1,
    )
    keep_3, sent_3 = run(Step.half_3, cut, keep_3, x_3)
    z_3 = over_z(sent_3, 1)
    keep_4, sent_4 = run(Step.half_4, cut, keep_4, x_4)
    z_4 = over_z(sent_4, 1)
    pred_2, gsum_2, part_2 = run(
        Step.stats_2, lambda p, r, i, b, g, h: stats([p], [r], [(g, 0), (h, 1)], 0, i, b),
        keep_2, w_2, inv, part_1, g_2, g_1,
    )
    first, share = run(Step.first, lambda *v: first_message(*v, slides), info, gsum_0, gsum_2, prior, row)
    keep_3, sent_3 = run(Step.quarter_3, cut, keep_3, z_3)
    w_3 = over_z(sent_3, 2)
    keep_4, sent_4 = run(Step.quarter_4, cut, keep_4, z_4)
    w_4 = over_z(sent_4, 2)

    def sum_up(names, value):
        value = run(names[0], add, value, over_x(value))
        others = [over_z(value, 1), over_z(value, 2), over_z(value, 3)]
        value = run(names[1], add, value, *others)
        others = [over_core(value), over_y(value), shift(value, lambda k: k ^ 3, "genes")]
        return run(names[2], join_parts, value, *others)

    first = sum_up((Step.first_1, Step.first_2, Step.first_3), first)
    pred_3, gsum_3, _, spot_unit, spot_slope, spot_cos = run(
        Step.stats_3,
        lambda p, q, r, t, i, b, g, h: stats([p, q], [r, t], [(g, 0), (h, 1)], 1, i, b, True, spots_scale),
        keep_3, keep_4, w_3, w_4, inv, part_2, g_2, g_1,
    )
    second = run(Step.second, second_message, info, gsum_1, gsum_3, spot_cos)
    second = sum_up((Step.second_1, Step.second_2, Step.second_3), second)
    shared = (spot_unit, spot_slope, inv)
    d2, weight_2, cos2 = run(
        Step.grad_2, lambda p, s, u, v, i, g, h: grad_of(p, [(g, 0), (h, 1)], 0, s, 1, u, v, i, genes_scale),
        pred_2, first, *shared, g_2, g_1,
    )
    b_2 = over_z(d2, 2)
    d0, weight_0, cos0 = run(
        Step.grad_0, lambda p, s, u, v, i, b, g, h: grad_of(p, [(g, 0), (h, 0)], 0, s, 0, u, v, i, genes_scale, b),
        pred_0, first, *shared, weight_2, g_0, g_1,
    )
    home_r = over_y(run(Step.home_0, parted, pred_2, pred_3))
    home = run(Step.home_1, parted, pred_0, pred_1)
    lo_2 = run(Step.lo_2, lambda p, r: stack(p, r, rows), d2, b_2)
    c_2, xlo_2 = over_z(lo_2, 1), over_x(lo_2)
    xlo_2 = early(Step.taken_xlo2, xlo_2)
    b_0 = over_z(run(Step.go_0, copy, d0), 2)
    b_0 = early(Step.taken_b0, b_0)
    d3, weight_3, cos3 = run(
        Step.grad_3, lambda p, s, u, v, i, b, g, h: grad_of(p, [(g, 0), (h, 1)], 1, s, 1, u, v, i, genes_scale, b),
        pred_3, second, *shared, weight_0, g_2, g_1,
    )
    d1, weight_1, cos1 = run(
        Step.grad_1, lambda p, s, u, v, i, b, g, h: grad_of(p, [(g, 0), (h, 0)], 1, s, 0, u, v, i, genes_scale, b),
        pred_1, second, *shared, weight_3, g_0, g_1,
    )
    d3, losses, own_cos, group_cos = run(
        Step.finish,
        lambda i, g, w, a, b, c, d, *v: finish(i, g, w, (a, b, c, d), *v, slides, scale, spots_all, genes_all),
        info, d3, weight_1, cos0, cos1, cos2, cos3, first, second, share, row,
    )
    b_3 = over_z(d3, 2)
    home, sent = run(Step.home_2, traded, home, home_r)
    home_r = over_core(sent)
    lo_0 = run(Step.lo_0, lambda p, r: stack(p, r, rows), d0, b_0)
    c_0, xlo_0 = over_z(lo_0, 1), over_x(lo_0)
    xlo_0 = early(Step.taken_xlo0, xlo_0)
    hi_2 = run(Step.hi_2, copy, c_2)
    xhi_2 = over_x(hi_2)
    home, sent = run(Step.home_3, lambda i, p, r: by_z(i, p, r), info, home, home_r)
    home_r = over_z(sent, 1)
    lo_3 = run(Step.lo_3, lambda p, r: stack(p, r, rows), d3, b_3)
    c_3, xlo_3 = over_z(lo_3, 1), over_x(lo_3)
    xlo_3 = early(Step.taken_xlo3, xlo_3)
    hi_0 = run(Step.hi_0, copy, c_0)
    xhi_0 = over_x(hi_0)
    xhi_0 = early(Step.taken_xhi0, xhi_0)
    b_1 = over_z(run(Step.go_1, copy, d1), 2)
    b_1 = early(Step.taken_b1, b_1)
    weights = (wah, wal, wbh, wbl)
    back_share = lambda a, b, c, d, *v: share_of((a, b, c, d), [(p, 0) for p in v])
    *parts_2, dh2, dl2 = run(Step.share_2, back_share, *weights, lo_2, hi_2, xlo_2, xhi_2)
    chip_a = both(over_core, parts_2[2:])
    hi_3 = run(Step.hi_3, copy, c_3)
    xhi_3 = over_x(hi_3)
    chip_a = over_y(run(Step.chip_a, add_rows, *parts_2[:2], *chip_a))
    chip_a = early(Step.taken_chip_a, chip_a)
    lo_1 = run(Step.lo_1, lambda p, r: stack(p, r, rows), d1, b_1)
    c_1, xlo_1 = over_z(lo_1, 1), over_x(lo_1)
    xlo_1 = early(Step.taken_xlo1, xlo_1)
    *parts_3, dh3, dl3 = run(Step.share_3, back_share, *weights, lo_3, hi_3, xlo_3, xhi_3)
    chip_b = both(over_core, parts_3[2:])
    hi_1 = run(Step.hi_1, copy, c_1)
    xhi_1 = over_x(hi_1)
    chip_b = over_y(run(Step.chip_b, add_rows, *parts_3[:2], *chip_b))
    home, sent = run(Step.home_4, traded, home, home_r)
    home_r = over_z(sent, 2)
    mg = run(
        Step.back,
        lambda a, b, c, d, e, f, *v: back([(0, a, b), (1, c, d), (1, e, f)], v[0:2], v[2:4]),
        *e2, *e3, *e4, dh2, dl2, dh3, dl3,
    )
    offset = run(Step.offsets, lambda *v: offsets(v, rows), lo_3, hi_3, xlo_3, xhi_3)
    outcome = run(
        Step.near,
        lambda i, wh, wl, e0h, e0l, e1h, e1l, mg, off, a, b, c, d, p: half_of(
            i, 0, (wh, wl), [a, b, c, d], (0, 1), ((0, p),), [e0h, e0l, e1h, e1l, mg, off]
        ),
        info, wah, wal, *e0, *e1, mg, offset, lo_0, hi_0, lo_1, hi_1, chip_a,
    )
    near_grad, near = outcome[0], outcome[1:]
    grad_logits, *shares = run(
        Step.far,
        lambda i, wh, wl, e0h, e0l, e1h, e1l, mg, off, a, b, c, d, grad, *v: half_of(
            i, 2, (wh, wl), [a, b, c, d], (0, 1), (), [e0h, e0l, e1h, e1l, mg, off], grad, v
        ),
        info, wbh, wbl, *e0, *e1, mg, offset, xlo_0, xhi_0, xlo_1, xhi_1, near_grad, *near,
    )
    core_a, core_b = both(over_core, shares[2:4]), both(over_core, shares[6:])
    pred_out = run(Step.settle, lambda i, p, r: settle(i, p, r), info, home, home_r)
    shares[4:6] = run(Step.late, add_below, *shares[4:6], chip_b)
    summands = []
    for kept, core in ((shares[0:2], core_a), (shares[4:6], core_b)):
        for n in range(2):
            summands += [kept[n], core[n]]
    grad_expression = run(Step.gather, gather_expression, *summands)
    run.run(order)
    get = lambda v: run.value(v)
    losses = get(losses)
    return (
        get(pred_out), get(own_cos)[0], get(group_cos)[0], losses[0, 0], losses[0, 1], get(grad_logits), get(grad_expression)
    )


order = (
    Step.own, Step.weigh_a, Step.weigh_b, Step.blend_0b, Step.blend_1, Step.own_b, Step.blend_0a, Step.rows,
    Step.beyond_a, Step.blend_2, Step.half_0, Step.half_1, Step.blend_3, Step.beyond_b, Step.quarter_0,
    Step.blend_4, Step.half_2, Step.rows_on, Step.taken_w0, Step.quarter_1, Step.quarter_2, Step.half_4,
    Step.half_3, Step.stats_0, Step.stats_1, Step.stats_2, Step.quarter_4, Step.first, Step.quarter_3, Step.first_1,
    Step.first_2, Step.stats_3, Step.home_0, Step.first_3, Step.grad_2, Step.second, Step.second_1, Step.second_2,
    Step.lo_2, Step.grad_0, Step.go_0, Step.second_3, Step.grad_3, Step.home_1, Step.home_2, Step.grad_1, Step.go_1,
    Step.finish, Step.lo_0, Step.hi_2, Step.lo_3, Step.taken_xlo2, Step.share_2, Step.home_3, Step.hi_0,
    Step.taken_xlo3, Step.chip_a, Step.hi_3, Step.taken_xlo0, Step.lo_1, Step.offsets, Step.share_3, Step.hi_1,
    Step.taken_chip_a, Step.back, Step.taken_xlo1, Step.home_4, Step.chip_b, Step.near, Step.far, Step.settle,
    Step.late, Step.gather,
)


def solution(mesh):
    fits = mesh.shape["cells"] == 8 and mesh.shape["genes"] == 4
    return jax.shard_map(
        slice_4x2 if fits else spread,
        mesh=mesh,
        in_specs=(
            P("cells", "genes"),
            P("cells", "genes"),
            P(None, "genes"),
            P(),
            P("cells"),
            P(),
            P(),
        ),
        out_specs=(
            P("cells", "genes"),
            P("genes"),
            P("cells"),
            P(),
            P(),
            P("cells", "genes"),
            P("cells", "genes"),
        ),
        check_vma=False,
    )
```

```python
import functools

import jax
import jax.numpy as jnp
from jax import lax
from jax.experimental import pallas as pl
from jax.experimental.pallas import tpu as pltpu
from jax.sharding import PartitionSpec as P

eps_norm = 1e-06
density_weight = 0.01
high = lax.Precision.HIGH
highest = lax.Precision.HIGHEST


def slide_of(spot_index, slide_ends):
    return jnp.sum((spot_index[:, None] >= slide_ends[None, :]).astype(jnp.int32), axis=1)


def live_of(group_live, group_index, slot_dev):
    groups = group_live.shape[0]
    here = jnp.arange(groups, dtype=jnp.int32) == group_index
    return jnp.arange(slot_dev, dtype=jnp.int32) < jnp.sum(jnp.where(here, group_live, 0))


def spread(logits, expression, spatial, density_prior, cell_slide, group_live, spot_counts):
    slot_dev, spot_dev = logits.shape
    gene_dev = expression.shape[1]
    groups, parts = lax.axis_size("cells"), lax.axis_size("genes")
    spots_all, genes_all = spot_dev * parts, gene_dev * parts
    spot_rows = spots_all // groups
    slides = spot_counts.shape[0]
    group_index, gene_index = lax.axis_index("cells"), lax.axis_index("genes")
    scale = float(slot_dev * groups) * float(spots_all)
    slide_ends = jnp.cumsum(spot_counts)
    spot_slide = slide_of(jnp.arange(spots_all, dtype=jnp.int32), slide_ends)
    own_slide = lax.dynamic_slice_in_dim(spot_slide, gene_index * spot_dev, spot_dev)
    slot_live = live_of(group_live, group_index, slot_dev)
    allowed = slot_live[:, None] & (cell_slide[:, None] == own_slide[None, :])
    weight = jnp.where(allowed, jnp.exp(logits), 0.0)
    spot_total = lax.psum(jnp.sum(weight, axis=0), "cells")
    mapping = weight / spot_total[None, :]
    full_map, full_total = (
        lax.all_gather(mapping, "genes", axis=1, tiled=True),
        lax.all_gather(spot_total, "genes", axis=0, tiled=True),
    )
    pred_rows = lax.psum_scatter(
        lax.dot_general(full_map, expression, (((0,), (0,)), ((), ())), precision=highest),
        "cells",
        scatter_dimension=0,
        tiled=True,
    )
    spatial_rows = lax.dynamic_slice_in_dim(spatial, group_index * spot_rows, spot_rows, 0)
    triple = (pred_rows * spatial_rows, pred_rows * pred_rows, spatial_rows * spatial_rows)
    gene_dot, gene_pp, gene_gg = lax.psum(
        jnp.stack([jnp.sum(part, axis=0) for part in triple]), "cells"
    )
    spot_dot, spot_pp, spot_gg = lax.psum(
        jnp.stack([jnp.sum(part, axis=1) for part in triple]), "genes"
    )
    gene_unit = lax.rsqrt(gene_pp + eps_norm) * lax.rsqrt(gene_gg + eps_norm)
    gene_cos = gene_dot * gene_unit
    spot_unit = lax.rsqrt(spot_pp + eps_norm) * lax.rsqrt(spot_gg + eps_norm)
    spot_cos = spot_dot * spot_unit
    gene_term = gene_unit[None, :] * spatial_rows - (gene_cos / (gene_pp + eps_norm))[None, :] * pred_rows
    spot_term = spot_unit[:, None] * spatial_rows - (spot_cos / (spot_pp + eps_norm))[:, None] * pred_rows
    grad_rows = -(scale / genes_all) * gene_term - scale / spots_all * spot_term
    loss_part = jnp.sum(gene_cos) / (genes_all * groups) + jnp.sum(spot_cos) / (spots_all * parts)
    cos_loss = -lax.psum(loss_part, ("cells", "genes"))
    grad_full = lax.all_gather(grad_rows, "cells", axis=0, tiled=True)
    member = spot_slide[None, :] == jnp.arange(slides, dtype=jnp.int32)[:, None]
    prior_total = jnp.sum(jnp.where(member, density_prior[None, :], 0.0), axis=1)
    prior_norm = density_prior / jnp.sum(jnp.where(member, prior_total[:, None], 0.0), axis=0)
    slide_sum = jnp.sum(jnp.where(member, full_total[None, :], 0.0), axis=1)
    share = full_total / jnp.sum(jnp.where(member, slide_sum[:, None], 0.0), axis=0)
    density_loss = jnp.sum(prior_norm * (jnp.log(prior_norm) - jnp.log(share))) / slides
    mass_grad = scale * density_weight * (share - prior_norm) / slides
    own_mass_grad = lax.dynamic_slice_in_dim(mass_grad, gene_index * spot_dev, spot_dev)
    partial_grad = lax.dot_general(expression, grad_full, (((1,), (1,)), ((), ())), precision=highest)
    map_grad = lax.psum_scatter(partial_grad, "genes", scatter_dimension=1, tiled=True)
    grad_expression = jnp.dot(full_map, grad_full, precision=highest)
    spot_weight = lax.psum(jnp.sum(mapping * map_grad, axis=0), "cells")
    grad_logits = mapping * (map_grad - spot_weight[None, :] + own_mass_grad[None, :])
    return (pred_rows, gene_cos, spot_cos, cos_loss, density_loss, grad_logits, grad_expression)


def shift(value, moves, axis):
    if isinstance(value, Later):
        return Later(value, moved=value, move=lambda v: shift(v, moves, axis))
    count = lax.axis_size(axis)
    pairs = [(k, moves(k)) for k in range(count) if moves(k) is not None]
    return lax.ppermute(value, axis, pairs)


def over_x(value):
    return shift(value, lambda k: k ^ 1, "cells")


def over_y(value):
    return shift(value, lambda k: k ^ 2, "genes")


def over_core(value):
    return shift(value, lambda k: k ^ 1, "genes")


def over_z(value, step):
    return shift(value, lambda k: k ^ (2 * step), "cells")


class Step:
    (
        own, weigh_b, blend_0b, weigh_a, blend_1, blend_0a, beyond_a, own_b, blend_2, half_0, half_1,
        beyond_b, rows, quarter_0, blend_3, blend_4, half_2, quarter_1, rows_on, stats_0, quarter_2,
        stats_1, half_3, half_4, stats_2, first, quarter_3, quarter_4, stats_3, second, grad_2, grad_0,
        home_0, home_1, lo_2, go_0, grad_3, grad_1, finish, home_2, lo_0, hi_2, home_3, lo_3, hi_0, go_1,
        share_2, hi_3, chip_a, lo_1, share_3, hi_1, chip_b, home_4, back_2, back_3, offsets, near, far_lo,
        far_hi, settle, late, gather, taken_z1, taken_x2, taken_w0, taken_x3, taken_w1, taken_xlo2,
        taken_b0, taken_xlo0, taken_xlo3, taken_xhi0, taken_b1, taken_chip_a, taken_xlo1, first_1, first_2,
        first_3, second_1, second_2, second_3,
    ) = range(82)


class Later:
    def __init__(self, like, step=None, place=None, moved=None, move=None):
        self.shape, self.dtype = like.shape, like.dtype
        self.step, self.place, self.moved, self.move = step, place, moved, move


class Steps:
    def __init__(self):
        self.steps, self.values, self.arrived = {}, {}, {}

    def __call__(self, name, step, *operands):
        shapes = [jax.ShapeDtypeStruct(v.shape, v.dtype) for v in operands]
        out = jax.eval_shape(step, *shapes)
        leaves, tree = jax.tree.flatten(out)
        self.steps[name] = (step, operands)
        return jax.tree.unflatten(tree, [Later(v, name, n) for n, v in enumerate(leaves)])

    def value(self, operand):
        if not isinstance(operand, Later):
            return operand
        if operand.step is not None:
            return self.values[operand.step][operand.place]
        if operand not in self.arrived:
            self.arrived[operand] = operand.move(self.value(operand.moved))
        return self.arrived[operand]

    def run(self, order):
        last = None
        for name in order:
            step, operands = self.steps[name]
            operands = [self.value(v) for v in operands]
            if last is not None:
                operands, _ = lax.optimization_barrier((operands, last))
            self.values[name] = jax.tree.leaves(step(*operands))
            last = self.values[name][0]


f32, bf16 = jnp.float32, jnp.bfloat16


def split(value):
    upper = value.astype(bf16)
    return upper, (value - upper.astype(f32)).astype(bf16)


def mul(p, q):
    return jnp.dot(p, q, preferred_element_type=f32)


def mul_t(p, q):
    return lax.dot_general(p, q, (((1,), (1,)), ((), ())), preferred_element_type=f32)


def whole(shape):
    return pl.BlockSpec(shape, lambda *k: (0,) * len(shape), pipeline_mode=pl.Buffered(1))


def like(*shape, dtype=f32):
    return jax.ShapeDtypeStruct(shape, dtype)


def room(mebi):
    return pltpu.CompilerParams(vmem_limit_bytes=mebi << 20)


light = pl.CostEstimate(flops=1, bytes_accessed=1, transcendentals=0)


def in_hbm(value):
    return pltpu.with_memory_space_constraint(value, pltpu.HBM)


def weigh_kernel(slides, base, info, table, code, wh, wl, th, tl, tot):
    k = base + pl.program_id(0)
    depth, width = table.shape
    half = width // 2
    odd = info[info.shape[0] - 2]
    lane = lax.broadcasted_iota(jnp.int32, (1, width), 1)
    spot = info[4] + info[k] * width + jnp.where(odd == 1, lane ^ half, lane)
    slide = slide_rows(spot, info, slides).astype(f32)
    alive = info[6 + slides + info[5]]

    def step(a, total):
        at = pl.multiple_of(a * 128, 128)
        own = jnp.broadcast_to(code[pl.ds(a, 1), :].astype(f32), (128, 128)).T
        own = jnp.concatenate([own] * (width // 128), axis=1)
        live = at + lax.broadcasted_iota(jnp.int32, (128, width), 0) < alive
        value = table[pl.ds(at, 128), :]
        value = jnp.where(odd == 1, jnp.concatenate([value[:, half:], value[:, :half]], axis=1), value)
        w = jnp.where((own == slide) & live, jnp.exp(value), 0.0)
        wh[pl.ds(at, 128), :], wl[pl.ds(at, 128), :] = split(w)
        th[:, pl.ds(at, 128)], tl[:, pl.ds(at, 128)] = split(w.T)
        return total + jnp.sum(w, axis=0, keepdims=True)

    total = lax.fori_loop(0, depth // 128, step, jnp.zeros((1, width), f32), unroll=True)
    tot[...] = jnp.broadcast_to(total, tot.shape)


def weigh(info, logits, code, slides, base):
    depth, spots = logits.shape
    rows = spots // 4
    wide = pl.BlockSpec((depth, rows), lambda k, info: (0, k))
    tall = pl.BlockSpec((rows, depth), lambda k, info: (k, 0))
    return pl.pallas_call(
        functools.partial(weigh_kernel, slides, base),
        name="weigh",
        grid_spec=pltpu.PrefetchScalarGridSpec(
            num_scalar_prefetch=1,
            grid=(2,),
            in_specs=[
                pl.BlockSpec((depth, rows), lambda k, info: (0, info[base + k])),
                pl.BlockSpec(code.shape, lambda k, info: (0, 0)),
            ],
            out_specs=[wide, wide, tall, tall, pl.BlockSpec((8, rows), lambda k, info: (0, k))],
        ),
        out_shape=[
            like(depth, 2 * rows, dtype=bf16),
            like(depth, 2 * rows, dtype=bf16),
            like(2 * rows, depth, dtype=bf16),
            like(2 * rows, depth, dtype=bf16),
            like(8, 2 * rows),
        ],
        cost_estimate=light,
        compiler_params=room(12),
    )(info, in_hbm(logits), in_hbm(code))


def blend_kernel(groups, pair, sources, halved, has_total, save, *refs):
    k = pl.program_id(0)
    parts = []
    for half in halved:
        parts.append(jnp.where(k < 2, refs[0][...], refs[1][...]) if half else refs[0][...])
        refs = refs[1 + half :]
    width = parts[0].shape[1]
    lefts, refs = refs[: 2 * sources], refs[2 * sources :]
    tots, outs = (refs[:sources], refs[sources:]) if has_total else ((), refs)

    @pl.when(k == 0)
    def _():
        for out, chunks in zip(outs, groups):
            out[...] = jnp.zeros_like(out)
            if has_total:
                for m, (n, begin) in enumerate(chunks):
                    out[len(chunks) * pair :, m * pair : (m + 1) * pair] = tots[n][:, begin : begin + pair]

    for c, part in enumerate(parts):
        place = slice(c * width, (c + 1) * width)
        upper, lower = split(part)
        if save:
            outs[-2][:, place], outs[-1][:, place] = upper, lower
        values = []
        for n in range(sources):
            th, tl = lefts[2 * n : 2 * n + 2]
            values.append(mul(th[...], upper) + mul(th[...], lower) + mul(tl[...], upper))
        for out, chunks in zip(outs, groups):
            for m, (n, begin) in enumerate(chunks):
                out[m * pair : (m + 1) * pair, place] += values[n][begin : begin + pair]


def blend(sources, parts, groups, tots=(), save=True):
    spots, depth = sources[0][0].shape
    halved = [isinstance(part, tuple) for part in parts]
    pair, width = spots // 2, (parts[0][0] if halved[0] else parts[0]).shape[1]
    deep, wide = depth // 4, len(parts) * width
    extra = 8 if tots else 0
    column = pl.BlockSpec((spots, deep), lambda k: (0, k))
    row = pl.BlockSpec((deep, width), lambda k: (k, 0))
    top = pl.BlockSpec((deep, width), lambda k: (jnp.minimum(k, 1), 0))
    bottom = pl.BlockSpec((deep, width), lambda k: (jnp.maximum(k - 2, 0), 0))
    both = pl.BlockSpec((deep, wide), lambda k: (k, 0))
    specs, given = [], []
    for part, half in zip(parts, halved):
        specs += [top, bottom] if half else [row]
        given += part if half else [part]
    number = len(sources)
    heights = [len(chunks) * pair + extra for chunks in groups]
    return pl.pallas_call(
        functools.partial(blend_kernel, groups, pair, number, halved, bool(tots), save),
        name="blend",
        grid=(4,),
        in_specs=specs + [column] * 2 * number + [whole(t.shape) for t in tots],
        out_specs=[pl.BlockSpec((h, wide), lambda k: (0, 0)) for h in heights] + [both, both] * save,
        out_shape=[like(h, wide) for h in heights] + [like(depth, wide, dtype=bf16)] * 2 * save,
        cost_estimate=light,
        compiler_params=room(14),
    )(*given, *[t for source in sources for t in source], *tots)


def stats_kernel(first, last, spots_scale, pieces, *refs):
    refs = list(refs)
    glue = lambda parts: jnp.concatenate([ref[...] for ref in parts], axis=1)
    close, found = glue(refs[:pieces]), glue(refs[pieces : 2 * pieces])
    gp, gq = refs[2 * pieces : 2 * pieces + 2]
    refs = refs[2 * pieces + 2 :]
    rows = gp.shape[0]
    if first:
        inv, row = refs[-2:]
        total = close[rows : rows + 1, :rows] + found[rows : rows + 1, :rows]
        row[...] = jnp.broadcast_to(total, row.shape)
        for b in range(0, rows, 128):
            inv[b : b + 128, :] = 1.0 / jnp.broadcast_to(total[:, b : b + 128], (128, 128)).T
        inverse = inv[...]
    else:
        inverse = refs[0][...]
        before = refs[1]
        refs = refs[2:]
    pred, gsum, part = refs[:3]
    width = close.shape[1]
    value = (close[:rows] + found[:rows]) * jnp.concatenate([inverse] * (width // 128), axis=1)
    pred[...] = value
    g = jnp.concatenate([gp[...], gq[...]], axis=1)
    sums = []
    for n, product in enumerate((value * g, value * value, g * g)):
        gsum[n : n + 1, :] = jnp.sum(product, axis=0, keepdims=True)
        lanes = sum(product[:, c : c + 128] for c in range(0, width, 128))
        if not first:
            lanes = lanes + before[:, n * 128 : n * 128 + 128]
        sums.append(lanes)
        part[:, n * 128 : n * 128 + 128] = lanes
    gsum[3:, :] = jnp.zeros((5, width), f32)
    if last:
        unit_out, slope_out, cos_out = refs[3:]
        dot, pp, gg = [jnp.sum(lanes, axis=1, keepdims=True) for lanes in sums]
        unit = lax.rsqrt(pp + eps_norm) * lax.rsqrt(gg + eps_norm)
        cos = dot * unit
        wide = lambda v: jnp.broadcast_to(v, (rows, 128))
        unit_out[...] = wide(unit * spots_scale)
        slope_out[...] = wide(spots_scale * cos / (pp + eps_norm))
        for b in range(0, rows, 128):
            turned = wide(cos)[b : b + 128].T
            cos_out[:, b : b + 128] = turned[:8]


def part_blocks(parts, cut, rows):
    width = parts[0][0].shape[1]
    return [
        pl.BlockSpec((rows, width // 2), functools.partial(lambda n, k: (n, cut), n), pipeline_mode=pl.Buffered(1))
        for _, n in parts
    ]


def stats(close, found, parts, cut, inv=None, before=None, last=False, spots_scale=0.0):
    width = parts[0][0].shape[1]
    rows = close[0].shape[0] - (8 if inv is None else 0)
    first = inv is None
    outs = [like(rows, width), like(8, width), like(rows, 384)]
    if first:
        outs += [like(rows, 128), like(8, rows)]
    if last:
        outs += [like(rows, 128), like(rows, 128), like(8, rows)]
    extra = () if first else (inv, before)
    landed = [whole(v.shape) for v in close + found]
    return pl.pallas_call(
        functools.partial(stats_kernel, first, last, spots_scale, len(close)),
        name="stats",
        grid=(1,),
        in_specs=landed + part_blocks(parts, cut, rows) + [whole(v.shape) for v in extra],
        out_specs=[whole(o.shape) for o in outs],
        out_shape=outs,
        cost_estimate=light,
        compiler_params=room(8),
    )(*close, *found, *[p for p, _ in parts], *extra)


def grad_kernel(genes_scale, chain, pred, gp, gq, red, unit_in, slope_in, inv, *refs):
    width = pred.shape[1]
    out, weight, cos_out = refs[-3:]
    dot, pp, gg = red[0:1, :], red[1:2, :], red[2:3, :]
    unit = lax.rsqrt(pp + eps_norm) * lax.rsqrt(gg + eps_norm)
    cos = dot * unit
    cos_out[...] = jnp.broadcast_to(cos, cos_out.shape)
    slope = genes_scale * cos / (pp + eps_norm)
    wide = lambda v: jnp.concatenate([v[...]] * (width // 128), axis=1)
    g = jnp.concatenate([gp[...], gq[...]], axis=1)
    p = pred[...]
    grad = (slope + wide(slope_in)) * p - (genes_scale * unit + wide(unit_in)) * g
    out[...] = grad * wide(inv)
    product = grad * p
    lanes = sum(product[:, c : c + 128] for c in range(0, width, 128))
    weight[...] = lanes + refs[0][...] if chain else lanes


def grad_of(pred, parts, cut, red, q, unit, slope, inv, genes_scale, before=None):
    rows, width = pred.shape
    extra = () if before is None else (before,)
    outs = [like(rows, width), like(rows, 128), like(8, width)]
    return pl.pallas_call(
        functools.partial(grad_kernel, genes_scale, before is not None),
        name="grad",
        grid=(1,),
        in_specs=[whole(pred.shape)] + part_blocks(parts, cut, rows) + [pl.BlockSpec((8, width), lambda k: (0, q))]
        + [whole(v.shape) for v in (unit, slope, inv) + extra],
        out_specs=[whole(o.shape) for o in outs],
        out_shape=outs,
        cost_estimate=light,
        compiler_params=room(8),
    )(pred, *[p for p, _ in parts], red, unit, slope, inv, *extra)


def share_kernel(wah, wal, wbh, wbl, a, b, c, d, p0, p1, q0, q1, dh, dl):
    k = pl.program_id(0)
    deep, half = p0.shape
    wh = jnp.where(k < 2, wah[...], wbh[...])
    wl = jnp.where(k < 2, wal[...], wbl[...])

    @pl.when(k == 0)
    def _():
        for out in (p0, p1, q0, q1):
            out[...] = jnp.zeros_like(out)

    value = jnp.where(k < 2, jnp.where(k == 0, a[...], b[...]), jnp.where(k == 2, c[...], d[...]))
    upper, lower = split(value)
    dh[...], dl[...] = upper, lower
    for place, top, bottom in ((slice(0, half), p0, p1), (slice(half, 2 * half), q0, q1)):
        up, low = upper[:, place], lower[:, place]
        value = mul(wh, up) + mul(wh, low) + mul(wl, up)
        top[...] += value[:deep]
        bottom[...] += value[deep:]


def share_of(weights, pieces):
    depth, spots = weights[0].shape[0], 2 * weights[0].shape[1]
    rows, width = spots // 4, pieces[0][0].shape[1]
    near = pl.BlockSpec((depth, rows), lambda k: (0, jnp.minimum(k, 1)))
    far = pl.BlockSpec((depth, rows), lambda k: (0, jnp.maximum(k - 2, 0)))
    row = pl.BlockSpec((rows, width), lambda k: (k, 0))
    return pl.pallas_call(
        share_kernel,
        name="share",
        grid=(4,),
        in_specs=[near, near, far, far]
        + [
            pl.BlockSpec((rows, width), functools.partial(lambda n, k: (n, 0), n), pipeline_mode=pl.Buffered(1))
            for _, n in pieces
        ],
        out_specs=[pl.BlockSpec((depth // 2, width // 2), lambda k: (0, 0))] * 4 + [row, row],
        out_shape=[like(depth // 2, width // 2)] * 4 + [like(spots, width, dtype=bf16)] * 2,
        cost_estimate=light,
        compiler_params=room(14),
    )(*weights, *[piece for piece, _ in pieces])


def back_kernel(widths, chain, *refs):
    out, dh, dl = refs[-1], refs[2 * len(widths)], refs[2 * len(widths) + 1]
    begin, total = 0, refs[-2][...] if chain else None
    for n, width in enumerate(widths):
        eh, el = refs[2 * n : 2 * n + 2]
        upper, lower = dh[:, begin : begin + width], dl[:, begin : begin + width]
        begin += width
        value = mul_t(eh[...], upper) + mul_t(eh[...], lower) + mul_t(el[...], upper)
        total = value if total is None else total + value
    out[...] = total


def back(lefts, d, past=None):
    depth = lefts[0][0].shape[0]
    spots, width = d[0].shape
    rows = spots // 4
    row = pl.BlockSpec((rows, width), lambda k: (k, 0))
    column = pl.BlockSpec((depth, rows), lambda k: (0, k))
    parts = [part for both in lefts for part in both]
    return pl.pallas_call(
        functools.partial(back_kernel, [upper.shape[1] for upper, _ in lefts], past is not None),
        name="back",
        grid=(4,),
        in_specs=[whole(part.shape) for part in parts] + [row] * 2 + ([] if past is None else [column]),
        out_specs=column,
        out_shape=like(depth, spots),
        cost_estimate=light,
        compiler_params=room(12),
    )(*parts, *d, *(() if past is None else (past,)))


def half_kernel(sides, grads, chain, added, blocks, info, wh, wl, *refs):
    k = pl.program_id(0)
    refs = list(refs)
    if grads:
        eh0, el0, eh1, el1, mg, offset = refs[:6]
        refs = refs[6:]
    pieces, refs = (refs[:blocks], refs[blocks : 2 * blocks]), refs[2 * blocks :]
    number = 4 * len(sides)
    more, past = refs[: len(added)], refs[len(added) + (chain and grads) :][:number]
    shares = refs[-number:]
    grad = refs[-number - 1]
    deep, half = shares[0].shape

    @pl.when(k == 0)
    def _():
        for n, share in enumerate(shares):
            share[...] = past[n][...] if chain else jnp.zeros_like(share)
        for n, ref in zip(added, more):
            shares[n][...] += ref[:deep]
            shares[n + 1][...] += ref[deep:]

    total = mg[...] if grads else None
    for n in range(2):
        piece = pieces[n][0][...] if blocks == 1 else jnp.where(k == 0, pieces[n][0][...], pieces[n][1][...])
        upper, lower = split(piece)
        if grads:
            eh, el = ((eh0, el0), (eh1, el1))[n]
            total += mul_t(eh[...], upper) + mul_t(eh[...], lower) + mul_t(el[...], upper)
        for m, side in enumerate(sides):
            place = slice(side * half, (side + 1) * half)
            up, low = upper[:, place], lower[:, place]
            value = mul(wh[...], up) + mul(wh[...], low) + mul(wl[...], up)
            at = 2 * (len(sides) * n + m)
            shares[at][...] += value[:deep]
            shares[at + 1][...] += value[deep:]
    if grads:
        value = (wh[...].astype(f32) + wl[...].astype(f32)) * (total + offset[0:1, :])
        width = value.shape[1] // 2
        turned = jnp.concatenate([value[:, width:], value[:, :width]], axis=1)
        grad[...] = jnp.where(info[info.shape[0] - 2] == 1, turned, value)


def half_of(info, base, weights, pieces, sides, added=(), grads=(), grad=None, past=()):
    depth, width = weights[0].shape[0], pieces[0].shape[1]
    rows = weights[0].shape[1] // 2
    spots = 4 * rows
    blocks = len(pieces) // 2
    local = pl.BlockSpec((depth, rows), lambda k, info: (0, base % 2 + k))
    column = pl.BlockSpec((depth, rows), lambda k, info: (0, base + k))
    line = pl.BlockSpec((8, rows), lambda k, info: (0, base + k))
    part = whole((depth // 2, width // 2))
    specs, given = [local, local], list(weights)
    if grads:
        specs += [whole((depth, width))] * 4 + [column, line]
        given += grads
    specs += [pl.BlockSpec((rows, width), lambda k, info: (0, 0), pipeline_mode=pl.Buffered(1))] * len(pieces)
    given += pieces
    specs += [whole((depth, width // 2))] * len(added)
    given += [array for _, array in added]
    aliases = {}
    if grad is not None:
        aliases = {1 + len(given): 0}
        specs.append(pl.BlockSpec(memory_space=pl.ANY))
        given.append(grad)
    specs += [part] * len(past)
    given += past
    number = 4 * len(sides)
    outs = [like(depth, spots)] if grads else []
    out_specs = [pl.BlockSpec((depth, rows), lambda k, info: (0, info[base + k]))] if grads else []
    return pl.pallas_call(
        functools.partial(half_kernel, sides, bool(grads), bool(past), [n for n, _ in added], blocks),
        name="half",
        grid_spec=pltpu.PrefetchScalarGridSpec(
            num_scalar_prefetch=1,
            grid=(blocks,),
            in_specs=specs,
            out_specs=out_specs + [pl.BlockSpec((depth // 2, width // 2), lambda k, info: (0, 0))] * number,
        ),
        out_shape=outs + [like(depth // 2, width // 2)] * number,
        input_output_aliases=aliases,
        cost_estimate=light,
        compiler_params=room(26 if grads else 14),
    )(info, *given)


def small(kernel, name, outs, *operands, info=None, blocks=None, scratch=()):
    specs = []
    for n, operand in enumerate(operands):
        shape, index = (operand.shape, None) if blocks is None or n not in blocks else blocks[n]
        if index is None:
            index = lambda k, *info, rank=len(shape): (0,) * rank
        specs.append(pl.BlockSpec(shape, index, pipeline_mode=pl.Buffered(1)))
    out_specs = [whole(o.shape) for o in outs]
    scalars = () if info is None else (info,)
    return pl.pallas_call(
        kernel,
        name=name,
        grid_spec=pltpu.PrefetchScalarGridSpec(
            num_scalar_prefetch=len(scalars), grid=(1,), in_specs=specs, out_specs=out_specs, scratch_shapes=list(scratch)
        ),
        out_shape=outs,
        cost_estimate=light,
        compiler_params=room(8),
    )(*scalars, *operands)


def add(*parts):
    def kernel(*refs):
        total = refs[0][...]
        for ref in refs[1:-1]:
            total = total + ref[...]
        refs[-1][...] = total

    return small(kernel, "add", [like(*parts[0].shape)], *parts)[0]


def add_rows(p, q, r, t):
    rows = p.shape[0]

    def kernel(p, q, r, t, out):
        out[:rows], out[rows:] = p[...] + r[...], q[...] + t[...]

    return small(kernel, "add_rows", [like(2 * rows, p.shape[1])], p, q, r, t)[0]


def add_below(p, q, both):
    rows = p.shape[0]

    def kernel(p, q, both, first, second):
        first[...], second[...] = p[...] + both[:rows], q[...] + both[rows:]

    return small(kernel, "add_below", [like(*p.shape)] * 2, p, q, both)


def halves(table, axis, *others):
    rows, columns = table.shape
    half = (rows // 2, columns) if axis == 0 else (rows, columns // 2)

    def kernel(*refs):
        total = refs[0][...]
        for ref in refs[1:-2]:
            total = total + ref[...]
        if axis == 0:
            refs[-2][...], refs[-1][...] = total[: rows // 2], total[rows // 2 :]
        else:
            refs[-2][...], refs[-1][...] = total[:, : columns // 2], total[:, columns // 2 :]

    return small(kernel, "halves", [like(*half)] * 2, table, *others)


def copy(value):
    def kernel(value, out):
        out[...] = value[...]

    return small(kernel, "copy", [like(*value.shape)], value)[0]


def take(value):
    anywhere = pl.BlockSpec(memory_space=pl.ANY)
    return pl.pallas_call(
        lambda value, out: None,
        name="take",
        in_specs=[anywhere],
        out_specs=anywhere,
        out_shape=like(*value.shape),
        input_output_aliases={0: 0},
        cost_estimate=light,
        compiler_params=room(1),
    )(value)


def part_total(rows, *parts):
    width = parts[0].shape[1]

    def kernel(*refs):
        total = refs[0][...]
        for ref in refs[1:-2]:
            total = total + ref[...]
        for n, out in enumerate(refs[-2:]):
            out[:rows] = total[n * rows : (n + 1) * rows]
            line = total[2 * rows :, n * rows : (n + 1) * rows]
            out[rows:] = jnp.concatenate([line, jnp.zeros((8, width - rows), f32)], axis=1)

    return small(kernel, "part_total", [like(rows + 8, width)] * 2, *parts)


def stack(p, r, rows):
    extra = p.shape[0] - rows

    def kernel(p, r, out):
        out[:rows], out[rows : 2 * rows] = p[:rows], r[:rows]
        if extra:
            out[2 * rows : 2 * rows + extra], out[2 * rows + extra :] = p[rows:], r[rows:]

    return small(kernel, "stack", [like(2 * p.shape[0], p.shape[1])], p, r)[0]


def rows_of(info, table, rows, per_part):
    shape = (rows, table.shape[1])

    def kernel(info, a, b, c, d, first, second, rest):
        first[...], second[...] = a[...], b[...]
        rest[:rows], rest[rows:] = c[...], d[...]

    def index(part):
        return lambda k, info: ((info[info.shape[0] - 3] ^ part) * per_part + info[info.shape[0] - 4], 0)

    return small(
        kernel, "rows", [like(*shape), like(*shape), like(2 * rows, shape[1])], *[table] * 4, info=info,
        blocks={r: (shape, index(r)) for r in range(4)},
    )


def rows_on(kept, landed):
    rows = kept.shape[0]

    def kernel(kept, landed, own, sent):
        own[...] = landed[:rows]
        sent[:rows], sent[rows:] = kept[...], landed[rows:]

    return small(kernel, "rows_on", [like(*kept.shape), like(2 * rows, kept.shape[1])], kept, landed)


def chosen(part, refs):
    low = jnp.where(part == 0, refs[0][...], refs[1][...])
    return jnp.where(part < 2, low, jnp.where(part == 2, refs[2][...], refs[3][...]))


def parted(low, upper):
    rows, width = low.shape
    half = width // 2

    def kernel(low, upper, out):
        for n in range(2):
            cut = slice(n * half, (n + 1) * half)
            out[n * rows : (n + 1) * rows, :half] = low[:, cut]
            out[n * rows : (n + 1) * rows, half:] = upper[:, cut]

    return small(kernel, "parted", [like(2 * rows, width)], low, upper)[0]


def traded(p, r):
    rows = p.shape[0] // 2

    def kernel(p, r, kept, sent):
        kept[:rows], kept[rows:] = p[:rows], r[:rows]
        sent[:rows], sent[rows:] = p[rows:], r[rows:]

    return small(kernel, "traded", [like(*p.shape)] * 2, p, r)


def by_z(info, p, r):
    rows = p.shape[0] // 2

    def kernel(info, p, r, kept, sent):
        turn = info[info.shape[0] - 3] ^ info[info.shape[0] - 1]
        pieces = (p[:rows], r[:rows], p[rows:], r[rows:])
        for out, first in ((kept, 0), (sent, 1)):
            for n in range(2):
                out[n * rows : (n + 1) * rows] = chosen(turn ^ (first + 2 * n), pieces)

    return small(kernel, "by_z", [like(*p.shape)] * 2, p, r, info=info)


def settle(info, p, r):
    rows = p.shape[0] // 2

    def kernel(info, p, r, out):
        pieces = (p[:rows], p[rows:], r[:rows], r[rows:])
        for n, z in enumerate((0, 2, 1, 3)):
            out[n * rows : (n + 1) * rows] = chosen(info[info.shape[0] - 1] ^ z, pieces)

    return small(kernel, "settle", [like(4 * rows, p.shape[1])], p, r, info=info)[0]


def slide_rows(index, info, slides):
    end, slide = 0, jnp.zeros(index.shape, jnp.int32)
    for q in range(slides):
        end = end + info[6 + q]
        slide = slide + (index >= end).astype(jnp.int32)
    return slide


def total_of(value):
    return jnp.sum(jnp.sum(value, axis=1, keepdims=True), axis=0, keepdims=True)


def first_message(info, low, high, prior, row, slides):
    rows, width = row.shape[1], low.shape[1]

    def kernel(info, low, high, prior, row, out, share):
        line = lax.broadcasted_iota(jnp.int32, prior.shape, 0)
        lane = lax.broadcasted_iota(jnp.int32, prior.shape, 1)
        slide = slide_rows(line * 128 + lane, info, slides)
        begin = info[4] + info[info.shape[0] - 4] * rows
        spot = begin + lax.broadcasted_iota(jnp.int32, (1, rows), 1)
        own = slide_rows(spot, info, slides)
        here = prior[pl.ds(begin // 128, rows // 128), :]
        here = jnp.concatenate([here[n : n + 1] for n in range(rows // 128)], axis=1)
        totals = jnp.zeros((1, rows), f32)
        for q in range(slides):
            totals = jnp.where(own == q, total_of(jnp.where(slide == q, prior[...], 0.0)), totals)
        here = here / totals
        share[...] = jnp.broadcast_to(here, share.shape)
        total = row[0:1, :]
        values = [total_of(jnp.where(own == q, total, 0.0)) for q in range(slides)]
        values += [total_of(jnp.where(own == q, here, 0.0)) for q in range(slides)]
        values += [total_of(here * (jnp.log(here) - jnp.log(total)))]
        place = lax.broadcasted_iota(jnp.int32, (1, 2 * width), 1)
        extra = jnp.zeros((1, 2 * width), f32)
        for n, value in enumerate(values):
            extra = jnp.where(place == n, value, extra)
        out[...] = jnp.zeros_like(out)
        out[0:3, :width], out[0:3, width:] = low[0:3, :], high[0:3, :]
        out[3:4, :] = extra

    outs = [like(8, 2 * width), like(8, rows)]
    return small(kernel, "first", outs, low, high, prior, row, info=info)


def second_message(info, low, high, cos):
    rows, width = cos.shape[1], low.shape[1]

    def kernel(info, low, high, cos, out):
        place = lax.broadcasted_iota(jnp.int32, (4, 2 * width), 1)
        line = lax.broadcasted_iota(jnp.int32, (4, 2 * width), 0)
        mine = (line == info[info.shape[0] - 3]) & (place // rows == info[info.shape[0] - 4])
        wide = jnp.concatenate([cos[0:4, :]] * (2 * width // rows), axis=1)
        out[0:3, :width], out[0:3, width:] = low[0:3, :], high[0:3, :]
        out[3:4, :] = jnp.where(place[0:1] == 0, total_of(cos[0:1, :]), 0.0)
        out[4:8, :] = jnp.where(mine, wide, 0.0)

    return small(kernel, "second", [like(8, 2 * width)], low, high, cos, info=info)[0]


def join_parts(mine, *others):
    width = mine.shape[1] // 4

    def kernel(mine, *refs):
        total = mine[...]
        line = lax.broadcasted_iota(jnp.int32, total.shape, 0)
        for part, ref in enumerate(refs[:-1], 1):
            value = ref[...]
            turned = jnp.concatenate(
                [value[:, (n ^ part) * width : ((n ^ part) + 1) * width] for n in range(4)], axis=1
            )
            total = total + jnp.where(line < 3, turned, value)
        refs[-1][...] = total

    return small(kernel, "join", [like(*mine.shape)], mine, *others)[0]


def finish(info, grad, weight, cosines, first, second, share, row, slides, scale, spots_all, genes_all):
    rows, width = grad.shape

    def kernel(info, grad, weight, c0, c1, c2, c3, first, second, share, row, out, losses, genes, spots):
        spot = info[4] + info[info.shape[0] - 4] * rows + lax.broadcasted_iota(jnp.int32, (1, rows), 1)
        own = slide_rows(spot, info, slides)
        found = lambda n: first[3:4, n : n + 1]
        mass = jnp.zeros((1, rows), f32)
        density = found(2 * slides)
        for q in range(slides):
            mass = jnp.where(own == q, found(q), mass)
            density = density + found(slides + q) * jnp.log(found(q))
        total = row[0:1, :]
        mass_grad = scale * density_weight * (total / mass - share[0:1, :]) / slides
        summed = jnp.broadcast_to(jnp.sum(weight[...], axis=1, keepdims=True), (rows, 128))
        turned = jnp.concatenate([summed[n : n + 128].T[0:1] for n in range(0, rows, 128)], axis=1)
        offset = (mass_grad - turned) / total
        loss = -(total_of(c0[0:1] + c1[0:1] + c2[0:1] + c3[0:1]) / genes_all + second[3:4, 0:1] / spots_all)
        place = lax.broadcasted_iota(jnp.int32, losses.shape, 1)
        losses[...] = jnp.where(place == 0, loss, density / slides)
        out[:rows] = grad[...]
        wide = jnp.concatenate([offset, jnp.zeros((1, width - rows), f32)], axis=1)
        out[rows:] = jnp.broadcast_to(wide, (8, width))
        both = jnp.concatenate([c0[0:1, : width // 2], c1[0:1, : width // 2]], axis=1)
        genes[...] = jnp.broadcast_to(both, genes.shape)
        group = jnp.zeros((1, width), f32)
        for n in range(8):
            line = second[4 + n // 2 : 5 + n // 2, n % 2 * width : n % 2 * width + width]
            group = jnp.where(info[5] == n, line, group)
        spots[...] = jnp.broadcast_to(group, spots.shape)

    outs = [like(rows + 8, width), like(8, 128), like(8, width), like(8, width)]
    return small(kernel, "finish", outs, grad, weight, *cosines, first, second, share, row, info=info)


def offsets(tails, rows):
    def kernel(a, b, c, d, out):
        for n, ref in enumerate((a, b, c, d)):
            for m in range(2):
                place = slice((2 * n + m) * rows, (2 * n + m + 1) * rows)
                out[:, place] = ref[8 * m : 8 * m + 8, :rows]

    spec = ((16, tails[0].shape[1]), lambda k: (rows // 8, 0))
    return small(kernel, "offsets", [like(8, 8 * rows)], *tails, blocks={n: spec for n in range(4)})[0]


def gather_expression(*parts):
    depth, half = parts[0].shape
    each = len(parts) // 4

    def kernel(*refs):
        out = refs[-1]
        for n in range(2):

            @pl.when(pl.program_id(0) == n)
            def _():
                for m in range(2):
                    total = sum(ref[...] for ref in refs[(2 * m + n) * each : (2 * m + n + 1) * each])
                    out[:, m * half : (m + 1) * half] = total

    return pl.pallas_call(
        kernel,
        name="gather",
        grid=(2,),
        in_specs=[whole((depth, half))] * len(parts),
        out_specs=pl.BlockSpec((depth, 2 * half), lambda k: (k, 0)),
        out_shape=like(2 * depth, 2 * half),
        cost_estimate=light,
        compiler_params=room(40),
    )(*parts)


def slice_4x2(logits, expression, spatial, density_prior, cell_slide, group_live, spot_counts):
    slot_dev, spot_dev = logits.shape
    gene_dev = expression.shape[1]
    groups, parts = 8, 4
    spots_all, genes_all = spot_dev * parts, gene_dev * parts
    slides = spot_counts.shape[0]
    rows = spot_dev // 8
    group_index, gene_index = lax.axis_index("cells"), lax.axis_index("genes")
    z, x = group_index // 2, group_index % 2
    scale = float(slot_dev * groups) * float(spots_all)
    spots_scale, genes_scale = scale / spots_all, scale / genes_all
    run = Steps()
    early = lambda name, value: run(name, take, value) if name in order else value

    place = 4 * x + 2 * (z % 2) + z // 2
    info = jnp.concatenate(
        [
            jnp.stack([(2 * m ^ place) // 2 for m in range(4)] + [gene_index * spot_dev, group_index]),
            spot_counts,
            group_live,
            jnp.stack([place, gene_index, place % 2, z]),
        ]
    ).astype(jnp.int32)
    prior = density_prior.reshape(-1, 128)

    pair = 2 * rows
    code = cell_slide.reshape(-1, 128)
    both = lambda move, values: [move(v) for v in values]
    cut = lambda *v: halves(v[0], 0, *v[1:])
    one, two = [[(0, 0), (0, pair)]], [[(0, 0), (0, pair)], [(1, 0), (1, pair)]]
    own_a, own_b = run(Step.own, lambda e: halves(in_hbm(e), 1), expression)
    across_a = over_y(own_a)
    beside_a, beside_b = over_core(own_a), over_core(own_b)
    wbh, wbl, tbh, tbl, tot_b = run(Step.weigh_b, lambda *v: weigh(*v, slides, 2), info, logits, code)
    sent_0, *e0 = run(
        Step.blend_0b, lambda h, l, p, q, t: blend([(h, l)], [p, q], one, (t,)), tbh, tbl, own_a, beside_a, tot_b
    )
    x_0 = over_x(sent_0)
    wah, wal, tah, tal, tot_a = run(Step.weigh_a, lambda *v: weigh(*v, slides, 0), info, logits, code)
    full = lambda groups, gather: lambda ah, al, bh, bl, *v: blend([(ah, al), (bh, bl)], gather(*v), groups)
    turned = (tah, tal, tbh, tbl)
    keep_1, sent_1, *e1 = run(
        Step.blend_1, full([[(0, 0), (1, 0)], [(0, pair), (1, pair)]], lambda p, q: [p, q]), *turned, own_b, beside_b
    )
    z_1 = over_z(sent_1, 1)
    z_1 = early(Step.taken_z1, z_1)
    (keep_0,) = run(
        Step.blend_0a, lambda h, l, p, q, t: blend([(h, l)], [p, q], one, (t,), False), tah, tal, own_a, beside_a, tot_a
    )
    beyond_a = both(over_core, run(Step.beyond_a, cut, across_a))
    across_b = over_y(run(Step.own_b, copy, own_b))
    keep_2, sent_2, *e2 = run(Step.blend_2, full(two, lambda p, *q: [p, q]), *turned, across_a, *beyond_a)
    x_2 = over_x(sent_2)
    x_2 = early(Step.taken_x2, x_2)
    keep_0, sent_0 = run(Step.half_0, lambda *v: part_total(pair, *v), keep_0, x_0)
    z_0 = over_z(sent_0, 1)
    keep_1, sent_1 = run(Step.half_1, cut, keep_1, z_1)
    x_1 = over_x(sent_1)
    beyond_b = both(over_core, run(Step.beyond_b, cut, across_b))
    g_0, g_1, g_far = run(Step.rows, lambda i, t: rows_of(i, t, rows, spot_dev // rows), info, spatial)
    g_far = over_y(g_far)
    keep_0, sent_0 = run(Step.quarter_0, lambda *v: part_total(rows, *v), keep_0, z_0)
    w_0 = over_z(sent_0, 2)
    w_0 = early(Step.taken_w0, w_0)
    keep_3, sent_3, *e3 = run(Step.blend_3, full(two, lambda p: [p]), *turned, across_b)
    x_3 = over_x(sent_3)
    keep_4, sent_4, *e4 = run(Step.blend_4, full(two, lambda *q: [q]), *turned, *beyond_b)
    x_4 = over_x(sent_4)
    x_3 = early(Step.taken_x3, x_3)
    keep_2, sent_2 = run(Step.half_2, cut, keep_2, x_2)
    z_2 = over_z(sent_2, 1)
    keep_1, sent_1 = run(Step.quarter_1, cut, keep_1, x_1)
    w_1 = over_z(sent_1, 2)
    w_1 = early(Step.taken_w1, w_1)
    g_2, g_1 = run(Step.rows_on, rows_on, g_1, g_far)
    g_1 = over_core(g_1)
    pred_0, gsum_0, part_0, inv, row = run(
        Step.stats_0, lambda p, r, g, h: stats([p], [r], [(g, 0), (h, 0)], 0), keep_0, w_0, g_0, g_1
    )
    keep_2, sent_2 = run(Step.quarter_2, cut, keep_2, z_2)
    w_2 = over_z(sent_2, 2)
    pred_1, gsum_1, part_1 = run(
        Step.stats_1, lambda p, r, i, b, g, h: stats([p], [r], [(g, 0), (h, 0)], 1, i, b),
        keep_1, w_1, inv, part_0, g_0, g_1,
    )
    keep_3, sent_3 = run(Step.half_3, cut, keep_3, x_3)
    z_3 = over_z(sent_3, 1)
    keep_4, sent_4 = run(Step.half_4, cut, keep_4, x_4)
    z_4 = over_z(sent_4, 1)
    pred_2, gsum_2, part_2 = run(
        Step.stats_2, lambda p, r, i, b, g, h: stats([p], [r], [(g, 0), (h, 1)], 0, i, b),
        keep_2, w_2, inv, part_1, g_2, g_1,
    )
    first, share = run(Step.first, lambda *v: first_message(*v, slides), info, gsum_0, gsum_2, prior, row)
    keep_3, sent_3 = run(Step.quarter_3, cut, keep_3, z_3)
    w_3 = over_z(sent_3, 2)
    keep_4, sent_4 = run(Step.quarter_4, cut, keep_4, z_4)
    w_4 = over_z(sent_4, 2)

    def sum_up(names, value):
        value = run(names[0], add, value, over_x(value))
        others = [over_z(value, 1), over_z(value, 2), over_z(value, 3)]
        value = run(names[1], add, value, *others)
        others = [over_core(value), over_y(value), shift(value, lambda k: k ^ 3, "genes")]
        return run(names[2], join_parts, value, *others)

    first = sum_up((Step.first_1, Step.first_2, Step.first_3), first)
    pred_3, gsum_3, _, spot_unit, spot_slope, spot_cos = run(
        Step.stats_3,
        lambda p, q, r, t, i, b, g, h: stats([p, q], [r, t], [(g, 0), (h, 1)], 1, i, b, True, spots_scale),
        keep_3, keep_4, w_3, w_4, inv, part_2, g_2, g_1,
    )
    second = run(Step.second, second_message, info, gsum_1, gsum_3, spot_cos)
    second = sum_up((Step.second_1, Step.second_2, Step.second_3), second)
    shared = (spot_unit, spot_slope, inv)
    d2, weight_2, cos2 = run(
        Step.grad_2, lambda p, s, u, v, i, g, h: grad_of(p, [(g, 0), (h, 1)], 0, s, 1, u, v, i, genes_scale),
        pred_2, first, *shared, g_2, g_1,
    )
    b_2 = over_z(d2, 2)
    d0, weight_0, cos0 = run(
        Step.grad_0, lambda p, s, u, v, i, b, g, h: grad_of(p, [(g, 0), (h, 0)], 0, s, 0, u, v, i, genes_scale, b),
        pred_0, first, *shared, weight_2, g_0, g_1,
    )
    home_r = over_y(run(Step.home_0, parted, pred_2, pred_3))
    home = run(Step.home_1, parted, pred_0, pred_1)
    lo_2 = run(Step.lo_2, lambda p, r: stack(p, r, rows), d2, b_2)
    c_2, xlo_2 = over_z(lo_2, 1), over_x(lo_2)
    xlo_2 = early(Step.taken_xlo2, xlo_2)
    b_0 = over_z(run(Step.go_0, copy, d0), 2)
    b_0 = early(Step.taken_b0, b_0)
    d3, weight_3, cos3 = run(
        Step.grad_3, lambda p, s, u, v, i, b, g, h: grad_of(p, [(g, 0), (h, 1)], 1, s, 1, u, v, i, genes_scale, b),
        pred_3, second, *shared, weight_0, g_2, g_1,
    )
    d1, weight_1, cos1 = run(
        Step.grad_1, lambda p, s, u, v, i, b, g, h: grad_of(p, [(g, 0), (h, 0)], 1, s, 0, u, v, i, genes_scale, b),
        pred_1, second, *shared, weight_3, g_0, g_1,
    )
    d3, losses, own_cos, group_cos = run(
        Step.finish,
        lambda i, g, w, a, b, c, d, *v: finish(i, g, w, (a, b, c, d), *v, slides, scale, spots_all, genes_all),
        info, d3, weight_1, cos0, cos1, cos2, cos3, first, second, share, row,
    )
    b_3 = over_z(d3, 2)
    home, sent = run(Step.home_2, traded, home, home_r)
    home_r = over_core(sent)
    lo_0 = run(Step.lo_0, lambda p, r: stack(p, r, rows), d0, b_0)
    c_0, xlo_0 = over_z(lo_0, 1), over_x(lo_0)
    xlo_0 = early(Step.taken_xlo0, xlo_0)
    hi_2 = run(Step.hi_2, copy, c_2)
    xhi_2 = over_x(hi_2)
    home, sent = run(Step.home_3, lambda i, p, r: by_z(i, p, r), info, home, home_r)
    home_r = over_z(sent, 1)
    lo_3 = run(Step.lo_3, lambda p, r: stack(p, r, rows), d3, b_3)
    c_3, xlo_3 = over_z(lo_3, 1), over_x(lo_3)
    xlo_3 = early(Step.taken_xlo3, xlo_3)
    hi_0 = run(Step.hi_0, copy, c_0)
    xhi_0 = over_x(hi_0)
    xhi_0 = early(Step.taken_xhi0, xhi_0)
    b_1 = over_z(run(Step.go_1, copy, d1), 2)
    b_1 = early(Step.taken_b1, b_1)
    weights = (wah, wal, wbh, wbl)
    back_share = lambda a, b, c, d, *v: share_of((a, b, c, d), [(p, 0) for p in v])
    *parts_2, dh2, dl2 = run(Step.share_2, back_share, *weights, lo_2, hi_2, xlo_2, xhi_2)
    chip_a = both(over_core, parts_2[2:])
    hi_3 = run(Step.hi_3, copy, c_3)
    xhi_3 = over_x(hi_3)
    chip_a = over_y(run(Step.chip_a, add_rows, *parts_2[:2], *chip_a))
    chip_a = early(Step.taken_chip_a, chip_a)
    lo_1 = run(Step.lo_1, lambda p, r: stack(p, r, rows), d1, b_1)
    c_1, xlo_1 = over_z(lo_1, 1), over_x(lo_1)
    xlo_1 = early(Step.taken_xlo1, xlo_1)
    *parts_3, dh3, dl3 = run(Step.share_3, back_share, *weights, lo_3, hi_3, xlo_3, xhi_3)
    chip_b = both(over_core, parts_3[2:])
    hi_1 = run(Step.hi_1, copy, c_1)
    xhi_1 = over_x(hi_1)
    chip_b = over_y(run(Step.chip_b, add_rows, *parts_3[:2], *chip_b))
    home, sent = run(Step.home_4, traded, home, home_r)
    home_r = over_z(sent, 2)
    mg = run(Step.back_2, lambda a, b, c, d: back([(a, b)], (c, d)), *e2, dh2, dl2)
    mg = run(Step.back_3, lambda a, b, c, d, e, f, g: back([(a, b), (c, d)], (e, f), g), *e3, *e4, dh3, dl3, mg)
    offset = run(Step.offsets, lambda *v: offsets(v, rows), lo_3, hi_3, xlo_3, xhi_3)
    outcome = run(
        Step.near,
        lambda i, wh, wl, e0h, e0l, e1h, e1l, mg, off, a, b, c, d, p: half_of(
            i, 0, (wh, wl), [a, b, c, d], (0, 1), ((0, p),), [e0h, e0l, e1h, e1l, mg, off]
        ),
        info, wah, wal, *e0, *e1, mg, offset, lo_0, hi_0, lo_1, hi_1, chip_a,
    )
    near_grad, near = outcome[0], outcome[1:]
    def far(base):
        return lambda i, wh, wl, e0h, e0l, e1h, e1l, mg, off, a, b, grad, *v: half_of(
            i, base, (wh, wl), [a, b], (0, 1), (), [e0h, e0l, e1h, e1l, mg, off], grad, v
        )

    passed = run(Step.far_lo, far(2), info, wbh, wbl, *e0, *e1, mg, offset, xlo_0, xlo_1, near_grad, *near)
    grad_logits, *shares = run(Step.far_hi, far(3), info, wbh, wbl, *e0, *e1, mg, offset, xhi_0, xhi_1, *passed)
    core_a, core_b = both(over_core, shares[2:4]), both(over_core, shares[6:])
    pred_out = run(Step.settle, lambda i, p, r: settle(i, p, r), info, home, home_r)
    shares[4:6] = run(Step.late, add_below, *shares[4:6], chip_b)
    summands = []
    for kept, core in ((shares[0:2], core_a), (shares[4:6], core_b)):
        for n in range(2):
            summands += [kept[n], core[n]]
    grad_expression = run(Step.gather, gather_expression, *summands)
    run.run(order)
    get = lambda v: run.value(v)
    losses = get(losses)
    return (
        get(pred_out), get(own_cos)[0], get(group_cos)[0], losses[0, 0], losses[0, 1], get(grad_logits), get(grad_expression)
    )


order = (
    Step.own, Step.weigh_b, Step.blend_0b, Step.weigh_a, Step.blend_1, Step.own_b, Step.blend_0a, Step.beyond_a,
    Step.blend_2, Step.half_0, Step.half_1, Step.rows, Step.beyond_b, Step.blend_3, Step.quarter_0, Step.blend_4,
    Step.half_2, Step.rows_on, Step.taken_w0, Step.quarter_1, Step.half_4, Step.quarter_2, Step.half_3,
    Step.stats_0, Step.taken_w1, Step.stats_1, Step.stats_2, Step.quarter_4, Step.first, Step.quarter_3,
    Step.first_1, Step.first_2, Step.stats_3, Step.first_3, Step.grad_2, Step.home_0, Step.grad_0, Step.second,
    Step.second_1, Step.home_1, Step.second_2, Step.lo_2, Step.go_0, Step.second_3, Step.grad_3, Step.home_2,
    Step.grad_1, Step.go_1, Step.finish, Step.lo_0, Step.hi_2, Step.taken_xlo2, Step.home_3, Step.lo_3,
    Step.share_2, Step.hi_0, Step.taken_xlo3, Step.back_2, Step.chip_a, Step.hi_3, Step.taken_xlo0, Step.lo_1,
    Step.offsets, Step.share_3, Step.hi_1, Step.taken_chip_a, Step.taken_xlo1, Step.back_3, Step.home_4,
    Step.chip_b, Step.near, Step.far_lo, Step.far_hi, Step.settle, Step.late, Step.gather,
)


def solution(mesh):
    fits = mesh.shape["cells"] == 8 and mesh.shape["genes"] == 4
    return jax.shard_map(
        slice_4x2 if fits else spread,
        mesh=mesh,
        in_specs=(
            P("cells", "genes"),
            P("cells", "genes"),
            P(None, "genes"),
            P(),
            P("cells"),
            P(),
            P(),
        ),
        out_specs=(
            P("cells", "genes"),
            P("genes"),
            P("cells"),
            P(),
            P(),
            P("cells", "genes"),
            P("cells", "genes"),
        ),
        check_vma=False,
    )
```

```python
import functools

import jax
import jax.numpy as jnp
from jax import lax
from jax.experimental import pallas as pl
from jax.experimental.pallas import tpu as pltpu
from jax.sharding import PartitionSpec as P

eps_norm = 1e-06
density_weight = 0.01
high = lax.Precision.HIGH
highest = lax.Precision.HIGHEST


def slide_of(spot_index, slide_ends):
    return jnp.sum((spot_index[:, None] >= slide_ends[None, :]).astype(jnp.int32), axis=1)


def live_of(group_live, group_index, slot_dev):
    groups = group_live.shape[0]
    here = jnp.arange(groups, dtype=jnp.int32) == group_index
    return jnp.arange(slot_dev, dtype=jnp.int32) < jnp.sum(jnp.where(here, group_live, 0))


def spread(logits, expression, spatial, density_prior, cell_slide, group_live, spot_counts):
    slot_dev, spot_dev = logits.shape
    gene_dev = expression.shape[1]
    groups, parts = lax.axis_size("cells"), lax.axis_size("genes")
    spots_all, genes_all = spot_dev * parts, gene_dev * parts
    spot_rows = spots_all // groups
    slides = spot_counts.shape[0]
    group_index, gene_index = lax.axis_index("cells"), lax.axis_index("genes")
    scale = float(slot_dev * groups) * float(spots_all)
    slide_ends = jnp.cumsum(spot_counts)
    spot_slide = slide_of(jnp.arange(spots_all, dtype=jnp.int32), slide_ends)
    own_slide = lax.dynamic_slice_in_dim(spot_slide, gene_index * spot_dev, spot_dev)
    slot_live = live_of(group_live, group_index, slot_dev)
    allowed = slot_live[:, None] & (cell_slide[:, None] == own_slide[None, :])
    weight = jnp.where(allowed, jnp.exp(logits), 0.0)
    spot_total = lax.psum(jnp.sum(weight, axis=0), "cells")
    mapping = weight / spot_total[None, :]
    full_map, full_total = (
        lax.all_gather(mapping, "genes", axis=1, tiled=True),
        lax.all_gather(spot_total, "genes", axis=0, tiled=True),
    )
    pred_rows = lax.psum_scatter(
        lax.dot_general(full_map, expression, (((0,), (0,)), ((), ())), precision=highest),
        "cells",
        scatter_dimension=0,
        tiled=True,
    )
    spatial_rows = lax.dynamic_slice_in_dim(spatial, group_index * spot_rows, spot_rows, 0)
    triple = (pred_rows * spatial_rows, pred_rows * pred_rows, spatial_rows * spatial_rows)
    gene_dot, gene_pp, gene_gg = lax.psum(
        jnp.stack([jnp.sum(part, axis=0) for part in triple]), "cells"
    )
    spot_dot, spot_pp, spot_gg = lax.psum(
        jnp.stack([jnp.sum(part, axis=1) for part in triple]), "genes"
    )
    gene_unit = lax.rsqrt(gene_pp + eps_norm) * lax.rsqrt(gene_gg + eps_norm)
    gene_cos = gene_dot * gene_unit
    spot_unit = lax.rsqrt(spot_pp + eps_norm) * lax.rsqrt(spot_gg + eps_norm)
    spot_cos = spot_dot * spot_unit
    gene_term = gene_unit[None, :] * spatial_rows - (gene_cos / (gene_pp + eps_norm))[None, :] * pred_rows
    spot_term = spot_unit[:, None] * spatial_rows - (spot_cos / (spot_pp + eps_norm))[:, None] * pred_rows
    grad_rows = -(scale / genes_all) * gene_term - scale / spots_all * spot_term
    loss_part = jnp.sum(gene_cos) / (genes_all * groups) + jnp.sum(spot_cos) / (spots_all * parts)
    cos_loss = -lax.psum(loss_part, ("cells", "genes"))
    grad_full = lax.all_gather(grad_rows, "cells", axis=0, tiled=True)
    member = spot_slide[None, :] == jnp.arange(slides, dtype=jnp.int32)[:, None]
    prior_total = jnp.sum(jnp.where(member, density_prior[None, :], 0.0), axis=1)
    prior_norm = density_prior / jnp.sum(jnp.where(member, prior_total[:, None], 0.0), axis=0)
    slide_sum = jnp.sum(jnp.where(member, full_total[None, :], 0.0), axis=1)
    share = full_total / jnp.sum(jnp.where(member, slide_sum[:, None], 0.0), axis=0)
    density_loss = jnp.sum(prior_norm * (jnp.log(prior_norm) - jnp.log(share))) / slides
    mass_grad = scale * density_weight * (share - prior_norm) / slides
    own_mass_grad = lax.dynamic_slice_in_dim(mass_grad, gene_index * spot_dev, spot_dev)
    partial_grad = lax.dot_general(expression, grad_full, (((1,), (1,)), ((), ())), precision=highest)
    map_grad = lax.psum_scatter(partial_grad, "genes", scatter_dimension=1, tiled=True)
    grad_expression = jnp.dot(full_map, grad_full, precision=highest)
    spot_weight = lax.psum(jnp.sum(mapping * map_grad, axis=0), "cells")
    grad_logits = mapping * (map_grad - spot_weight[None, :] + own_mass_grad[None, :])
    return (pred_rows, gene_cos, spot_cos, cos_loss, density_loss, grad_logits, grad_expression)


def shift(value, moves, axis):
    if isinstance(value, Later):
        return Later(value, moved=value, move=lambda v: shift(v, moves, axis))
    count = lax.axis_size(axis)
    pairs = [(k, moves(k)) for k in range(count) if moves(k) is not None]
    return lax.ppermute(value, axis, pairs)


def over_x(value):
    return shift(value, lambda k: k ^ 1, "cells")


def over_y(value):
    return shift(value, lambda k: k ^ 2, "genes")


def over_core(value):
    return shift(value, lambda k: k ^ 1, "genes")


def over_z(value, step):
    return shift(value, lambda k: k ^ (2 * step), "cells")


class Step:
    (
        own, weigh_b, blend_0b, weigh_a, blend_1, blend_0a, beyond_a, own_b, blend_2, half_0, half_1,
        beyond_b, rows, quarter_0, blend_3, blend_4, half_2, quarter_1, rows_on, stats_0, quarter_2,
        stats_1, half_3, half_4, stats_2, first, quarter_3, quarter_4, stats_3, second, grad_2, grad_0,
        home_0, home_1, lo_2, go_0, grad_3, grad_1, finish, home_2, lo_0, hi_2, home_3, lo_3, hi_0, go_1,
        share_2, hi_3, chip_a, lo_1, share_3, hi_1, chip_b, home_4, back_2, back_3, offsets, near, far_lo,
        far_hi, settle, late, gather, taken_z1, taken_x2, taken_w0, taken_x3, taken_w1, taken_xlo2,
        taken_b0, taken_xlo0, taken_xlo3, taken_xhi0, taken_b1, taken_chip_a, taken_xlo1, first_1, first_2,
        first_3, second_1, second_2, second_3,
    ) = range(82)


class Later:
    def __init__(self, like, step=None, place=None, moved=None, move=None):
        self.shape, self.dtype = like.shape, like.dtype
        self.step, self.place, self.moved, self.move = step, place, moved, move


class Steps:
    def __init__(self):
        self.steps, self.values, self.arrived = {}, {}, {}

    def __call__(self, name, step, *operands):
        shapes = [jax.ShapeDtypeStruct(v.shape, v.dtype) for v in operands]
        out = jax.eval_shape(step, *shapes)
        leaves, tree = jax.tree.flatten(out)
        self.steps[name] = (step, operands)
        return jax.tree.unflatten(tree, [Later(v, name, n) for n, v in enumerate(leaves)])

    def value(self, operand):
        if not isinstance(operand, Later):
            return operand
        if operand.step is not None:
            return self.values[operand.step][operand.place]
        if operand not in self.arrived:
            self.arrived[operand] = operand.move(self.value(operand.moved))
        return self.arrived[operand]

    def run(self, order):
        last = None
        for name in order:
            step, operands = self.steps[name]
            operands = [self.value(v) for v in operands]
            if last is not None:
                operands, _ = lax.optimization_barrier((operands, last))
            self.values[name] = jax.tree.leaves(step(*operands))
            last = self.values[name][0]


f32, bf16 = jnp.float32, jnp.bfloat16


def split(value):
    upper = value.astype(bf16)
    return upper, (value - upper.astype(f32)).astype(bf16)


def mul(p, q):
    return jnp.dot(p, q, preferred_element_type=f32)


def mul_t(p, q):
    return lax.dot_general(p, q, (((1,), (1,)), ((), ())), preferred_element_type=f32)


def whole(shape):
    return pl.BlockSpec(shape, lambda *k: (0,) * len(shape), pipeline_mode=pl.Buffered(1))


def like(*shape, dtype=f32):
    return jax.ShapeDtypeStruct(shape, dtype)


def room(mebi):
    return pltpu.CompilerParams(vmem_limit_bytes=mebi << 20)


light = pl.CostEstimate(flops=1, bytes_accessed=1, transcendentals=0)


def in_hbm(value):
    return pltpu.with_memory_space_constraint(value, pltpu.HBM)


def weigh_kernel(slides, base, info, table, code, wh, wl, th, tl, tot):
    k = base + pl.program_id(0)
    depth, width = table.shape
    half = width // 2
    odd = info[info.shape[0] - 2]
    lane = lax.broadcasted_iota(jnp.int32, (1, width), 1)
    spot = info[4] + info[k] * width + jnp.where(odd == 1, lane ^ half, lane)
    slide = slide_rows(spot, info, slides).astype(f32)
    alive = info[6 + slides + info[5]]

    def step(a, total):
        at = pl.multiple_of(a * 128, 128)
        own = jnp.broadcast_to(code[pl.ds(a, 1), :].astype(f32), (128, 128)).T
        own = jnp.concatenate([own] * (width // 128), axis=1)
        live = at + lax.broadcasted_iota(jnp.int32, (128, width), 0) < alive
        value = table[pl.ds(at, 128), :]
        value = jnp.where(odd == 1, jnp.concatenate([value[:, half:], value[:, :half]], axis=1), value)
        w = jnp.where((own == slide) & live, jnp.exp(value), 0.0)
        wh[pl.ds(at, 128), :], wl[pl.ds(at, 128), :] = split(w)
        th[:, pl.ds(at, 128)], tl[:, pl.ds(at, 128)] = split(w.T)
        return total + jnp.sum(w, axis=0, keepdims=True)

    total = lax.fori_loop(0, depth // 128, step, jnp.zeros((1, width), f32), unroll=True)
    tot[...] = jnp.broadcast_to(total, tot.shape)


def weigh(info, logits, code, slides, base):
    depth, spots = logits.shape
    rows = spots // 4
    wide = pl.BlockSpec((depth, rows), lambda k, info: (0, k))
    tall = pl.BlockSpec((rows, depth), lambda k, info: (k, 0))
    return pl.pallas_call(
        functools.partial(weigh_kernel, slides, base),
        name="weigh",
        grid_spec=pltpu.PrefetchScalarGridSpec(
            num_scalar_prefetch=1,
            grid=(2,),
            in_specs=[
                pl.BlockSpec((depth, rows), lambda k, info: (0, info[base + k])),
                pl.BlockSpec(code.shape, lambda k, info: (0, 0)),
            ],
            out_specs=[wide, wide, tall, tall, pl.BlockSpec((8, rows), lambda k, info: (0, k))],
        ),
        out_shape=[
            like(depth, 2 * rows, dtype=bf16),
            like(depth, 2 * rows, dtype=bf16),
            like(2 * rows, depth, dtype=bf16),
            like(2 * rows, depth, dtype=bf16),
            like(8, 2 * rows),
        ],
        cost_estimate=light,
        compiler_params=room(12),
    )(info, in_hbm(logits), in_hbm(code))


def blend_kernel(groups, pair, sources, halved, has_total, save, *refs):
    k = pl.program_id(0)
    parts = []
    for half in halved:
        parts.append(jnp.where(k < 2, refs[0][...], refs[1][...]) if half else refs[0][...])
        refs = refs[1 + half :]
    width = parts[0].shape[1]
    lefts, refs = refs[: 2 * sources], refs[2 * sources :]
    tots, outs = (refs[:sources], refs[sources:]) if has_total else ((), refs)

    @pl.when(k == 0)
    def _():
        for out, chunks in zip(outs, groups):
            out[...] = jnp.zeros_like(out)
            if has_total:
                for m, (n, begin) in enumerate(chunks):
                    out[len(chunks) * pair :, m * pair : (m + 1) * pair] = tots[n][:, begin : begin + pair]

    for c, part in enumerate(parts):
        place = slice(c * width, (c + 1) * width)
        upper, lower = split(part)
        if save:
            outs[-2][:, place], outs[-1][:, place] = upper, lower
        values = []
        for n in range(sources):
            th, tl = lefts[2 * n : 2 * n + 2]
            values.append(mul(th[...], upper) + mul(th[...], lower) + mul(tl[...], upper))
        for out, chunks in zip(outs, groups):
            for m, (n, begin) in enumerate(chunks):
                out[m * pair : (m + 1) * pair, place] += values[n][begin : begin + pair]


def blend(sources, parts, groups, tots=(), save=True):
    spots, depth = sources[0][0].shape
    halved = [isinstance(part, tuple) for part in parts]
    pair, width = spots // 2, (parts[0][0] if halved[0] else parts[0]).shape[1]
    deep, wide = depth // 4, len(parts) * width
    extra = 8 if tots else 0
    column = pl.BlockSpec((spots, deep), lambda k: (0, k))
    row = pl.BlockSpec((deep, width), lambda k: (k, 0))
    top = pl.BlockSpec((deep, width), lambda k: (jnp.minimum(k, 1), 0))
    bottom = pl.BlockSpec((deep, width), lambda k: (jnp.maximum(k - 2, 0), 0))
    both = pl.BlockSpec((deep, wide), lambda k: (k, 0))
    specs, given = [], []
    for part, half in zip(parts, halved):
        specs += [top, bottom] if half else [row]
        given += part if half else [part]
    number = len(sources)
    heights = [len(chunks) * pair + extra for chunks in groups]
    return pl.pallas_call(
        functools.partial(blend_kernel, groups, pair, number, halved, bool(tots), save),
        name="blend",
        grid=(4,),
        in_specs=specs + [column] * 2 * number + [whole(t.shape) for t in tots],
        out_specs=[pl.BlockSpec((h, wide), lambda k: (0, 0)) for h in heights] + [both, both] * save,
        out_shape=[like(h, wide) for h in heights] + [like(depth, wide, dtype=bf16)] * 2 * save,
        cost_estimate=light,
        compiler_params=room(14),
    )(*given, *[t for source in sources for t in source], *tots)


def stats_kernel(first, last, spots_scale, pieces, *refs):
    refs = list(refs)
    glue = lambda parts: jnp.concatenate([ref[...] for ref in parts], axis=1)
    close, found = glue(refs[:pieces]), glue(refs[pieces : 2 * pieces])
    gp, gq = refs[2 * pieces : 2 * pieces + 2]
    refs = refs[2 * pieces + 2 :]
    rows = gp.shape[0]
    if first:
        inv, row = refs[-2:]
        total = close[rows : rows + 1, :rows] + found[rows : rows + 1, :rows]
        row[...] = jnp.broadcast_to(total, row.shape)
        for b in range(0, rows, 128):
            inv[b : b + 128, :] = 1.0 / jnp.broadcast_to(total[:, b : b + 128], (128, 128)).T
        inverse = inv[...]
    else:
        inverse = refs[0][...]
        before = refs[1]
        refs = refs[2:]
    pred, gsum, part = refs[:3]
    width = close.shape[1]
    value = (close[:rows] + found[:rows]) * jnp.concatenate([inverse] * (width // 128), axis=1)
    pred[...] = value
    g = jnp.concatenate([gp[...], gq[...]], axis=1)
    sums = []
    for n, product in enumerate((value * g, value * value, g * g)):
        gsum[n : n + 1, :] = jnp.sum(product, axis=0, keepdims=True)
        lanes = sum(product[:, c : c + 128] for c in range(0, width, 128))
        if not first:
            lanes = lanes + before[:, n * 128 : n * 128 + 128]
        sums.append(lanes)
        part[:, n * 128 : n * 128 + 128] = lanes
    gsum[3:, :] = jnp.zeros((5, width), f32)
    if last:
        unit_out, slope_out, cos_out = refs[3:]
        dot, pp, gg = [jnp.sum(lanes, axis=1, keepdims=True) for lanes in sums]
        unit = lax.rsqrt(pp + eps_norm) * lax.rsqrt(gg + eps_norm)
        cos = dot * unit
        wide = lambda v: jnp.broadcast_to(v, (rows, 128))
        unit_out[...] = wide(unit * spots_scale)
        slope_out[...] = wide(spots_scale * cos / (pp + eps_norm))
        for b in range(0, rows, 128):
            turned = wide(cos)[b : b + 128].T
            cos_out[:, b : b + 128] = turned[:8]


def part_blocks(parts, cut, rows):
    width = parts[0][0].shape[1]
    return [
        pl.BlockSpec((rows, width // 2), functools.partial(lambda n, k: (n, cut), n), pipeline_mode=pl.Buffered(1))
        for _, n in parts
    ]


def stats(close, found, parts, cut, inv=None, before=None, last=False, spots_scale=0.0):
    width = parts[0][0].shape[1]
    rows = close[0].shape[0] - (8 if inv is None else 0)
    first = inv is None
    outs = [like(rows, width), like(8, width), like(rows, 384)]
    if first:
        outs += [like(rows, 128), like(8, rows)]
    if last:
        outs += [like(rows, 128), like(rows, 128), like(8, rows)]
    extra = () if first else (inv, before)
    landed = [whole(v.shape) for v in close + found]
    return pl.pallas_call(
        functools.partial(stats_kernel, first, last, spots_scale, len(close)),
        name="stats",
        grid=(1,),
        in_specs=landed + part_blocks(parts, cut, rows) + [whole(v.shape) for v in extra],
        out_specs=[whole(o.shape) for o in outs],
        out_shape=outs,
        cost_estimate=light,
        compiler_params=room(8),
    )(*close, *found, *[p for p, _ in parts], *extra)


def grad_kernel(genes_scale, chain, pred, gp, gq, red, unit_in, slope_in, inv, *refs):
    width = pred.shape[1]
    out, weight, cos_out = refs[-3:]
    dot, pp, gg = red[0:1, :], red[1:2, :], red[2:3, :]
    unit = lax.rsqrt(pp + eps_norm) * lax.rsqrt(gg + eps_norm)
    cos = dot * unit
    cos_out[...] = jnp.broadcast_to(cos, cos_out.shape)
    slope = genes_scale * cos / (pp + eps_norm)
    wide = lambda v: jnp.concatenate([v[...]] * (width // 128), axis=1)
    g = jnp.concatenate([gp[...], gq[...]], axis=1)
    p = pred[...]
    grad = (slope + wide(slope_in)) * p - (genes_scale * unit + wide(unit_in)) * g
    out[...] = grad * wide(inv)
    product = grad * p
    lanes = sum(product[:, c : c + 128] for c in range(0, width, 128))
    weight[...] = lanes + refs[0][...] if chain else lanes


def grad_of(pred, parts, cut, red, q, unit, slope, inv, genes_scale, before=None):
    rows, width = pred.shape
    extra = () if before is None else (before,)
    outs = [like(rows, width), like(rows, 128), like(8, width)]
    return pl.pallas_call(
        functools.partial(grad_kernel, genes_scale, before is not None),
        name="grad",
        grid=(1,),
        in_specs=[whole(pred.shape)] + part_blocks(parts, cut, rows) + [pl.BlockSpec((8, width), lambda k: (0, q))]
        + [whole(v.shape) for v in (unit, slope, inv) + extra],
        out_specs=[whole(o.shape) for o in outs],
        out_shape=outs,
        cost_estimate=light,
        compiler_params=room(8),
    )(pred, *[p for p, _ in parts], red, unit, slope, inv, *extra)


def share_kernel(wah, wal, wbh, wbl, a, b, c, d, p0, p1, q0, q1, dh, dl):
    k = pl.program_id(0)
    deep, half = p0.shape
    wh = jnp.where(k < 2, wah[...], wbh[...])
    wl = jnp.where(k < 2, wal[...], wbl[...])

    @pl.when(k == 0)
    def _():
        for out in (p0, p1, q0, q1):
            out[...] = jnp.zeros_like(out)

    value = jnp.where(k < 2, jnp.where(k == 0, a[...], b[...]), jnp.where(k == 2, c[...], d[...]))
    upper, lower = split(value)
    dh[...], dl[...] = upper, lower
    for place, top, bottom in ((slice(0, half), p0, p1), (slice(half, 2 * half), q0, q1)):
        up, low = upper[:, place], lower[:, place]
        value = mul(wh, up) + mul(wh, low) + mul(wl, up)
        top[...] += value[:deep]
        bottom[...] += value[deep:]


def share_of(weights, pieces):
    depth, spots = weights[0].shape[0], 2 * weights[0].shape[1]
    rows, width = spots // 4, pieces[0][0].shape[1]
    near = pl.BlockSpec((depth, rows), lambda k: (0, jnp.minimum(k, 1)))
    far = pl.BlockSpec((depth, rows), lambda k: (0, jnp.maximum(k - 2, 0)))
    row = pl.BlockSpec((rows, width), lambda k: (k, 0))
    return pl.pallas_call(
        share_kernel,
        name="share",
        grid=(4,),
        in_specs=[near, near, far, far]
        + [
            pl.BlockSpec((rows, width), functools.partial(lambda n, k: (n, 0), n), pipeline_mode=pl.Buffered(1))
            for _, n in pieces
        ],
        out_specs=[pl.BlockSpec((depth // 2, width // 2), lambda k: (0, 0))] * 4 + [row, row],
        out_shape=[like(depth // 2, width // 2)] * 4 + [like(spots, width, dtype=bf16)] * 2,
        cost_estimate=light,
        compiler_params=room(14),
    )(*weights, *[piece for piece, _ in pieces])


def back_kernel(widths, chain, *refs):
    out, dh, dl = refs[-1], refs[2 * len(widths)], refs[2 * len(widths) + 1]
    begin, total = 0, refs[-2][...] if chain else None
    for n, width in enumerate(widths):
        eh, el = refs[2 * n : 2 * n + 2]
        upper, lower = dh[:, begin : begin + width], dl[:, begin : begin + width]
        begin += width
        value = mul_t(eh[...], upper) + mul_t(eh[...], lower) + mul_t(el[...], upper)
        total = value if total is None else total + value
    out[...] = total


def back(lefts, d, past=None):
    depth = lefts[0][0].shape[0]
    spots, width = d[0].shape
    rows = spots // 4
    row = pl.BlockSpec((rows, width), lambda k: (k, 0))
    column = pl.BlockSpec((depth, rows), lambda k: (0, k))
    parts = [part for both in lefts for part in both]
    return pl.pallas_call(
        functools.partial(back_kernel, [upper.shape[1] for upper, _ in lefts], past is not None),
        name="back",
        grid=(4,),
        in_specs=[whole(part.shape) for part in parts] + [row] * 2 + ([] if past is None else [column]),
        out_specs=column,
        out_shape=like(depth, spots),
        cost_estimate=light,
        compiler_params=room(12),
    )(*parts, *d, *(() if past is None else (past,)))


def half_kernel(sides, grads, chain, added, blocks, info, wh, wl, *refs):
    k = pl.program_id(0)
    refs = list(refs)
    if grads:
        eh0, el0, eh1, el1, mg, offset = refs[:6]
        refs = refs[6:]
    pieces, refs = (refs[:blocks], refs[blocks : 2 * blocks]), refs[2 * blocks :]
    number = 4 * len(sides)
    more, past = refs[: len(added)], refs[len(added) + (chain and grads) :][:number]
    shares = refs[-number:]
    grad = refs[-number - 1]
    deep, half = shares[0].shape

    @pl.when(k == 0)
    def _():
        for n, share in enumerate(shares):
            share[...] = past[n][...] if chain else jnp.zeros_like(share)
        for n, ref in zip(added, more):
            shares[n][...] += ref[:deep]
            shares[n + 1][...] += ref[deep:]

    total = mg[...] if grads else None
    for n in range(2):
        piece = pieces[n][0][...] if blocks == 1 else jnp.where(k == 0, pieces[n][0][...], pieces[n][1][...])
        upper, lower = split(piece)
        if grads:
            eh, el = ((eh0, el0), (eh1, el1))[n]
            total += mul_t(eh[...], upper) + mul_t(eh[...], lower) + mul_t(el[...], upper)
        for m, side in enumerate(sides):
            place = slice(side * half, (side + 1) * half)
            up, low = upper[:, place], lower[:, place]
            value = mul(wh[...], up) + mul(wh[...], low) + mul(wl[...], up)
            at = 2 * (len(sides) * n + m)
            shares[at][...] += value[:deep]
            shares[at + 1][...] += value[deep:]
    if grads:
        value = (wh[...].astype(f32) + wl[...].astype(f32)) * (total + offset[0:1, :])
        width = value.shape[1] // 2
        turned = jnp.concatenate([value[:, width:], value[:, :width]], axis=1)
        grad[...] = jnp.where(info[info.shape[0] - 2] == 1, turned, value)


def half_of(info, base, weights, pieces, sides, added=(), grads=(), grad=None, past=()):
    depth, width = weights[0].shape[0], pieces[0].shape[1]
    rows = weights[0].shape[1] // 2
    spots = 4 * rows
    blocks = len(pieces) // 2
    local = pl.BlockSpec((depth, rows), lambda k, info: (0, base % 2 + k))
    column = pl.BlockSpec((depth, rows), lambda k, info: (0, base + k))
    line = pl.BlockSpec((8, rows), lambda k, info: (0, base + k))
    part = whole((depth // 2, width // 2))
    specs, given = [local, local], list(weights)
    if grads:
        specs += [whole((depth, width))] * 4 + [column, line]
        given += grads
    specs += [pl.BlockSpec((rows, width), lambda k, info: (0, 0), pipeline_mode=pl.Buffered(1))] * len(pieces)
    given += pieces
    specs += [whole((depth, width // 2))] * len(added)
    given += [array for _, array in added]
    aliases = {}
    if grad is not None:
        aliases = {1 + len(given): 0}
        specs.append(pl.BlockSpec(memory_space=pl.ANY))
        given.append(grad)
    specs += [part] * len(past)
    given += past
    number = 4 * len(sides)
    outs = [like(depth, spots)] if grads else []
    out_specs = [pl.BlockSpec((depth, rows), lambda k, info: (0, info[base + k]))] if grads else []
    return pl.pallas_call(
        functools.partial(half_kernel, sides, bool(grads), bool(past), [n for n, _ in added], blocks),
        name="half",
        grid_spec=pltpu.PrefetchScalarGridSpec(
            num_scalar_prefetch=1,
            grid=(blocks,),
            in_specs=specs,
            out_specs=out_specs + [pl.BlockSpec((depth // 2, width // 2), lambda k, info: (0, 0))] * number,
        ),
        out_shape=outs + [like(depth // 2, width // 2)] * number,
        input_output_aliases=aliases,
        cost_estimate=light,
        compiler_params=room(26 if grads else 14),
    )(info, *given)


def small(kernel, name, outs, *operands, info=None, blocks=None, scratch=()):
    specs = []
    for n, operand in enumerate(operands):
        shape, index = (operand.shape, None) if blocks is None or n not in blocks else blocks[n]
        if index is None:
            index = lambda k, *info, rank=len(shape): (0,) * rank
        specs.append(pl.BlockSpec(shape, index, pipeline_mode=pl.Buffered(1)))
    out_specs = [whole(o.shape) for o in outs]
    scalars = () if info is None else (info,)
    return pl.pallas_call(
        kernel,
        name=name,
        grid_spec=pltpu.PrefetchScalarGridSpec(
            num_scalar_prefetch=len(scalars), grid=(1,), in_specs=specs, out_specs=out_specs, scratch_shapes=list(scratch)
        ),
        out_shape=outs,
        cost_estimate=light,
        compiler_params=room(8),
    )(*scalars, *operands)


def add(*parts):
    def kernel(*refs):
        total = refs[0][...]
        for ref in refs[1:-1]:
            total = total + ref[...]
        refs[-1][...] = total

    return small(kernel, "add", [like(*parts[0].shape)], *parts)[0]


def add_rows(p, q, r, t):
    rows = p.shape[0]

    def kernel(p, q, r, t, out):
        out[:rows], out[rows:] = p[...] + r[...], q[...] + t[...]

    return small(kernel, "add_rows", [like(2 * rows, p.shape[1])], p, q, r, t)[0]


def add_below(p, q, both):
    rows = p.shape[0]

    def kernel(p, q, both, first, second):
        first[...], second[...] = p[...] + both[:rows], q[...] + both[rows:]

    return small(kernel, "add_below", [like(*p.shape)] * 2, p, q, both)


def halves(table, axis, *others):
    rows, columns = table.shape
    half = (rows // 2, columns) if axis == 0 else (rows, columns // 2)

    def kernel(*refs):
        total = refs[0][...]
        for ref in refs[1:-2]:
            total = total + ref[...]
        if axis == 0:
            refs[-2][...], refs[-1][...] = total[: rows // 2], total[rows // 2 :]
        else:
            refs[-2][...], refs[-1][...] = total[:, : columns // 2], total[:, columns // 2 :]

    return small(kernel, "halves", [like(*half)] * 2, table, *others)


def copy(value):
    def kernel(value, out):
        out[...] = value[...]

    return small(kernel, "copy", [like(*value.shape)], value)[0]


def take(value):
    anywhere = pl.BlockSpec(memory_space=pl.ANY)
    return pl.pallas_call(
        lambda value, out: None,
        name="take",
        in_specs=[anywhere],
        out_specs=anywhere,
        out_shape=like(*value.shape),
        input_output_aliases={0: 0},
        cost_estimate=light,
        compiler_params=room(1),
    )(value)


def part_total(rows, *parts):
    width = parts[0].shape[1]

    def kernel(*refs):
        total = refs[0][...]
        for ref in refs[1:-2]:
            total = total + ref[...]
        for n, out in enumerate(refs[-2:]):
            out[:rows] = total[n * rows : (n + 1) * rows]
            line = total[2 * rows :, n * rows : (n + 1) * rows]
            out[rows:] = jnp.concatenate([line, jnp.zeros((8, width - rows), f32)], axis=1)

    return small(kernel, "part_total", [like(rows + 8, width)] * 2, *parts)


def stack(p, r, rows):
    extra = p.shape[0] - rows

    def kernel(p, r, out):
        out[:rows], out[rows : 2 * rows] = p[:rows], r[:rows]
        if extra:
            out[2 * rows : 2 * rows + extra], out[2 * rows + extra :] = p[rows:], r[rows:]

    return small(kernel, "stack", [like(2 * p.shape[0], p.shape[1])], p, r)[0]


def rows_of(info, table, rows, per_part):
    shape = (rows, table.shape[1])

    def kernel(info, a, b, c, d, first, second, rest):
        first[...], second[...] = a[...], b[...]
        rest[:rows], rest[rows:] = c[...], d[...]

    def index(part):
        return lambda k, info: ((info[info.shape[0] - 3] ^ part) * per_part + info[info.shape[0] - 4], 0)

    return small(
        kernel, "rows", [like(*shape), like(*shape), like(2 * rows, shape[1])], *[table] * 4, info=info,
        blocks={r: (shape, index(r)) for r in range(4)},
    )


def rows_on(kept, landed):
    rows = kept.shape[0]

    def kernel(kept, landed, own, sent):
        own[...] = landed[:rows]
        sent[:rows], sent[rows:] = kept[...], landed[rows:]

    return small(kernel, "rows_on", [like(*kept.shape), like(2 * rows, kept.shape[1])], kept, landed)


def chosen(part, refs):
    low = jnp.where(part == 0, refs[0][...], refs[1][...])
    return jnp.where(part < 2, low, jnp.where(part == 2, refs[2][...], refs[3][...]))


def parted(low, upper):
    rows, width = low.shape
    half = width // 2

    def kernel(low, upper, out):
        for n in range(2):
            cut = slice(n * half, (n + 1) * half)
            out[n * rows : (n + 1) * rows, :half] = low[:, cut]
            out[n * rows : (n + 1) * rows, half:] = upper[:, cut]

    return small(kernel, "parted", [like(2 * rows, width)], low, upper)[0]


def traded(p, r):
    rows = p.shape[0] // 2

    def kernel(p, r, kept, sent):
        kept[:rows], kept[rows:] = p[:rows], r[:rows]
        sent[:rows], sent[rows:] = p[rows:], r[rows:]

    return small(kernel, "traded", [like(*p.shape)] * 2, p, r)


def by_z(info, p, r):
    rows = p.shape[0] // 2

    def kernel(info, p, r, kept, sent):
        turn = info[info.shape[0] - 3] ^ info[info.shape[0] - 1]
        for out, first in ((kept, 0), (sent, 1)):
            for n in range(2):
                place = turn ^ (first + 2 * n)
                line = pl.ds(pl.multiple_of(place // 2 * rows, rows), rows)
                out[n * rows : (n + 1) * rows] = jnp.where(place % 2 == 0, p[line], r[line])

    return small(kernel, "by_z", [like(*p.shape)] * 2, p, r, info=info)


def settle(info, p, r):
    rows = p.shape[0] // 2

    def kernel(info, p, r, out):
        for n, z in enumerate((0, 2, 1, 3)):
            place = info[info.shape[0] - 1] ^ z
            line = pl.ds(pl.multiple_of(place % 2 * rows, rows), rows)
            out[n * rows : (n + 1) * rows] = jnp.where(place < 2, p[line], r[line])

    return small(kernel, "settle", [like(4 * rows, p.shape[1])], p, r, info=info)[0]


def slide_rows(index, info, slides):
    end, slide = 0, jnp.zeros(index.shape, jnp.int32)
    for q in range(slides):
        end = end + info[6 + q]
        slide = slide + (index >= end).astype(jnp.int32)
    return slide


def total_of(value):
    return jnp.sum(jnp.sum(value, axis=1, keepdims=True), axis=0, keepdims=True)


def first_message(info, low, high, prior, row, slides):
    rows, width = row.shape[1], low.shape[1]

    def kernel(info, low, high, prior, row, out, share):
        line = lax.broadcasted_iota(jnp.int32, prior.shape, 0)
        lane = lax.broadcasted_iota(jnp.int32, prior.shape, 1)
        slide = slide_rows(line * 128 + lane, info, slides)
        begin = info[4] + info[info.shape[0] - 4] * rows
        spot = begin + lax.broadcasted_iota(jnp.int32, (1, rows), 1)
        own = slide_rows(spot, info, slides)
        here = prior[pl.ds(begin // 128, rows // 128), :]
        here = jnp.concatenate([here[n : n + 1] for n in range(rows // 128)], axis=1)
        totals = jnp.zeros((1, rows), f32)
        for q in range(slides):
            totals = jnp.where(own == q, total_of(jnp.where(slide == q, prior[...], 0.0)), totals)
        here = here / totals
        share[...] = jnp.broadcast_to(here, share.shape)
        total = row[0:1, :]
        values = [total_of(jnp.where(own == q, total, 0.0)) for q in range(slides)]
        values += [total_of(jnp.where(own == q, here, 0.0)) for q in range(slides)]
        values += [total_of(here * (jnp.log(here) - jnp.log(total)))]
        place = lax.broadcasted_iota(jnp.int32, (1, 2 * width), 1)
        extra = jnp.zeros((1, 2 * width), f32)
        for n, value in enumerate(values):
            extra = jnp.where(place == n, value, extra)
        out[...] = jnp.zeros_like(out)
        out[0:3, :width], out[0:3, width:] = low[0:3, :], high[0:3, :]
        out[3:4, :] = extra

    outs = [like(8, 2 * width), like(8, rows)]
    return small(kernel, "first", outs, low, high, prior, row, info=info)


def second_message(info, low, high, cos):
    rows, width = cos.shape[1], low.shape[1]

    def kernel(info, low, high, cos, out):
        place = lax.broadcasted_iota(jnp.int32, (4, 2 * width), 1)
        line = lax.broadcasted_iota(jnp.int32, (4, 2 * width), 0)
        mine = (line == info[info.shape[0] - 3]) & (place // rows == info[info.shape[0] - 4])
        wide = jnp.concatenate([cos[0:4, :]] * (2 * width // rows), axis=1)
        out[0:3, :width], out[0:3, width:] = low[0:3, :], high[0:3, :]
        out[3:4, :] = jnp.where(place[0:1] == 0, total_of(cos[0:1, :]), 0.0)
        out[4:8, :] = jnp.where(mine, wide, 0.0)

    return small(kernel, "second", [like(8, 2 * width)], low, high, cos, info=info)[0]


def join_parts(mine, *others):
    width = mine.shape[1] // 4

    def kernel(mine, *refs):
        total = mine[...]
        line = lax.broadcasted_iota(jnp.int32, total.shape, 0)
        for part, ref in enumerate(refs[:-1], 1):
            value = ref[...]
            turned = jnp.concatenate(
                [value[:, (n ^ part) * width : ((n ^ part) + 1) * width] for n in range(4)], axis=1
            )
            total = total + jnp.where(line < 3, turned, value)
        refs[-1][...] = total

    return small(kernel, "join", [like(*mine.shape)], mine, *others)[0]


def finish(info, grad, weight, cosines, first, second, share, row, slides, scale, spots_all, genes_all):
    rows, width = grad.shape

    def kernel(info, grad, weight, c0, c1, c2, c3, first, second, share, row, out, losses, genes, spots):
        spot = info[4] + info[info.shape[0] - 4] * rows + lax.broadcasted_iota(jnp.int32, (1, rows), 1)
        own = slide_rows(spot, info, slides)
        found = lambda n: first[3:4, n : n + 1]
        mass = jnp.zeros((1, rows), f32)
        density = found(2 * slides)
        for q in range(slides):
            mass = jnp.where(own == q, found(q), mass)
            density = density + found(slides + q) * jnp.log(found(q))
        total = row[0:1, :]
        mass_grad = scale * density_weight * (total / mass - share[0:1, :]) / slides
        summed = jnp.broadcast_to(jnp.sum(weight[...], axis=1, keepdims=True), (rows, 128))
        turned = jnp.concatenate([summed[n : n + 128].T[0:1] for n in range(0, rows, 128)], axis=1)
        offset = (mass_grad - turned) / total
        loss = -(total_of(c0[0:1] + c1[0:1] + c2[0:1] + c3[0:1]) / genes_all + second[3:4, 0:1] / spots_all)
        place = lax.broadcasted_iota(jnp.int32, losses.shape, 1)
        losses[...] = jnp.where(place == 0, loss, density / slides)
        out[:rows] = grad[...]
        wide = jnp.concatenate([offset, jnp.zeros((1, width - rows), f32)], axis=1)
        out[rows:] = jnp.broadcast_to(wide, (8, width))
        both = jnp.concatenate([c0[0:1, : width // 2], c1[0:1, : width // 2]], axis=1)
        genes[...] = jnp.broadcast_to(both, genes.shape)
        group = jnp.zeros((1, width), f32)
        for n in range(8):
            line = second[4 + n // 2 : 5 + n // 2, n % 2 * width : n % 2 * width + width]
            group = jnp.where(info[5] == n, line, group)
        spots[...] = jnp.broadcast_to(group, spots.shape)

    outs = [like(rows + 8, width), like(8, 128), like(8, width), like(8, width)]
    return small(kernel, "finish", outs, grad, weight, *cosines, first, second, share, row, info=info)


def offsets(tails, rows):
    def kernel(a, b, c, d, out):
        for n, ref in enumerate((a, b, c, d)):
            for m in range(2):
                place = slice((2 * n + m) * rows, (2 * n + m + 1) * rows)
                out[:, place] = ref[8 * m : 8 * m + 8, :rows]

    spec = ((16, tails[0].shape[1]), lambda k: (rows // 8, 0))
    return small(kernel, "offsets", [like(8, 8 * rows)], *tails, blocks={n: spec for n in range(4)})[0]


def gather_expression(*parts):
    depth, half = parts[0].shape
    each = len(parts) // 4

    def kernel(*refs):
        out = refs[-1]
        for n in range(2):

            @pl.when(pl.program_id(0) == n)
            def _():
                for m in range(2):
                    total = sum(ref[...] for ref in refs[(2 * m + n) * each : (2 * m + n + 1) * each])
                    out[:, m * half : (m + 1) * half] = total

    return pl.pallas_call(
        kernel,
        name="gather",
        grid=(2,),
        in_specs=[whole((depth, half))] * len(parts),
        out_specs=pl.BlockSpec((depth, 2 * half), lambda k: (k, 0)),
        out_shape=like(2 * depth, 2 * half),
        cost_estimate=light,
        compiler_params=room(40),
    )(*parts)


def slice_4x2(logits, expression, spatial, density_prior, cell_slide, group_live, spot_counts):
    slot_dev, spot_dev = logits.shape
    gene_dev = expression.shape[1]
    groups, parts = 8, 4
    spots_all, genes_all = spot_dev * parts, gene_dev * parts
    slides = spot_counts.shape[0]
    rows = spot_dev // 8
    group_index, gene_index = lax.axis_index("cells"), lax.axis_index("genes")
    z, x = group_index // 2, group_index % 2
    scale = float(slot_dev * groups) * float(spots_all)
    spots_scale, genes_scale = scale / spots_all, scale / genes_all
    run = Steps()
    early = lambda name, value: run(name, take, value) if name in order else value

    place = 4 * x + 2 * (z % 2) + z // 2
    info = jnp.concatenate(
        [
            jnp.stack([(2 * m ^ place) // 2 for m in range(4)] + [gene_index * spot_dev, group_index]),
            spot_counts,
            group_live,
            jnp.stack([place, gene_index, place % 2, z]),
        ]
    ).astype(jnp.int32)
    prior = density_prior.reshape(-1, 128)

    pair = 2 * rows
    code = cell_slide.reshape(-1, 128)
    both = lambda move, values: [move(v) for v in values]
    cut = lambda *v: halves(v[0], 0, *v[1:])
    one, two = [[(0, 0), (0, pair)]], [[(0, 0), (0, pair)], [(1, 0), (1, pair)]]
    own_a, own_b = run(Step.own, lambda e: halves(in_hbm(e), 1), expression)
    across_a = over_y(own_a)
    beside_a, beside_b = over_core(own_a), over_core(own_b)
    wbh, wbl, tbh, tbl, tot_b = run(Step.weigh_b, lambda *v: weigh(*v, slides, 2), info, logits, code)
    sent_0, *e0 = run(
        Step.blend_0b, lambda h, l, p, q, t: blend([(h, l)], [p, q], one, (t,)), tbh, tbl, own_a, beside_a, tot_b
    )
    x_0 = over_x(sent_0)
    wah, wal, tah, tal, tot_a = run(Step.weigh_a, lambda *v: weigh(*v, slides, 0), info, logits, code)
    full = lambda groups, gather: lambda ah, al, bh, bl, *v: blend([(ah, al), (bh, bl)], gather(*v), groups)
    turned = (tah, tal, tbh, tbl)
    keep_1, sent_1, *e1 = run(
        Step.blend_1, full([[(0, 0), (1, 0)], [(0, pair), (1, pair)]], lambda p, q: [p, q]), *turned, own_b, beside_b
    )
    z_1 = over_z(sent_1, 1)
    z_1 = early(Step.taken_z1, z_1)
    (keep_0,) = run(
        Step.blend_0a, lambda h, l, p, q, t: blend([(h, l)], [p, q], one, (t,), False), tah, tal, own_a, beside_a, tot_a
    )
    beyond_a = both(over_core, run(Step.beyond_a, cut, across_a))
    across_b = over_y(run(Step.own_b, copy, own_b))
    keep_2, sent_2, *e2 = run(Step.blend_2, full(two, lambda p, *q: [p, q]), *turned, across_a, *beyond_a)
    x_2 = over_x(sent_2)
    x_2 = early(Step.taken_x2, x_2)
    keep_0, sent_0 = run(Step.half_0, lambda *v: part_total(pair, *v), keep_0, x_0)
    z_0 = over_z(sent_0, 1)
    keep_1, sent_1 = run(Step.half_1, cut, keep_1, z_1)
    x_1 = over_x(sent_1)
    beyond_b = both(over_core, run(Step.beyond_b, cut, across_b))
    g_0, g_1, g_far = run(Step.rows, lambda i, t: rows_of(i, t, rows, spot_dev // rows), info, spatial)
    g_far = over_y(g_far)
    keep_0, sent_0 = run(Step.quarter_0, lambda *v: part_total(rows, *v), keep_0, z_0)
    w_0 = over_z(sent_0, 2)
    w_0 = early(Step.taken_w0, w_0)
    keep_3, sent_3, *e3 = run(Step.blend_3, full(two, lambda p: [p]), *turned, across_b)
    x_3 = over_x(sent_3)
    keep_4, sent_4, *e4 = run(Step.blend_4, full(two, lambda *q: [q]), *turned, *beyond_b)
    x_4 = over_x(sent_4)
    x_3 = early(Step.taken_x3, x_3)
    keep_2, sent_2 = run(Step.half_2, cut, keep_2, x_2)
    z_2 = over_z(sent_2, 1)
    keep_1, sent_1 = run(Step.quarter_1, cut, keep_1, x_1)
    w_1 = over_z(sent_1, 2)
    w_1 = early(Step.taken_w1, w_1)
    g_2, g_1 = run(Step.rows_on, rows_on, g_1, g_far)
    g_1 = over_core(g_1)
    pred_0, gsum_0, part_0, inv, row = run(
        Step.stats_0, lambda p, r, g, h: stats([p], [r], [(g, 0), (h, 0)], 0), keep_0, w_0, g_0, g_1
    )
    keep_2, sent_2 = run(Step.quarter_2, cut, keep_2, z_2)
    w_2 = over_z(sent_2, 2)
    pred_1, gsum_1, part_1 = run(
        Step.stats_1, lambda p, r, i, b, g, h: stats([p], [r], [(g, 0), (h, 0)], 1, i, b),
        keep_1, w_1, inv, part_0, g_0, g_1,
    )
    keep_3, sent_3 = run(Step.half_3, cut, keep_3, x_3)
    z_3 = over_z(sent_3, 1)
    keep_4, sent_4 = run(Step.half_4, cut, keep_4, x_4)
    z_4 = over_z(sent_4, 1)
    pred_2, gsum_2, part_2 = run(
        Step.stats_2, lambda p, r, i, b, g, h: stats([p], [r], [(g, 0), (h, 1)], 0, i, b),
        keep_2, w_2, inv, part_1, g_2, g_1,
    )
    first, share = run(Step.first, lambda *v: first_message(*v, slides), info, gsum_0, gsum_2, prior, row)
    keep_3, sent_3 = run(Step.quarter_3, cut, keep_3, z_3)
    w_3 = over_z(sent_3, 2)
    keep_4, sent_4 = run(Step.quarter_4, cut, keep_4, z_4)
    w_4 = over_z(sent_4, 2)

    def sum_up(names, value):
        value = run(names[0], add, value, over_x(value))
        others = [over_z(value, 1), over_z(value, 2), over_z(value, 3)]
        value = run(names[1], add, value, *others)
        others = [over_core(value), over_y(value), shift(value, lambda k: k ^ 3, "genes")]
        return run(names[2], join_parts, value, *others)

    first = sum_up((Step.first_1, Step.first_2, Step.first_3), first)
    pred_3, gsum_3, _, spot_unit, spot_slope, spot_cos = run(
        Step.stats_3,
        lambda p, q, r, t, i, b, g, h: stats([p, q], [r, t], [(g, 0), (h, 1)], 1, i, b, True, spots_scale),
        keep_3, keep_4, w_3, w_4, inv, part_2, g_2, g_1,
    )
    second = run(Step.second, second_message, info, gsum_1, gsum_3, spot_cos)
    second = sum_up((Step.second_1, Step.second_2, Step.second_3), second)
    shared = (spot_unit, spot_slope, inv)
    d2, weight_2, cos2 = run(
        Step.grad_2, lambda p, s, u, v, i, g, h: grad_of(p, [(g, 0), (h, 1)], 0, s, 1, u, v, i, genes_scale),
        pred_2, first, *shared, g_2, g_1,
    )
    b_2 = over_z(d2, 2)
    d0, weight_0, cos0 = run(
        Step.grad_0, lambda p, s, u, v, i, b, g, h: grad_of(p, [(g, 0), (h, 0)], 0, s, 0, u, v, i, genes_scale, b),
        pred_0, first, *shared, weight_2, g_0, g_1,
    )
    home_r = over_y(run(Step.home_0, parted, pred_2, pred_3))
    home = run(Step.home_1, parted, pred_0, pred_1)
    lo_2 = run(Step.lo_2, lambda p, r: stack(p, r, rows), d2, b_2)
    c_2, xlo_2 = over_z(lo_2, 1), over_x(lo_2)
    xlo_2 = early(Step.taken_xlo2, xlo_2)
    b_0 = over_z(run(Step.go_0, copy, d0), 2)
    b_0 = early(Step.taken_b0, b_0)
    d3, weight_3, cos3 = run(
        Step.grad_3, lambda p, s, u, v, i, b, g, h: grad_of(p, [(g, 0), (h, 1)], 1, s, 1, u, v, i, genes_scale, b),
        pred_3, second, *shared, weight_0, g_2, g_1,
    )
    d1, weight_1, cos1 = run(
        Step.grad_1, lambda p, s, u, v, i, b, g, h: grad_of(p, [(g, 0), (h, 0)], 1, s, 0, u, v, i, genes_scale, b),
        pred_1, second, *shared, weight_3, g_0, g_1,
    )
    d3, losses, own_cos, group_cos = run(
        Step.finish,
        lambda i, g, w, a, b, c, d, *v: finish(i, g, w, (a, b, c, d), *v, slides, scale, spots_all, genes_all),
        info, d3, weight_1, cos0, cos1, cos2, cos3, first, second, share, row,
    )
    b_3 = over_z(d3, 2)
    home, sent = run(Step.home_2, traded, home, home_r)
    home_r = over_core(sent)
    lo_0 = run(Step.lo_0, lambda p, r: stack(p, r, rows), d0, b_0)
    c_0, xlo_0 = over_z(lo_0, 1), over_x(lo_0)
    xlo_0 = early(Step.taken_xlo0, xlo_0)
    hi_2 = run(Step.hi_2, copy, c_2)
    xhi_2 = over_x(hi_2)
    home, sent = run(Step.home_3, lambda i, p, r: by_z(i, p, r), info, home, home_r)
    home_r = over_z(sent, 1)
    lo_3 = run(Step.lo_3, lambda p, r: stack(p, r, rows), d3, b_3)
    c_3, xlo_3 = over_z(lo_3, 1), over_x(lo_3)
    xlo_3 = early(Step.taken_xlo3, xlo_3)
    hi_0 = run(Step.hi_0, copy, c_0)
    xhi_0 = over_x(hi_0)
    xhi_0 = early(Step.taken_xhi0, xhi_0)
    b_1 = over_z(run(Step.go_1, copy, d1), 2)
    b_1 = early(Step.taken_b1, b_1)
    weights = (wah, wal, wbh, wbl)
    back_share = lambda a, b, c, d, *v: share_of((a, b, c, d), [(p, 0) for p in v])
    *parts_2, dh2, dl2 = run(Step.share_2, back_share, *weights, lo_2, hi_2, xlo_2, xhi_2)
    chip_a = both(over_core, parts_2[2:])
    hi_3 = run(Step.hi_3, copy, c_3)
    xhi_3 = over_x(hi_3)
    chip_a = over_y(run(Step.chip_a, add_rows, *parts_2[:2], *chip_a))
    chip_a = early(Step.taken_chip_a, chip_a)
    lo_1 = run(Step.lo_1, lambda p, r: stack(p, r, rows), d1, b_1)
    c_1, xlo_1 = over_z(lo_1, 1), over_x(lo_1)
    xlo_1 = early(Step.taken_xlo1, xlo_1)
    *parts_3, dh3, dl3 = run(Step.share_3, back_share, *weights, lo_3, hi_3, xlo_3, xhi_3)
    chip_b = both(over_core, parts_3[2:])
    hi_1 = run(Step.hi_1, copy, c_1)
    xhi_1 = over_x(hi_1)
    chip_b = over_y(run(Step.chip_b, add_rows, *parts_3[:2], *chip_b))
    home, sent = run(Step.home_4, traded, home, home_r)
    home_r = over_z(sent, 2)
    mg = run(Step.back_2, lambda a, b, c, d: back([(a, b)], (c, d)), *e2, dh2, dl2)
    mg = run(Step.back_3, lambda a, b, c, d, e, f, g: back([(a, b), (c, d)], (e, f), g), *e3, *e4, dh3, dl3, mg)
    offset = run(Step.offsets, lambda *v: offsets(v, rows), lo_3, hi_3, xlo_3, xhi_3)
    outcome = run(
        Step.near,
        lambda i, wh, wl, e0h, e0l, e1h, e1l, mg, off, a, b, c, d, p: half_of(
            i, 0, (wh, wl), [a, b, c, d], (0, 1), ((0, p),), [e0h, e0l, e1h, e1l, mg, off]
        ),
        info, wah, wal, *e0, *e1, mg, offset, lo_0, hi_0, lo_1, hi_1, chip_a,
    )
    near_grad, near = outcome[0], outcome[1:]
    def far(base):
        return lambda i, wh, wl, e0h, e0l, e1h, e1l, mg, off, a, b, grad, *v: half_of(
            i, base, (wh, wl), [a, b], (0, 1), (), [e0h, e0l, e1h, e1l, mg, off], grad, v
        )

    passed = run(Step.far_lo, far(2), info, wbh, wbl, *e0, *e1, mg, offset, xlo_0, xlo_1, near_grad, *near)
    grad_logits, *shares = run(Step.far_hi, far(3), info, wbh, wbl, *e0, *e1, mg, offset, xhi_0, xhi_1, *passed)
    core_a, core_b = both(over_core, shares[2:4]), both(over_core, shares[6:])
    pred_out = run(Step.settle, lambda i, p, r: settle(i, p, r), info, home, home_r)
    shares[4:6] = run(Step.late, add_below, *shares[4:6], chip_b)
    summands = []
    for kept, core in ((shares[0:2], core_a), (shares[4:6], core_b)):
        for n in range(2):
            summands += [kept[n], core[n]]
    grad_expression = run(Step.gather, gather_expression, *summands)
    run.run(order)
    get = lambda v: run.value(v)
    losses = get(losses)
    return (
        get(pred_out), get(own_cos)[0], get(group_cos)[0], losses[0, 0], losses[0, 1], get(grad_logits), get(grad_expression)
    )


order = (
    Step.own, Step.weigh_b, Step.blend_0b, Step.weigh_a, Step.blend_1, Step.own_b, Step.blend_0a, Step.beyond_a,
    Step.blend_2, Step.half_0, Step.half_1, Step.rows, Step.beyond_b, Step.blend_3, Step.quarter_0, Step.blend_4,
    Step.half_2, Step.rows_on, Step.taken_w0, Step.quarter_1, Step.half_4, Step.quarter_2, Step.half_3,
    Step.stats_0, Step.taken_w1, Step.stats_1, Step.stats_2, Step.quarter_4, Step.first, Step.quarter_3,
    Step.first_1, Step.first_2, Step.stats_3, Step.first_3, Step.grad_2, Step.home_0, Step.grad_0, Step.second,
    Step.second_1, Step.home_1, Step.second_2, Step.lo_2, Step.go_0, Step.second_3, Step.grad_3, Step.home_2,
    Step.grad_1, Step.go_1, Step.finish, Step.lo_0, Step.hi_2, Step.taken_xlo2, Step.home_3, Step.lo_3,
    Step.share_2, Step.hi_0, Step.taken_xlo3, Step.back_2, Step.chip_a, Step.hi_3, Step.taken_xlo0, Step.lo_1,
    Step.offsets, Step.share_3, Step.hi_1, Step.taken_chip_a, Step.taken_xlo1, Step.back_3, Step.home_4,
    Step.chip_b, Step.near, Step.far_lo, Step.far_hi, Step.settle, Step.late, Step.gather,
)


def solution(mesh):
    fits = mesh.shape["cells"] == 8 and mesh.shape["genes"] == 4
    return jax.shard_map(
        slice_4x2 if fits else spread,
        mesh=mesh,
        in_specs=(
            P("cells", "genes"),
            P("cells", "genes"),
            P(None, "genes"),
            P(),
            P("cells"),
            P(),
            P(),
        ),
        out_specs=(
            P("cells", "genes"),
            P("genes"),
            P("cells"),
            P(),
            P(),
            P("cells", "genes"),
            P("cells", "genes"),
        ),
        check_vma=False,
    )
```
